256 devices in a mesh: req: 64 (over x, z, core), tp: 4 (over y).
Axes of the slice: x: 4, y: 4, z: 8, core: 2. Of those that a mesh axis runs over, the one named last changes fastest.
Arguments:
- tokens: bfloat16 [65536, 2048], P('req'), may hold values from -6 to 6
- input_norm_gain: float32 [2048], replicated, may hold values from 0.1 to 1.9
- query_matrix: bfloat16 [2048, 2048], P(None, 'tp')
- key_matrix: bfloat16 [2048, 1024], P(None, 'tp')
- value_matrix: bfloat16 [2048, 1024], P(None, 'tp'), may hold values from -0.125 to 0.125
- output_matrix: bfloat16 [2048, 2048], P('tp'), may hold values from -0.125 to 0.125
- adapter_down_maps: bfloat16 [1024, 2048, 16], P('req', 'tp'), may hold values from -0.125 to 0.125
- adapter_up_maps: bfloat16 [1024, 16, 2048], P('req', None, 'tp'), may hold values from -1.5 to 1.5
- request_row_counts: int32 [64, 32], P('req'), may hold values from 1 to 40, 1024 in all within a row
- prompt_group_per_request: int32 [64, 32], P('req'), may hold values from 0 to 2, as said below
- adapter_per_request: int32 [64, 32], P('req'), may hold values from 0 to 1023, as said below
- adapter_table_slot: int32 [1024], replicated, may hold values from 0 to 1023, as said below
Outputs:
- mixed: bfloat16 [65536, 2048], P('req', 'tp')
The draws below stay inside these ranges and needn't reach their ends.
Inputs may be any that keep to these rules, and one draw needn't show every extreme that they name: `prompt_group_per_request`: on each device the requests form 3 consecutive groups numbered 0, 1, 2, each of 8 to 16 requests. `adapter_per_request`: the slots adapter_table_slot[a] of one device's 32 requests lie on 32 different indices of req, so a device sends at most 40 rows to one index of req, and some device sends exactly 40. `request_row_counts`: each device's requests fill its 1024 rows in order; each device has a request of exactly 40 rows. `adapter_table_slot`: every adapter has its own slot.
All inputs are finite; a program needn't handle non-finite values.
Results may differ from the reference program's by a relative error of at most 0.034.
Values may be sent and summed in bfloat16 or wider, within the bound.
A program may use at most 128 MiB of HBM per device.

```python
import math
import jax
import jax.numpy as jnp
import numpy as np
from jax import lax

MODEL_WIDTH = 2048
QUERY_HEADS = 16
KEY_VALUE_HEADS = 8
HEAD_WIDTH = 128
ADAPTER_RANK = 16
ADAPT_DEV = 16
TOKEN_ROWS_PART = 1024
REQ_DEV = 32
LMAX = 40
TOKENS = 65536
ADAPTER_TOTAL = 1024
N_REQ = 64
N_TP = 4


def query_key_pair(key):
    query_unrotated = jax.random.normal(jax.random.fold_in(key, 11), (MODEL_WIDTH, QUERY_HEADS * HEAD_WIDTH), jnp.float32)
    random_noise = jax.random.normal(jax.random.fold_in(key, 12), (MODEL_WIDTH, KEY_VALUE_HEADS * HEAD_WIDTH), jnp.float32)
    return (query_unrotated / math.sqrt(MODEL_WIDTH), random_noise / math.sqrt(MODEL_WIDTH))


def draw_query_matrix(key, part):
    return query_key_pair(key)[0].astype(jnp.bfloat16)


def draw_key_matrix(key, part):
    return query_key_pair(key)[1].astype(jnp.bfloat16)


def draw_prompt_group_per_request(key, part):
    quarter = REQ_DEV // 4
    halfway = REQ_DEV // 2
    first_size = jax.random.randint(jax.random.fold_in(key, 21), (N_REQ,), quarter, halfway + 1)
    lowest = jnp.maximum(quarter, halfway - first_size)
    highest = jnp.minimum(halfway, REQ_DEV - quarter - first_size)
    random_int = jax.random.randint(jax.random.fold_in(key, 22), (N_REQ,), 0, 1 << 20)
    second_size = lowest + random_int % (highest - lowest + 1)
    indices = jnp.arange(REQ_DEV, dtype=jnp.int32)[None, :]
    groups = (indices >= first_size[:, None]).astype(jnp.int32) + (indices >= (first_size + second_size)[:, None]).astype(jnp.int32)
    return groups.astype(jnp.int32)


def adapter_plan(key):
    slot_perm = jax.random.permutation(jax.random.fold_in(key, 41), ADAPTER_TOTAL).astype(jnp.int32)
    inverse = jnp.argsort(slot_perm, stable=True).astype(jnp.int32)
    device_keys = jax.random.split(jax.random.fold_in(key, 42), N_REQ)
    orders = jax.vmap(lambda one_key: jax.random.permutation(one_key, N_REQ))(device_keys).astype(jnp.int32)
    columns = jnp.arange(REQ_DEV, dtype=jnp.int32) % N_REQ
    holders = orders[:, columns]
    local_slot = jax.random.randint(jax.random.fold_in(key, 43), (N_REQ, REQ_DEV), 0, ADAPT_DEV).astype(jnp.int32)
    chosen = inverse[holders * ADAPT_DEV + local_slot]
    return (slot_perm, chosen.astype(jnp.int32))


def draw_adapter_table_slot(key, part):
    return adapter_plan(key)[0]


def draw_adapter_per_request(key, part):
    return adapter_plan(key)[1]


def levels(rng, dims, cuts, least, top_value):
    factor_of = 1.0
    for position, parts in cuts:
        steps = jax.random.uniform(jax.random.fold_in(jax.random.fold_in(rng, 6), position), (parts,), jnp.float32, least / len(cuts), top_value / len(cuts))
        factor_of = factor_of * jnp.repeat(jnp.exp(steps), dims[position] // parts).reshape((-1,) + (1,) * (len(dims) - 1 - position))
    return factor_of


def profile(amount, total, bound, skew):
    weights = [(1 << 20) // math.isqrt(rank ** skew) + 1 for rank in range(2, amount + 1)]
    spare, holding = total - bound - (amount - 1), [1] * (amount - 1)
    while spare > 0:
        candidates = [i for i in range(amount - 1) if holding[i] < bound]
        whole, left = sum([weights[i] for i in candidates]), spare
        for i in candidates:
            extra = min(bound - holding[i], max(1, left * weights[i] // whole), spare)
            holding[i] = holding[i] + extra
            spare = spare - extra
    return np.array([bound] + holding)


def uneven_parts(stream_key, amount, total, bound, lean):
    if amount == 2:
        one = jax.random.randint(stream_key, (), max(1, total - bound), min(bound, total - 1) + 1)
        return jnp.stack([one, total - one])
    tallies = jnp.asarray(profile(amount, total, bound, lean), jnp.int32)
    pairs = (amount - 1) // 2
    source_of, sink = tallies[1:1 + 2 * pairs:2], tallies[2:2 + 2 * pairs:2]
    slack = jnp.minimum(source_of - 1, bound - sink)
    shifted = jax.random.randint(jax.random.fold_in(stream_key, 1), (pairs,), 0, 1 << 20) % (slack + 1)
    tallies = tallies.at[1:1 + 2 * pairs:2].set(source_of - shifted).at[2:2 + 2 * pairs:2].set(sink + shifted)
    return tallies[jax.random.permutation(jax.random.fold_in(stream_key, 2), amount)]


def scatter_about(own_key, dims, deviation, bound, cuts=(), held_as=jnp.bfloat16):
    entries = deviation * jax.random.normal(own_key, dims, jnp.float32)
    if cuts:
        entries = entries * levels(own_key, dims, cuts, -0.22, 0.18)
    return jnp.clip(entries, -bound, bound).astype(held_as)


def setup_inputs(seed: int = 0) -> dict:
    arg_keys = jax.random.split(jax.random.key(seed), 13)
    return {
        "tokens": scatter_about(arg_keys[0], (TOKENS, MODEL_WIDTH), 1.0, 6.0, ((0, 64),)),
        "input_norm_gain": jnp.clip(1.0 + 0.18 * jax.random.normal(arg_keys[1], (MODEL_WIDTH,), jnp.float32), 0.1, 1.9),
        "query_matrix": draw_query_matrix(jax.random.fold_in(arg_keys[12], 71), 0),
        "key_matrix": draw_key_matrix(jax.random.fold_in(arg_keys[12], 71), 0),
        "value_matrix": scatter_about(arg_keys[4], (MODEL_WIDTH, KEY_VALUE_HEADS * HEAD_WIDTH), MODEL_WIDTH ** -0.5, 0.125, ((1, 4),)),
        "output_matrix": scatter_about(arg_keys[5], (QUERY_HEADS * HEAD_WIDTH, MODEL_WIDTH), (QUERY_HEADS * HEAD_WIDTH) ** -0.5, 0.125, ((0, 4),)),
        "adapter_down_maps": scatter_about(arg_keys[6], (ADAPTER_TOTAL, MODEL_WIDTH, ADAPTER_RANK), MODEL_WIDTH ** -0.5, 0.125, ((0, 64), (1, 4))),
        "adapter_up_maps": scatter_about(arg_keys[7], (ADAPTER_TOTAL, ADAPTER_RANK, QUERY_HEADS * HEAD_WIDTH), ADAPTER_RANK ** -0.5, 1.5, ((0, 64), (2, 4))),
        "request_row_counts": jax.vmap(lambda own: uneven_parts(own, REQ_DEV, TOKEN_ROWS_PART, LMAX, 2))(jax.random.split(arg_keys[8], N_REQ)).reshape((N_REQ, REQ_DEV)).astype(jnp.int32),
        "prompt_group_per_request": draw_prompt_group_per_request(jax.random.fold_in(arg_keys[12], 71), 0),
        "adapter_per_request": draw_adapter_per_request(jax.random.fold_in(arg_keys[12], 71), 0),
        "adapter_table_slot": draw_adapter_table_slot(jax.random.fold_in(arg_keys[12], 71), 0),
    }


def apply_rotary(vectors, token_positions):
    half_dim = HEAD_WIDTH // 2
    inverse = 1000000.0 ** (-(jnp.arange(half_dim, dtype=jnp.float32) * 2.0 / HEAD_WIDTH))
    angles = token_positions[:, None] * inverse[None, :]
    cosine = jnp.cos(angles)[:, None, :]
    sine_part = jnp.sin(angles)[:, None, :]
    first_half = vectors[..., :half_dim]
    second = vectors[..., half_dim:]
    return jnp.concatenate([first_half * cosine - second * sine_part, second * cosine + first_half * sine_part], -1)

def layout(lengths, groups):
    row_ids = jnp.arange(TOKEN_ROWS_PART, dtype=jnp.int32)
    row_ends = jnp.cumsum(lengths).astype(jnp.int32)
    starts = (row_ends - lengths).astype(jnp.int32)
    request_row = lax.optimization_barrier(jnp.sum((row_ids[:, None] >= row_ends[None, :]).astype(jnp.int32), 1))
    request_hot = (request_row[:, None] == jnp.arange(REQ_DEV, dtype=jnp.int32)[None, :]).astype(jnp.int32)
    previous = jnp.concatenate([jnp.full((1,), -1, jnp.int32), groups[:-1].astype(jnp.int32)])
    is_prompt = (groups != previous).astype(jnp.int32)
    prompt_len = lax.optimization_barrier(jnp.sum(lengths[None, :] * is_prompt[None, :] * (groups[None, :] == groups[:, None]).astype(jnp.int32), 1))
    offset_req = (1 - is_prompt) * prompt_len - starts
    group_row = lax.optimization_barrier(jnp.sum(request_hot * groups[None, :], 1))
    prompt_row = lax.optimization_barrier(jnp.sum(request_hot * is_prompt[None, :], 1))
    offset_row = lax.optimization_barrier(jnp.sum(request_hot * offset_req[None, :], 1))
    token_positions = (row_ids + offset_row).astype(jnp.float32)
    visible = (group_row[:, None] == group_row[None, :]) & (row_ids[None, :] <= row_ids[:, None])
    visible = visible & ((request_row[:, None] == request_row[None, :]) | (prompt_row[None, :] == 1))
    return (request_hot, visible, token_positions)

def reference(tokens, input_norm_gain, query_matrix, key_matrix, value_matrix, output_matrix, adapter_down_maps, adapter_up_maps, request_row_counts, prompt_group_per_request, adapter_per_request, adapter_table_slot):
    slice_heads = QUERY_HEADS * HEAD_WIDTH // N_TP

    def one_device(carried):
        block_tokens, lengths, groups, adapters = carried
        request_hot, visible, token_positions = layout(lengths, groups)
        owners = lax.optimization_barrier(jnp.sum((adapters[:, None] == jnp.arange(ADAPTER_TOTAL, dtype=jnp.int32)[None, :]).astype(jnp.int32) * adapter_table_slot[None, :], 1))
        slot_of_row = lax.optimization_barrier(jnp.sum(request_hot * owners[None, :], 1))
        float_tok = block_tokens.astype(jnp.float32)
        normalized_input = (float_tok * lax.rsqrt(lax.optimization_barrier(jnp.mean(float_tok * float_tok, -1, keepdims=True)) + 1e-06) * input_norm_gain).astype(jnp.bfloat16)
        down_map_rows = adapter_down_maps[slot_of_row].astype(jnp.float32)
        rank = jnp.einsum('td,tdr->tr', normalized_input.astype(jnp.float32), down_map_rows).astype(jnp.bfloat16)
        up_map_rows = adapter_up_maps[slot_of_row].astype(jnp.float32)
        query_delta = (2.0 * jnp.einsum('tr,trq->tq', rank.astype(jnp.float32), up_map_rows)).astype(jnp.bfloat16)
        query_full = jnp.dot(normalized_input, query_matrix, preferred_element_type=jnp.float32) + query_delta.astype(jnp.float32)
        query_heads = apply_rotary(query_full.reshape(TOKEN_ROWS_PART, QUERY_HEADS, HEAD_WIDTH), token_positions).astype(jnp.bfloat16)
        key_complete = jnp.dot(normalized_input, key_matrix, preferred_element_type=jnp.float32)
        key_head_rows = apply_rotary(key_complete.reshape(TOKEN_ROWS_PART, KEY_VALUE_HEADS, HEAD_WIDTH), token_positions).astype(jnp.bfloat16)
        value_head_rows = jnp.dot(normalized_input, value_matrix, preferred_element_type=jnp.float32).astype(jnp.bfloat16).reshape(TOKEN_ROWS_PART, KEY_VALUE_HEADS, HEAD_WIDTH)
        key_head_rows = jnp.repeat(key_head_rows, QUERY_HEADS // KEY_VALUE_HEADS, axis=1)
        value_head_rows = jnp.repeat(value_head_rows, QUERY_HEADS // KEY_VALUE_HEADS, axis=1)
        scores = jnp.einsum('qhd,khd->hqk', query_heads.astype(jnp.float32), key_head_rows.astype(jnp.float32)) / HEAD_WIDTH ** 0.5
        scores = jnp.where(visible[None], scores, jnp.float32(-1e+30))
        row_max = lax.optimization_barrier(jnp.max(scores, -1, keepdims=True))
        weights = jnp.exp(scores - row_max)
        probabilities = (weights / lax.optimization_barrier(jnp.sum(weights, -1, keepdims=True))).astype(jnp.bfloat16)
        attended = jnp.einsum('hqk,khd->qhd', probabilities.astype(jnp.float32), value_head_rows.astype(jnp.float32)).astype(jnp.bfloat16)
        attended = attended.reshape(TOKEN_ROWS_PART, N_TP, slice_heads).astype(jnp.float32)
        partial_value = jnp.einsum('tnq,nqd->ntd', attended, output_matrix.reshape(N_TP, slice_heads, MODEL_WIDTH).astype(jnp.float32)).astype(jnp.bfloat16)
        partial_value = lax.optimization_barrier(partial_value)
        summed = lax.optimization_barrier(jnp.sum(partial_value.astype(jnp.float32), 0))
        return (float_tok + summed).astype(jnp.bfloat16)
    outputs = lax.map(one_device, (tokens.reshape(N_REQ, TOKEN_ROWS_PART, MODEL_WIDTH), request_row_counts, prompt_group_per_request, adapter_per_request))
    return outputs.reshape(TOKENS, MODEL_WIDTH)
```

```python
import jax
import jax.numpy as jnp
from jax import lax
from jax.sharding import PartitionSpec as P

HEAD_WIDTH = 128
REQ_DEV = 32
LMAX = 40


def apply_rotary(vectors, token_positions):
    head_size = vectors.shape[-1]
    half_dim = head_size // 2
    inverse = 1000000.0 ** (-(jnp.arange(half_dim, dtype=jnp.float32) * 2.0 / head_size))
    angles = token_positions[:, None] * inverse[None, :]
    cosine = jnp.cos(angles)[:, None, :]
    sine_part = jnp.sin(angles)[:, None, :]
    first_half = vectors[..., :half_dim]
    second = vectors[..., half_dim:]
    return jnp.concatenate(
        [first_half * cosine - second * sine_part, second * cosine + first_half * sine_part], -1
    )


def layout(lengths, groups, tok_rows):
    req_slots = lengths.shape[0]
    row_ids = jnp.arange(tok_rows, dtype=jnp.int32)
    row_ends = jnp.cumsum(lengths)
    starts = row_ends - lengths
    request_row = jnp.sum((row_ids[:, None] >= row_ends[None, :]).astype(jnp.int32), 1)
    request_hot = (request_row[:, None] == jnp.arange(req_slots, dtype=jnp.int32)[None, :]).astype(
        jnp.int32
    )
    previous = jnp.concatenate([jnp.full((1,), -1, jnp.int32), groups[:-1]])
    is_prompt = (groups != previous).astype(jnp.int32)
    prompt_len = jnp.sum(
        lengths[None, :]
        * is_prompt[None, :]
        * (groups[None, :] == groups[:, None]).astype(jnp.int32),
        1,
    )
    offset_req = (1 - is_prompt) * prompt_len - starts
    group_row = jnp.sum(request_hot * groups[None, :], 1)
    prompt_row = jnp.sum(request_hot * is_prompt[None, :], 1)
    offset_row = jnp.sum(request_hot * offset_req[None, :], 1)
    token_positions = (row_ids + offset_row).astype(jnp.float32)
    visible = (group_row[:, None] == group_row[None, :]) & (row_ids[None, :] <= row_ids[:, None])
    visible = visible & (
        (request_row[:, None] == request_row[None, :]) | (prompt_row[None, :] == 1)
    )
    return (request_hot, starts, visible, token_positions, row_ids)


def per_device(
    tokens,
    input_norm_gain,
    query_matrix,
    key_matrix,
    value_matrix,
    output_matrix,
    adapter_down_maps,
    adapter_up_maps,
    request_row_counts,
    prompt_group_per_request,
    adapter_per_request,
    adapter_table_slot,
):
    tp_count = lax.axis_size("tp")
    req_count = lax.axis_size("req")
    tp_index = lax.axis_index("tp")
    tok_rows, width = tokens.shape
    piece_width = width // tp_count
    lengths = request_row_counts[0]
    groups = prompt_group_per_request[0]
    adapters = adapter_per_request[0]
    req_slots = lengths.shape[0]
    request_hot, starts, visible, token_positions, row_ids = layout(lengths, groups, tok_rows)
    adapters_per_part = adapter_down_maps.shape[0]
    rank_extent = adapter_down_maps.shape[2]
    slots = adapter_table_slot[adapters]
    holder = slots // adapters_per_part
    local_slot = slots % adapters_per_part
    holder_ids = jnp.arange(req_count, dtype=jnp.int32)
    holder_hot = (holder[None, :] == holder_ids[:, None]).astype(jnp.int32)
    wanted = jnp.sum(holder_hot * local_slot[None, :], 1)
    wanted_in = lax.all_to_all(
        wanted.reshape(req_count, 1), "req", split_axis=0, concat_axis=0, tiled=True
    ).reshape(req_count)
    down_sel = jnp.transpose(adapter_down_maps[wanted_in], (0, 2, 1))
    up_sel = adapter_up_maps[wanted_in]
    maps_out = jnp.concatenate([down_sel, up_sel], 1)
    maps_in = lax.all_to_all(maps_out, "req", split_axis=0, concat_axis=0, tiled=True)
    down_in = maps_in[:, :rank_extent, :].reshape(req_count * rank_extent, piece_width)
    up_in = maps_in[:, rank_extent:, :].reshape(req_count * rank_extent, piece_width)
    float_tok = tokens.astype(jnp.float32)
    normalized_input = (
        float_tok
        * lax.rsqrt(jnp.mean(float_tok * float_tok, -1, keepdims=True) + 1e-06)
        * input_norm_gain
    ).astype(jnp.bfloat16)
    normed_slice = lax.dynamic_slice_in_dim(
        normalized_input, tp_index * piece_width, piece_width, 1
    )
    holder_row = jnp.sum(request_hot * holder[None, :], 1)
    pick = (holder_row[:, None] == holder_ids[None, :])[:, :, None]
    wide_rank = jnp.dot(
        normed_slice, down_in.T, preferred_element_type=jnp.float32
    ).reshape(tok_rows, req_count, rank_extent)
    partial_rank = jnp.sum(jnp.where(pick, wide_rank, jnp.float32(0.0)), 1)
    for step in (1, 2):
        pairs = [(i, i ^ step) for i in range(tp_count)]
        partial_rank = partial_rank + lax.ppermute(partial_rank, "tp", pairs)
    rank = partial_rank.astype(jnp.bfloat16)
    spread = jnp.where(pick, rank[:, None, :], jnp.zeros((), jnp.bfloat16)).reshape(
        tok_rows, req_count * rank_extent
    )
    query_delta = (
        2.0 * jnp.dot(spread, up_in, preferred_element_type=jnp.float32)
    ).astype(jnp.bfloat16)
    heads_local = query_matrix.shape[1] // HEAD_WIDTH
    kv_local = key_matrix.shape[1] // HEAD_WIDTH
    query_full = jnp.dot(
        normalized_input, query_matrix, preferred_element_type=jnp.float32
    ) + query_delta.astype(jnp.float32)
    query_heads = apply_rotary(
        query_full.reshape(tok_rows, heads_local, HEAD_WIDTH), token_positions
    ).astype(jnp.bfloat16)
    key_complete = jnp.dot(normalized_input, key_matrix, preferred_element_type=jnp.float32)
    key_head_rows = apply_rotary(
        key_complete.reshape(tok_rows, kv_local, HEAD_WIDTH), token_positions
    ).astype(jnp.bfloat16)
    value_head_rows = (
        jnp.dot(normalized_input, value_matrix, preferred_element_type=jnp.float32)
        .astype(jnp.bfloat16)
        .reshape(tok_rows, kv_local, HEAD_WIDTH)
    )
    key_head_rows = jnp.repeat(key_head_rows, heads_local // kv_local, axis=1)
    value_head_rows = jnp.repeat(value_head_rows, heads_local // kv_local, axis=1)
    scores = (
        jnp.einsum("qhd,khd->hqk", query_heads, key_head_rows, preferred_element_type=jnp.float32)
        / HEAD_WIDTH**0.5
    )
    scores = jnp.where(visible[None], scores, jnp.float32(-1e30))
    row_max = jnp.max(scores, -1, keepdims=True)
    weights = jnp.exp(scores - row_max)
    probabilities = (weights / jnp.sum(weights, -1, keepdims=True)).astype(jnp.bfloat16)
    attended = jnp.einsum(
        "hqk,khd->qhd", probabilities, value_head_rows, preferred_element_type=jnp.float32
    ).astype(jnp.bfloat16)
    head_term = jnp.dot(
        attended.reshape(tok_rows, heads_local * HEAD_WIDTH),
        output_matrix,
        preferred_element_type=jnp.float32,
    )
    summed = lax.psum_scatter(
        head_term.astype(jnp.bfloat16), "tp", scatter_dimension=1, tiled=True
    ).astype(jnp.float32)
    residual = lax.dynamic_slice_in_dim(tokens, tp_index * piece_width, piece_width, 1)
    return (residual.astype(jnp.float32) + summed).astype(jnp.bfloat16)


def solution(mesh):
    return jax.shard_map(
        per_device,
        mesh=mesh,
        in_specs=(
            P("req", None),
            P(),
            P(None, "tp"),
            P(None, "tp"),
            P(None, "tp"),
            P("tp", None),
            P("req", "tp", None),
            P("req", None, "tp"),
            P("req", None),
            P("req", None),
            P("req", None),
            P(),
        ),
        out_specs=P("req", "tp"),
        check_vma=False,
    )
```

```python
import jax
import jax.numpy as jnp
from jax import lax
from jax.sharding import PartitionSpec as P

HEAD_WIDTH = 128
REQ_DEV = 32
LMAX = 40


def apply_rotary(vectors, token_positions):
    head_size = vectors.shape[-1]
    half_dim = head_size // 2
    inverse = 1000000.0 ** (-(jnp.arange(half_dim, dtype=jnp.float32) * 2.0 / head_size))
    angles = token_positions[:, None] * inverse[None, :]
    cosine = jnp.cos(angles)[:, None, :]
    sine_part = jnp.sin(angles)[:, None, :]
    first_half = vectors[..., :half_dim]
    second = vectors[..., half_dim:]
    return jnp.concatenate(
        [first_half * cosine - second * sine_part, second * cosine + first_half * sine_part], -1
    )


def layout(lengths, groups, tok_rows):
    req_slots = lengths.shape[0]
    row_ids = jnp.arange(tok_rows, dtype=jnp.int32)
    row_ends = jnp.cumsum(lengths)
    starts = row_ends - lengths
    request_row = jnp.sum((row_ids[:, None] >= row_ends[None, :]).astype(jnp.int32), 1)
    request_hot = (request_row[:, None] == jnp.arange(req_slots, dtype=jnp.int32)[None, :]).astype(
        jnp.int32
    )
    previous = jnp.concatenate([jnp.full((1,), -1, jnp.int32), groups[:-1]])
    is_prompt = (groups != previous).astype(jnp.int32)
    prompt_len = jnp.sum(
        lengths[None, :]
        * is_prompt[None, :]
        * (groups[None, :] == groups[:, None]).astype(jnp.int32),
        1,
    )
    offset_req = (1 - is_prompt) * prompt_len - starts
    group_row = jnp.sum(request_hot * groups[None, :], 1)
    prompt_row = jnp.sum(request_hot * is_prompt[None, :], 1)
    offset_row = jnp.sum(request_hot * offset_req[None, :], 1)
    token_positions = (row_ids + offset_row).astype(jnp.float32)
    prompt_start = jnp.sum(
        (starts * is_prompt)[None, :]
        * (groups[None, :] == jnp.arange(3, dtype=jnp.int32)[:, None]).astype(jnp.int32),
        1,
    )
    rows = (request_row, group_row, prompt_row, prompt_start)
    return (request_hot, starts, rows, token_positions, row_ids)


def per_device(
    tokens,
    input_norm_gain,
    query_matrix,
    key_matrix,
    value_matrix,
    output_matrix,
    adapter_down_maps,
    adapter_up_maps,
    request_row_counts,
    prompt_group_per_request,
    adapter_per_request,
    adapter_table_slot,
):
    tp_count = lax.axis_size("tp")
    req_count = lax.axis_size("req")
    tp_index = lax.axis_index("tp")
    tok_rows, width = tokens.shape
    piece_width = width // tp_count
    lengths = request_row_counts[0]
    groups = prompt_group_per_request[0]
    adapters = adapter_per_request[0]
    req_slots = lengths.shape[0]
    request_hot, starts, row_info, token_positions, row_ids = layout(lengths, groups, tok_rows)
    adapters_per_part = adapter_down_maps.shape[0]
    rank_extent = adapter_down_maps.shape[2]
    slots = adapter_table_slot[adapters]
    holder = slots // adapters_per_part
    local_slot = slots % adapters_per_part
    holder_ids = jnp.arange(req_count, dtype=jnp.int32)
    holder_hot = (holder[None, :] == holder_ids[:, None]).astype(jnp.int32)
    wanted = jnp.sum(holder_hot * local_slot[None, :], 1)
    wanted_in = lax.all_to_all(
        wanted.reshape(req_count, 1), "req", split_axis=0, concat_axis=0, tiled=True
    ).reshape(req_count)
    down_sel = jnp.transpose(adapter_down_maps[wanted_in], (0, 2, 1))
    up_sel = adapter_up_maps[wanted_in]
    maps_out = jnp.concatenate([down_sel, up_sel], 1)
    maps_in = lax.all_to_all(maps_out, "req", split_axis=0, concat_axis=0, tiled=True)
    down_in = maps_in[:, :rank_extent, :].reshape(req_count * rank_extent, piece_width)
    up_in = maps_in[:, rank_extent:, :].reshape(req_count * rank_extent, piece_width)
    float_tok = tokens.astype(jnp.float32)
    normalized_input = (
        float_tok
        * lax.rsqrt(jnp.mean(float_tok * float_tok, -1, keepdims=True) + 1e-06)
        * input_norm_gain
    ).astype(jnp.bfloat16)
    normed_slice = lax.dynamic_slice_in_dim(
        normalized_input, tp_index * piece_width, piece_width, 1
    )
    holder_row = jnp.sum(request_hot * holder[None, :], 1)
    pick = (holder_row[:, None] == holder_ids[None, :])[:, :, None]
    wide_rank = jnp.dot(
        normed_slice, down_in.T, preferred_element_type=jnp.float32
    ).reshape(tok_rows, req_count, rank_extent)
    partial_rank = jnp.sum(jnp.where(pick, wide_rank, jnp.float32(0.0)), 1)
    for step in (1, 2):
        pairs = [(i, i ^ step) for i in range(tp_count)]
        partial_rank = partial_rank + lax.ppermute(partial_rank, "tp", pairs)
    rank = partial_rank.astype(jnp.bfloat16)
    spread = jnp.where(pick, rank[:, None, :], jnp.zeros((), jnp.bfloat16)).reshape(
        tok_rows, req_count * rank_extent
    )
    query_delta = (
        2.0 * jnp.dot(spread, up_in, preferred_element_type=jnp.float32)
    ).astype(jnp.bfloat16)
    heads_local = query_matrix.shape[1] // HEAD_WIDTH
    kv_local = key_matrix.shape[1] // HEAD_WIDTH
    query_full = jnp.dot(
        normalized_input, query_matrix, preferred_element_type=jnp.float32
    ) + query_delta.astype(jnp.float32)
    query_heads = apply_rotary(
        query_full.reshape(tok_rows, heads_local, HEAD_WIDTH), token_positions
    ).astype(jnp.bfloat16)
    key_complete = jnp.dot(normalized_input, key_matrix, preferred_element_type=jnp.float32)
    key_head_rows = apply_rotary(
        key_complete.reshape(tok_rows, kv_local, HEAD_WIDTH), token_positions
    ).astype(jnp.bfloat16)
    value_head_rows = (
        jnp.dot(normalized_input, value_matrix, preferred_element_type=jnp.float32)
        .astype(jnp.bfloat16)
        .reshape(tok_rows, kv_local, HEAD_WIDTH)
    )
    request_row, group_row, prompt_row, prompt_start = row_info
    block = 128
    n_blocks = tok_rows // block
    rep = heads_local // kv_local
    prompt_rows = LMAX
    group_count = prompt_start.shape[0]
    pad_keys = jnp.zeros((block, kv_local, HEAD_WIDTH), jnp.bfloat16)
    key_pad = jnp.concatenate([pad_keys, key_head_rows], 0).reshape(
        n_blocks + 1, block, kv_local, HEAD_WIDTH
    )
    value_pad = jnp.concatenate([pad_keys, value_head_rows], 0).reshape(
        n_blocks + 1, block, kv_local, HEAD_WIDTH
    )
    key_win = jnp.concatenate([key_pad[:-1], key_pad[1:]], 1)
    value_win = jnp.concatenate([value_pad[:-1], value_pad[1:]], 1)
    win_row = (
        jnp.arange(n_blocks, dtype=jnp.int32)[:, None] * block
        - block
        + jnp.arange(2 * block, dtype=jnp.int32)[None, :]
    )
    clamp_start = jnp.clip(prompt_start, 0, tok_rows - prompt_rows)
    prompt_key_row = (
        clamp_start[:, None] + jnp.arange(prompt_rows, dtype=jnp.int32)[None, :]
    ).reshape(group_count * prompt_rows)
    prompt_owner = jnp.repeat(jnp.arange(group_count, dtype=jnp.int32), prompt_rows)
    extra = block - group_count * prompt_rows
    prompt_key_row = jnp.concatenate([prompt_key_row, jnp.zeros((extra,), jnp.int32)])
    prompt_owner = jnp.concatenate([prompt_owner, jnp.full((extra,), -1, jnp.int32)])
    key_prompt = key_head_rows[prompt_key_row]
    value_prompt = value_head_rows[prompt_key_row]
    win_safe = jnp.clip(win_row, 0, tok_rows - 1)
    query_blocks = query_heads.reshape(n_blocks, block, kv_local, rep, HEAD_WIDTH)
    q_rows = row_ids.reshape(n_blocks, block)
    chunk_blocks = 2
    pieces = []
    for c in range(n_blocks // chunk_blocks):
        bsl = slice(c * chunk_blocks, (c + 1) * chunk_blocks)
        qr = q_rows[bsl]
        wr = win_row[bsl]
        ws = win_safe[bsl]
        q_req = request_row[qr][:, :, None]
        q_grp = group_row[qr][:, :, None]
        win_vis = (
            (wr[:, None, :] >= 0)
            & (group_row[ws][:, None, :] == q_grp)
            & (wr[:, None, :] <= qr[:, :, None])
            & ((request_row[ws][:, None, :] == q_req) | (prompt_row[ws][:, None, :] == 1))
        )
        win_first = (qr[:, 0] - block)[:, None, None]
        p_row = prompt_key_row[None, None, :]
        prompt_vis = (
            (prompt_owner[None, None, :] == q_grp)
            & (group_row[prompt_key_row][None, None, :] == q_grp)
            & (prompt_row[prompt_key_row][None, None, :] == 1)
            & (p_row < win_first)
            & (p_row <= qr[:, :, None])
        )
        vis = jnp.concatenate([win_vis, prompt_vis], 2)
        keys = jnp.concatenate(
            [key_win[bsl], jnp.broadcast_to(key_prompt[None], (chunk_blocks,) + key_prompt.shape)], 1
        )
        values = jnp.concatenate(
            [value_win[bsl], jnp.broadcast_to(value_prompt[None], (chunk_blocks,) + value_prompt.shape)], 1
        )
        scores = (
            jnp.einsum(
                "bqgrd,bkgd->bgrqk", query_blocks[bsl], keys, preferred_element_type=jnp.float32
            )
            / HEAD_WIDTH**0.5
        )
        scores = jnp.where(vis[:, None, None], scores, jnp.float32(-1e30))
        row_max = jnp.max(scores, -1, keepdims=True)
        weights = jnp.exp(scores - row_max)
        probabilities = (weights / jnp.sum(weights, -1, keepdims=True)).astype(jnp.bfloat16)
        attended = jnp.einsum(
            "bgrqk,bkgd->bqgrd", probabilities, values, preferred_element_type=jnp.float32
        ).astype(jnp.bfloat16)
        head_term = jnp.dot(
            attended.reshape(chunk_blocks * block, heads_local * HEAD_WIDTH),
            output_matrix,
            preferred_element_type=jnp.float32,
        )
        pieces.append(
            lax.psum_scatter(head_term.astype(jnp.bfloat16), "tp", scatter_dimension=1, tiled=True)
        )
    summed = jnp.concatenate(pieces, 0).astype(jnp.float32)
    residual = lax.dynamic_slice_in_dim(tokens, tp_index * piece_width, piece_width, 1)
    return (residual.astype(jnp.float32) + summed).astype(jnp.bfloat16)


def solution(mesh):
    return jax.shard_map(
        per_device,
        mesh=mesh,
        in_specs=(
            P("req", None),
            P(),
            P(None, "tp"),
            P(None, "tp"),
            P(None, "tp"),
            P("tp", None),
            P("req", "tp", None),
            P("req", None, "tp"),
            P("req", None),
            P("req", None),
            P("req", None),
            P(),
        ),
        out_specs=P("req", "tp"),
        check_vma=False,
    )
```

```python
import jax
import jax.numpy as jnp
import functools
from jax import lax
from jax.experimental import pallas as pl
from jax.experimental.pallas import tpu as pltpu
from jax.sharding import PartitionSpec as P

HEAD_WIDTH = 128
REQ_DEV = 32
LMAX = 40


def apply_rotary(vectors, token_positions):
    head_size = vectors.shape[-1]
    half_dim = head_size // 2
    inverse = 1000000.0 ** (-(jnp.arange(half_dim, dtype=jnp.float32) * 2.0 / head_size))
    angles = token_positions[:, None] * inverse[None, :]
    cosine = jnp.cos(angles)[:, None, :]
    sine_part = jnp.sin(angles)[:, None, :]
    first_half = vectors[..., :half_dim]
    second = vectors[..., half_dim:]
    return jnp.concatenate(
        [first_half * cosine - second * sine_part, second * cosine + first_half * sine_part], -1
    )


def layout(lengths, groups, tok_rows):
    req_slots = lengths.shape[0]
    row_ids = jnp.arange(tok_rows, dtype=jnp.int32)
    row_ends = jnp.cumsum(lengths)
    starts = row_ends - lengths
    request_row = jnp.sum((row_ids[:, None] >= row_ends[None, :]).astype(jnp.int32), 1)
    request_hot = (request_row[:, None] == jnp.arange(req_slots, dtype=jnp.int32)[None, :]).astype(
        jnp.int32
    )
    previous = jnp.concatenate([jnp.full((1,), -1, jnp.int32), groups[:-1]])
    is_prompt = (groups != previous).astype(jnp.int32)
    prompt_len = jnp.sum(
        lengths[None, :]
        * is_prompt[None, :]
        * (groups[None, :] == groups[:, None]).astype(jnp.int32),
        1,
    )
    offset_req = (1 - is_prompt) * prompt_len - starts
    group_row = jnp.sum(request_hot * groups[None, :], 1)
    prompt_row = jnp.sum(request_hot * is_prompt[None, :], 1)
    offset_row = jnp.sum(request_hot * offset_req[None, :], 1)
    token_positions = (row_ids + offset_row).astype(jnp.float32)
    group_ids = jnp.arange(3, dtype=jnp.int32)
    group_hot = (groups[None, :] == group_ids[:, None]).astype(jnp.int32)
    prompt_start = jnp.sum((starts * is_prompt)[None, :] * group_hot, 1)
    prompt_len = jnp.sum((lengths * is_prompt)[None, :] * group_hot, 1)
    rows = (request_row, group_row, prompt_row, prompt_start, prompt_len)
    return (request_hot, starts, rows, token_positions, row_ids)


BLOCK = 128


def attend_kernel(
    q_ref, k_ref, v_ref, kp_ref, vp_ref, bias_ref, wo_ref, res_ref, out_ref,
    send_buf, recv_buf, send_sems, recv_sems, *, tp_count, heads, kv_heads, n_blocks
):
    me = lax.axis_index("tp")
    row_dev = lax.axis_index("req")
    piece = out_ref.shape[1]
    barrier = pltpu.get_barrier_semaphore()
    for k in range(1, tp_count):
        peer = lax.rem(me + k, tp_count)
        pl.semaphore_signal(
            barrier, inc=1, device_id=(row_dev, peer), device_id_type=pl.DeviceIdType.MESH
        )
    pl.semaphore_wait(barrier, tp_count - 1)
    rep = heads // kv_heads

    def copy_of(b, k, source):
        peer = lax.rem(me + k, tp_count)
        col = pl.multiple_of(peer * piece, piece)
        row = pl.multiple_of(b * BLOCK, BLOCK)
        return pltpu.make_async_remote_copy(
            src_ref=send_buf.at[b, :, pl.ds(col, piece)],
            dst_ref=recv_buf.at[source, pl.ds(row, BLOCK)],
            send_sem=send_sems.at[b * tp_count + k],
            recv_sem=recv_sems.at[source * n_blocks + b],
            device_id=(row_dev, peer),
            device_id_type=pl.DeviceIdType.MESH,
        )

    def block_body(b, carry):
        row = pl.multiple_of(b * BLOCK, BLOCK)
        bias = bias_ref[b]
        outs = []
        for h in range(heads):
            g = h // rep
            qh = q_ref[pl.ds(row, BLOCK), pl.ds(h * 128, 128)]
            kw = k_ref[pl.ds(row, 2 * BLOCK), pl.ds(g * 128, 128)]
            vw = v_ref[pl.ds(row, 2 * BLOCK), pl.ds(g * 128, 128)]
            kp = kp_ref[:, pl.ds(g * 128, 128)]
            vp = vp_ref[:, pl.ds(g * 128, 128)]
            keys = jnp.concatenate([kw, kp], 0)
            vals = jnp.concatenate([vw, vp], 0)
            s = lax.dot_general(
                qh, keys, (((1,), (1,)), ((), ())), preferred_element_type=jnp.float32
            ) / HEAD_WIDTH**0.5
            s = s + bias
            m = jnp.max(s, -1, keepdims=True)
            w = jnp.exp(s - m)
            p = (w / jnp.sum(w, -1, keepdims=True)).astype(jnp.bfloat16)
            outs.append(
                jnp.dot(p, vals, preferred_element_type=jnp.float32).astype(jnp.bfloat16)
            )
        att = jnp.concatenate(outs, 1)
        part = jnp.dot(att, wo_ref[...], preferred_element_type=jnp.float32)
        send_buf[b] = part.astype(jnp.bfloat16)
        for k in range(1, tp_count):
            copy_of(b, k, me).start()
        return carry

    lax.fori_loop(0, n_blocks, block_body, 0)

    def wait_body(b, carry):
        for k in range(1, tp_count):
            copy_of(b, k, me).wait_send()
            source = lax.rem(me + tp_count - k, tp_count)
            copy_of(b, k, source).wait_recv()
        return carry

    lax.fori_loop(0, n_blocks, wait_body, 0)
    own = pl.multiple_of(me * piece, piece)

    def finish_body(b, carry):
        row = pl.multiple_of(b * BLOCK, BLOCK)
        total = res_ref[pl.ds(row, BLOCK), :].astype(jnp.float32)
        total = total + send_buf[b, :, pl.ds(own, piece)].astype(jnp.float32)
        for k in range(1, tp_count):
            source = lax.rem(me + tp_count - k, tp_count)
            total = total + recv_buf[source, pl.ds(row, BLOCK), :].astype(jnp.float32)
        out_ref[pl.ds(row, BLOCK), :] = total.astype(out_ref.dtype)
        return carry

    lax.fori_loop(0, n_blocks, finish_body, 0)


def attend_and_reduce(q, k_pad, v_pad, k_prompt, v_prompt, bias, wo, residual, tp_count):
    rows, q_width = q.shape
    n_blocks = rows // BLOCK
    piece = residual.shape[1]
    width = wo.shape[1]
    kernel = functools.partial(
        attend_kernel,
        tp_count=tp_count,
        heads=q_width // HEAD_WIDTH,
        kv_heads=k_pad.shape[1] // HEAD_WIDTH,
        n_blocks=n_blocks,
    )
    vmem = pltpu.MemorySpace.VMEM
    return pl.pallas_call(
        kernel,
        out_shape=jax.ShapeDtypeStruct((rows, piece), jnp.bfloat16),
        in_specs=[pl.BlockSpec(memory_space=vmem)] * 8,
        out_specs=pl.BlockSpec(memory_space=vmem),
        scratch_shapes=[
            pltpu.VMEM((n_blocks, BLOCK, width), jnp.bfloat16),
            pltpu.VMEM((tp_count, rows, piece), jnp.bfloat16),
            pltpu.SemaphoreType.DMA((n_blocks * tp_count,)),
            pltpu.SemaphoreType.DMA((tp_count * n_blocks,)),
        ],
        compiler_params=pltpu.CompilerParams(
            collective_id=0, has_side_effects=True, vmem_limit_bytes=48 * 1024 * 1024
        ),
    )(q, k_pad, v_pad, k_prompt, v_prompt, bias, wo, residual)


def per_device(
    tokens,
    input_norm_gain,
    query_matrix,
    key_matrix,
    value_matrix,
    output_matrix,
    adapter_down_maps,
    adapter_up_maps,
    request_row_counts,
    prompt_group_per_request,
    adapter_per_request,
    adapter_table_slot,
):
    tp_count = lax.axis_size("tp")
    req_count = lax.axis_size("req")
    tp_index = lax.axis_index("tp")
    tok_rows, width = tokens.shape
    piece_width = width // tp_count
    lengths = request_row_counts[0]
    groups = prompt_group_per_request[0]
    adapters = adapter_per_request[0]
    req_slots = lengths.shape[0]
    request_hot, starts, row_info, token_positions, row_ids = layout(lengths, groups, tok_rows)
    adapters_per_part = adapter_down_maps.shape[0]
    rank_extent = adapter_down_maps.shape[2]
    slots = adapter_table_slot[adapters]
    holder = slots // adapters_per_part
    local_slot = slots % adapters_per_part
    holder_ids = jnp.arange(req_count, dtype=jnp.int32)
    holder_hot = (holder[None, :] == holder_ids[:, None]).astype(jnp.int32)
    wanted = jnp.sum(holder_hot * local_slot[None, :], 1)
    wanted_in = lax.all_to_all(
        wanted.reshape(req_count, 1), "req", split_axis=0, concat_axis=0, tiled=True
    ).reshape(req_count)
    down_sel = jnp.transpose(adapter_down_maps[wanted_in], (0, 2, 1))
    up_sel = adapter_up_maps[wanted_in]
    maps_out = jnp.concatenate([down_sel, up_sel], 1)
    maps_in = lax.all_to_all(maps_out, "req", split_axis=0, concat_axis=0, tiled=True)
    down_in = maps_in[:, :rank_extent, :].reshape(req_count * rank_extent, piece_width)
    up_in = maps_in[:, rank_extent:, :].reshape(req_count * rank_extent, piece_width)
    float_tok = tokens.astype(jnp.float32)
    normalized_input = (
        float_tok
        * lax.rsqrt(jnp.mean(float_tok * float_tok, -1, keepdims=True) + 1e-06)
        * input_norm_gain
    ).astype(jnp.bfloat16)
    normed_slice = lax.dynamic_slice_in_dim(
        normalized_input, tp_index * piece_width, piece_width, 1
    )
    holder_row = jnp.sum(request_hot * holder[None, :], 1)
    pick = (holder_row[:, None] == holder_ids[None, :])[:, :, None]
    wide_rank = jnp.dot(
        normed_slice, down_in.T, preferred_element_type=jnp.float32
    ).reshape(tok_rows, req_count, rank_extent)
    partial_rank = jnp.sum(jnp.where(pick, wide_rank, jnp.float32(0.0)), 1)
    for step in (1, 2):
        pairs = [(i, i ^ step) for i in range(tp_count)]
        partial_rank = partial_rank + lax.ppermute(partial_rank, "tp", pairs)
    rank = partial_rank.astype(jnp.bfloat16)
    spread = jnp.where(pick, rank[:, None, :], jnp.zeros((), jnp.bfloat16)).reshape(
        tok_rows, req_count * rank_extent
    )
    query_delta = (
        2.0 * jnp.dot(spread, up_in, preferred_element_type=jnp.float32)
    ).astype(jnp.bfloat16)
    heads_local = query_matrix.shape[1] // HEAD_WIDTH
    kv_local = key_matrix.shape[1] // HEAD_WIDTH
    query_full = jnp.dot(
        normalized_input, query_matrix, preferred_element_type=jnp.float32
    ) + query_delta.astype(jnp.float32)
    query_heads = apply_rotary(
        query_full.reshape(tok_rows, heads_local, HEAD_WIDTH), token_positions
    ).astype(jnp.bfloat16)
    key_complete = jnp.dot(normalized_input, key_matrix, preferred_element_type=jnp.float32)
    key_head_rows = apply_rotary(
        key_complete.reshape(tok_rows, kv_local, HEAD_WIDTH), token_positions
    ).astype(jnp.bfloat16)
    value_head_rows = (
        jnp.dot(normalized_input, value_matrix, preferred_element_type=jnp.float32)
        .astype(jnp.bfloat16)
        .reshape(tok_rows, kv_local, HEAD_WIDTH)
    )
    request_row, group_row, prompt_row, prompt_start, prompt_len = row_info
    n_blocks = tok_rows // BLOCK
    group_count = prompt_start.shape[0]
    kv_width = kv_local * HEAD_WIDTH
    key_flat = key_head_rows.reshape(tok_rows, kv_width)
    value_flat = value_head_rows.reshape(tok_rows, kv_width)
    front = jnp.zeros((BLOCK, kv_width), jnp.bfloat16)
    k_pad = jnp.concatenate([front, key_flat], 0)
    v_pad = jnp.concatenate([front, value_flat], 0)
    clamp_start = jnp.clip(prompt_start, 0, tok_rows - LMAX)
    extra = BLOCK - group_count * LMAX
    k_prompt = jnp.concatenate(
        [lax.dynamic_slice_in_dim(key_flat, clamp_start[g], LMAX, 0) for g in range(group_count)]
        + [jnp.zeros((extra, kv_width), jnp.bfloat16)],
        0,
    )
    v_prompt = jnp.concatenate(
        [lax.dynamic_slice_in_dim(value_flat, clamp_start[g], LMAX, 0) for g in range(group_count)]
        + [jnp.zeros((extra, kv_width), jnp.bfloat16)],
        0,
    )
    def windows(values, fill):
        padded = jnp.concatenate([jnp.full((BLOCK,), fill, values.dtype), values]).reshape(
            n_blocks + 1, BLOCK
        )
        return jnp.concatenate([padded[:-1], padded[1:]], 1)

    win_row = windows(row_ids, -1)
    win_req = windows(request_row, -1)
    win_grp = windows(group_row, -1)
    win_prm = windows(prompt_row, 0)
    q_row = row_ids.reshape(n_blocks, BLOCK)[:, :, None]
    q_req = request_row.reshape(n_blocks, BLOCK)[:, :, None]
    q_grp = group_row.reshape(n_blocks, BLOCK)[:, :, None]
    win_vis = (
        (win_row[:, None, :] >= 0)
        & (win_grp[:, None, :] == q_grp)
        & (win_row[:, None, :] <= q_row)
        & ((win_req[:, None, :] == q_req) | (win_prm[:, None, :] == 1))
    )
    p_row = (clamp_start[:, None] + jnp.arange(LMAX, dtype=jnp.int32)[None, :]).reshape(-1)
    p_lo = jnp.repeat(prompt_start, LMAX)
    p_hi = jnp.repeat(prompt_start + prompt_len, LMAX)
    p_grp = jnp.repeat(jnp.arange(group_count, dtype=jnp.int32), LMAX)
    p_row = jnp.concatenate([p_row, jnp.zeros((extra,), jnp.int32)])
    p_lo = jnp.concatenate([p_lo, jnp.ones((extra,), jnp.int32)])
    p_hi = jnp.concatenate([p_hi, jnp.zeros((extra,), jnp.int32)])
    p_grp = jnp.concatenate([p_grp, jnp.full((extra,), -1, jnp.int32)])
    win_first = q_row[:, :1, :] - BLOCK
    prompt_vis = (
        (p_grp[None, None, :] == q_grp)
        & (p_row[None, None, :] >= p_lo[None, None, :])
        & (p_row[None, None, :] < p_hi[None, None, :])
        & (p_row[None, None, :] < win_first)
        & (p_row[None, None, :] <= q_row)
    )
    vis = jnp.concatenate([win_vis, prompt_vis], 2)
    bias = jnp.where(vis, jnp.float32(0.0), jnp.float32(-1e30))
    residual = lax.dynamic_slice_in_dim(tokens, tp_index * piece_width, piece_width, 1)
    return attend_and_reduce(
        query_heads.reshape(tok_rows, heads_local * HEAD_WIDTH),
        k_pad,
        v_pad,
        k_prompt,
        v_prompt,
        bias,
        output_matrix,
        residual,
        tp_count,
    )


def solution(mesh):
    return jax.shard_map(
        per_device,
        mesh=mesh,
        in_specs=(
            P("req", None),
            P(),
            P(None, "tp"),
            P(None, "tp"),
            P(None, "tp"),
            P("tp", None),
            P("req", "tp", None),
            P("req", None, "tp"),
            P("req", None),
            P("req", None),
            P("req", None),
            P(),
        ),
        out_specs=P("req", "tp"),
        check_vma=False,
    )
```

```python
import jax
import jax.numpy as jnp
import functools
from jax import lax
from jax.experimental import pallas as pl
from jax.experimental.pallas import tpu as pltpu
from jax.sharding import PartitionSpec as P

HEAD_WIDTH = 128
REQ_DEV = 32
LMAX = 40


def apply_rotary(vectors, token_positions):
    head_size = vectors.shape[-1]
    half_dim = head_size // 2
    inverse = 1000000.0 ** (-(jnp.arange(half_dim, dtype=jnp.float32) * 2.0 / head_size))
    angles = token_positions[:, None] * inverse[None, :]
    cosine = jnp.cos(angles)[:, None, :]
    sine_part = jnp.sin(angles)[:, None, :]
    first_half = vectors[..., :half_dim]
    second = vectors[..., half_dim:]
    return jnp.concatenate(
        [first_half * cosine - second * sine_part, second * cosine + first_half * sine_part], -1
    )


def layout(lengths, groups, tok_rows):
    req_slots = lengths.shape[0]
    row_ids = jnp.arange(tok_rows, dtype=jnp.int32)
    row_ends = jnp.cumsum(lengths)
    starts = row_ends - lengths
    request_row = jnp.sum((row_ids[:, None] >= row_ends[None, :]).astype(jnp.int32), 1)
    request_hot = (request_row[:, None] == jnp.arange(req_slots, dtype=jnp.int32)[None, :]).astype(
        jnp.int32
    )
    previous = jnp.concatenate([jnp.full((1,), -1, jnp.int32), groups[:-1]])
    is_prompt = (groups != previous).astype(jnp.int32)
    prompt_len = jnp.sum(
        lengths[None, :]
        * is_prompt[None, :]
        * (groups[None, :] == groups[:, None]).astype(jnp.int32),
        1,
    )
    offset_req = (1 - is_prompt) * prompt_len - starts
    group_row = jnp.sum(request_hot * groups[None, :], 1)
    prompt_row = jnp.sum(request_hot * is_prompt[None, :], 1)
    offset_row = jnp.sum(request_hot * offset_req[None, :], 1)
    token_positions = (row_ids + offset_row).astype(jnp.float32)
    group_ids = jnp.arange(3, dtype=jnp.int32)
    group_hot = (groups[None, :] == group_ids[:, None]).astype(jnp.int32)
    prompt_start = jnp.sum((starts * is_prompt)[None, :] * group_hot, 1)
    prompt_len = jnp.sum((lengths * is_prompt)[None, :] * group_hot, 1)
    rows = (request_row, group_row, prompt_row, prompt_start, prompt_len)
    return (request_hot, starts, rows, token_positions, row_ids)


BLOCK = 128


def attend_kernel(
    q_ref, k_ref, v_ref, kp_ref, vp_ref, bias_ref, wo_ref, res_ref, out_ref,
    send_buf, recv_buf, send_sems, recv_sems, *, tp_count, heads, kv_heads, n_blocks
):
    me = lax.axis_index("tp")
    row_dev = lax.axis_index("req")
    piece = out_ref.shape[1]
    barrier = pltpu.get_barrier_semaphore()
    for k in range(1, tp_count):
        peer = lax.rem(me + k, tp_count)
        pl.semaphore_signal(
            barrier, inc=1, device_id=(row_dev, peer), device_id_type=pl.DeviceIdType.MESH
        )
    pl.semaphore_wait(barrier, tp_count - 1)
    rep = heads // kv_heads

    def copy_of(b, k, source):
        peer = lax.rem(me + k, tp_count)
        col = pl.multiple_of(peer * piece, piece)
        row = pl.multiple_of(b * BLOCK, BLOCK)
        return pltpu.make_async_remote_copy(
            src_ref=send_buf.at[b, :, pl.ds(col, piece)],
            dst_ref=recv_buf.at[source, pl.ds(row, BLOCK)],
            send_sem=send_sems.at[b * tp_count + k],
            recv_sem=recv_sems.at[source * n_blocks + b],
            device_id=(row_dev, peer),
            device_id_type=pl.DeviceIdType.MESH,
        )

    def block_body(b, carry):
        row = pl.multiple_of(b * BLOCK, BLOCK)
        bias = bias_ref[b]
        outs = []
        for h in range(heads):
            g = h // rep
            qh = q_ref[pl.ds(row, BLOCK), pl.ds(h * 128, 128)]
            kw = k_ref[pl.ds(row, 2 * BLOCK), pl.ds(g * 128, 128)]
            vw = v_ref[pl.ds(row, 2 * BLOCK), pl.ds(g * 128, 128)]
            kp = kp_ref[:, pl.ds(g * 128, 128)]
            vp = vp_ref[:, pl.ds(g * 128, 128)]
            keys = jnp.concatenate([kw, kp], 0)
            vals = jnp.concatenate([vw, vp], 0)
            s = lax.dot_general(
                qh, keys, (((1,), (1,)), ((), ())), preferred_element_type=jnp.float32
            ) / HEAD_WIDTH**0.5
            s = s + bias
            m = jnp.max(s, -1, keepdims=True)
            w = jnp.exp(s - m)
            p = (w / jnp.sum(w, -1, keepdims=True)).astype(jnp.bfloat16)
            outs.append(
                jnp.dot(p, vals, preferred_element_type=jnp.float32).astype(jnp.bfloat16)
            )
        att = jnp.concatenate(outs, 1)
        part = jnp.dot(att, wo_ref[...], preferred_element_type=jnp.float32)
        send_buf[b] = part.astype(jnp.bfloat16)
        for k in range(1, tp_count):
            copy_of(b, k, me).start()
        return carry

    lax.fori_loop(0, n_blocks, block_body, 0)

    def wait_body(b, carry):
        for k in range(1, tp_count):
            copy_of(b, k, me).wait_send()
            source = lax.rem(me + tp_count - k, tp_count)
            copy_of(b, k, source).wait_recv()
        return carry

    lax.fori_loop(0, n_blocks, wait_body, 0)
    own = pl.multiple_of(me * piece, piece)

    def finish_body(b, carry):
        row = pl.multiple_of(b * BLOCK, BLOCK)
        total = res_ref[pl.ds(row, BLOCK), :].astype(jnp.float32)
        total = total + send_buf[b, :, pl.ds(own, piece)].astype(jnp.float32)
        for k in range(1, tp_count):
            source = lax.rem(me + tp_count - k, tp_count)
            total = total + recv_buf[source, pl.ds(row, BLOCK), :].astype(jnp.float32)
        out_ref[pl.ds(row, BLOCK), :] = total.astype(out_ref.dtype)
        return carry

    lax.fori_loop(0, n_blocks, finish_body, 0)


def attend_and_reduce(q, k_pad, v_pad, k_prompt, v_prompt, bias, wo, residual, tp_count):
    rows, q_width = q.shape
    n_blocks = rows // BLOCK
    piece = residual.shape[1]
    width = wo.shape[1]
    kernel = functools.partial(
        attend_kernel,
        tp_count=tp_count,
        heads=q_width // HEAD_WIDTH,
        kv_heads=k_pad.shape[1] // HEAD_WIDTH,
        n_blocks=n_blocks,
    )
    vmem = pltpu.MemorySpace.VMEM
    return pl.pallas_call(
        kernel,
        out_shape=jax.ShapeDtypeStruct((rows, piece), jnp.bfloat16),
        in_specs=[pl.BlockSpec(memory_space=vmem)] * 8,
        out_specs=pl.BlockSpec(memory_space=vmem),
        scratch_shapes=[
            pltpu.VMEM((n_blocks, BLOCK, width), jnp.bfloat16),
            pltpu.VMEM((tp_count, rows, piece), jnp.bfloat16),
            pltpu.SemaphoreType.DMA((n_blocks * tp_count,)),
            pltpu.SemaphoreType.DMA((tp_count * n_blocks,)),
        ],
        compiler_params=pltpu.CompilerParams(
            collective_id=0, has_side_effects=True, vmem_limit_bytes=48 * 1024 * 1024
        ),
    )(q, k_pad, v_pad, k_prompt, v_prompt, bias, wo, residual)


def exchange_kernel(wanted_ref, table_ref, out_ref, staging, landing, send_sems, recv_sems):
    me = lax.axis_index("req")
    col = lax.axis_index("tp")
    count = lax.axis_size("req")
    barrier = pltpu.get_barrier_semaphore()

    def greet(k, carry):
        peer = lax.rem(me + k, count)
        pl.semaphore_signal(
            barrier, inc=1, device_id=(peer, col), device_id_type=pl.DeviceIdType.MESH
        )
        return carry

    lax.fori_loop(1, count, greet, 0)
    pl.semaphore_wait(barrier, count - 1)

    def send(k, carry):
        dest = lax.rem(me + k, count)
        staging[dest] = table_ref[wanted_ref[dest]]
        pltpu.make_async_remote_copy(
            src_ref=staging.at[dest],
            dst_ref=landing.at[me],
            send_sem=send_sems.at[k],
            recv_sem=recv_sems.at[k],
            device_id=(dest, col),
            device_id_type=pl.DeviceIdType.MESH,
        ).start()
        return carry

    lax.fori_loop(1, count, send, 0)
    out_ref[me] = table_ref[wanted_ref[me]]

    def finish(k, carry):
        dest = lax.rem(me + k, count)
        source = lax.rem(me + count - k, count)
        pltpu.make_async_remote_copy(
            src_ref=staging.at[dest],
            dst_ref=landing.at[me],
            send_sem=send_sems.at[k],
            recv_sem=recv_sems.at[k],
            device_id=(dest, col),
            device_id_type=pl.DeviceIdType.MESH,
        ).wait_send()
        pltpu.make_async_remote_copy(
            src_ref=staging.at[source],
            dst_ref=landing.at[source],
            send_sem=send_sems.at[k],
            recv_sem=recv_sems.at[k],
            device_id=(source, col),
            device_id_type=pl.DeviceIdType.MESH,
        ).wait_recv()
        out_ref[source] = landing[source]
        return carry

    lax.fori_loop(1, count, finish, 0)


def exchange_maps(wanted, table):
    count = wanted.shape[0]
    slab = table.shape[1:]
    vmem = pltpu.MemorySpace.VMEM
    return pl.pallas_call(
        exchange_kernel,
        out_shape=jax.ShapeDtypeStruct((count,) + slab, table.dtype),
        in_specs=[
            pl.BlockSpec(memory_space=pltpu.MemorySpace.SMEM),
            pl.BlockSpec(memory_space=vmem),
        ],
        out_specs=pl.BlockSpec(memory_space=vmem),
        scratch_shapes=[
            pltpu.VMEM((count,) + slab, table.dtype),
            pltpu.VMEM((count,) + slab, table.dtype),
            pltpu.SemaphoreType.DMA((count,)),
            pltpu.SemaphoreType.DMA((count,)),
        ],
        compiler_params=pltpu.CompilerParams(
            collective_id=1, has_side_effects=True, vmem_limit_bytes=32 * 1024 * 1024
        ),
    )(wanted, table)


def per_device(
    tokens,
    input_norm_gain,
    query_matrix,
    key_matrix,
    value_matrix,
    output_matrix,
    adapter_down_maps,
    adapter_up_maps,
    request_row_counts,
    prompt_group_per_request,
    adapter_per_request,
    adapter_table_slot,
):
    tp_count = lax.axis_size("tp")
    req_count = lax.axis_size("req")
    tp_index = lax.axis_index("tp")
    tok_rows, width = tokens.shape
    piece_width = width // tp_count
    lengths = request_row_counts[0]
    groups = prompt_group_per_request[0]
    adapters = adapter_per_request[0]
    req_slots = lengths.shape[0]
    request_hot, starts, row_info, token_positions, row_ids = layout(lengths, groups, tok_rows)
    adapters_per_part = adapter_down_maps.shape[0]
    rank_extent = adapter_down_maps.shape[2]
    slots = adapter_table_slot[adapters]
    holder = slots // adapters_per_part
    local_slot = slots % adapters_per_part
    holder_ids = jnp.arange(req_count, dtype=jnp.int32)
    holder_hot = (holder[None, :] == holder_ids[:, None]).astype(jnp.int32)
    wanted = jnp.sum(holder_hot * local_slot[None, :], 1)
    wanted_in = lax.all_to_all(
        wanted.reshape(req_count, 1), "req", split_axis=0, concat_axis=0, tiled=True
    ).reshape(req_count)
    table = jnp.concatenate([jnp.transpose(adapter_down_maps, (0, 2, 1)), adapter_up_maps], 1)
    maps_in = exchange_maps(wanted_in, table)
    down_in = maps_in[:, :rank_extent, :].reshape(req_count * rank_extent, piece_width)
    up_in = maps_in[:, rank_extent:, :].reshape(req_count * rank_extent, piece_width)
    float_tok = tokens.astype(jnp.float32)
    normalized_input = (
        float_tok
        * lax.rsqrt(jnp.mean(float_tok * float_tok, -1, keepdims=True) + 1e-06)
        * input_norm_gain
    ).astype(jnp.bfloat16)
    normed_slice = lax.dynamic_slice_in_dim(
        normalized_input, tp_index * piece_width, piece_width, 1
    )
    holder_row = jnp.sum(request_hot * holder[None, :], 1)
    pick = (holder_row[:, None] == holder_ids[None, :])[:, :, None]
    wide_rank = jnp.dot(
        normed_slice, down_in.T, preferred_element_type=jnp.float32
    ).reshape(tok_rows, req_count, rank_extent)
    partial_rank = jnp.sum(jnp.where(pick, wide_rank, jnp.float32(0.0)), 1)
    for step in (1, 2):
        pairs = [(i, i ^ step) for i in range(tp_count)]
        partial_rank = partial_rank + lax.ppermute(partial_rank, "tp", pairs)
    rank = partial_rank.astype(jnp.bfloat16)
    spread = jnp.where(pick, rank[:, None, :], jnp.zeros((), jnp.bfloat16)).reshape(
        tok_rows, req_count * rank_extent
    )
    query_delta = (
        2.0 * jnp.dot(spread, up_in, preferred_element_type=jnp.float32)
    ).astype(jnp.bfloat16)
    heads_local = query_matrix.shape[1] // HEAD_WIDTH
    kv_local = key_matrix.shape[1] // HEAD_WIDTH
    query_full = jnp.dot(
        normalized_input, query_matrix, preferred_element_type=jnp.float32
    ) + query_delta.astype(jnp.float32)
    query_heads = apply_rotary(
        query_full.reshape(tok_rows, heads_local, HEAD_WIDTH), token_positions
    ).astype(jnp.bfloat16)
    key_complete = jnp.dot(normalized_input, key_matrix, preferred_element_type=jnp.float32)
    key_head_rows = apply_rotary(
        key_complete.reshape(tok_rows, kv_local, HEAD_WIDTH), token_positions
    ).astype(jnp.bfloat16)
    value_head_rows = (
        jnp.dot(normalized_input, value_matrix, preferred_element_type=jnp.float32)
        .astype(jnp.bfloat16)
        .reshape(tok_rows, kv_local, HEAD_WIDTH)
    )
    request_row, group_row, prompt_row, prompt_start, prompt_len = row_info
    n_blocks = tok_rows // BLOCK
    group_count = prompt_start.shape[0]
    kv_width = kv_local * HEAD_WIDTH
    key_flat = key_head_rows.reshape(tok_rows, kv_width)
    value_flat = value_head_rows.reshape(tok_rows, kv_width)
    front = jnp.zeros((BLOCK, kv_width), jnp.bfloat16)
    k_pad = jnp.concatenate([front, key_flat], 0)
    v_pad = jnp.concatenate([front, value_flat], 0)
    clamp_start = jnp.clip(prompt_start, 0, tok_rows - LMAX)
    extra = BLOCK - group_count * LMAX
    k_prompt = jnp.concatenate(
        [lax.dynamic_slice_in_dim(key_flat, clamp_start[g], LMAX, 0) for g in range(group_count)]
        + [jnp.zeros((extra, kv_width), jnp.bfloat16)],
        0,
    )
    v_prompt = jnp.concatenate(
        [lax.dynamic_slice_in_dim(value_flat, clamp_start[g], LMAX, 0) for g in range(group_count)]
        + [jnp.zeros((extra, kv_width), jnp.bfloat16)],
        0,
    )
    def windows(values, fill):
        padded = jnp.concatenate([jnp.full((BLOCK,), fill, values.dtype), values]).reshape(
            n_blocks + 1, BLOCK
        )
        return jnp.concatenate([padded[:-1], padded[1:]], 1)

    win_row = windows(row_ids, -1)
    win_req = windows(request_row, -1)
    win_grp = windows(group_row, -1)
    win_prm = windows(prompt_row, 0)
    q_row = row_ids.reshape(n_blocks, BLOCK)[:, :, None]
    q_req = request_row.reshape(n_blocks, BLOCK)[:, :, None]
    q_grp = group_row.reshape(n_blocks, BLOCK)[:, :, None]
    win_vis = (
        (win_row[:, None, :] >= 0)
        & (win_grp[:, None, :] == q_grp)
        & (win_row[:, None, :] <= q_row)
        & ((win_req[:, None, :] == q_req) | (win_prm[:, None, :] == 1))
    )
    p_row = (clamp_start[:, None] + jnp.arange(LMAX, dtype=jnp.int32)[None, :]).reshape(-1)
    p_lo = jnp.repeat(prompt_start, LMAX)
    p_hi = jnp.repeat(prompt_start + prompt_len, LMAX)
    p_grp = jnp.repeat(jnp.arange(group_count, dtype=jnp.int32), LMAX)
    p_row = jnp.concatenate([p_row, jnp.zeros((extra,), jnp.int32)])
    p_lo = jnp.concatenate([p_lo, jnp.ones((extra,), jnp.int32)])
    p_hi = jnp.concatenate([p_hi, jnp.zeros((extra,), jnp.int32)])
    p_grp = jnp.concatenate([p_grp, jnp.full((extra,), -1, jnp.int32)])
    win_first = q_row[:, :1, :] - BLOCK
    prompt_vis = (
        (p_grp[None, None, :] == q_grp)
        & (p_row[None, None, :] >= p_lo[None, None, :])
        & (p_row[None, None, :] < p_hi[None, None, :])
        & (p_row[None, None, :] < win_first)
        & (p_row[None, None, :] <= q_row)
    )
    vis = jnp.concatenate([win_vis, prompt_vis], 2)
    bias = jnp.where(vis, jnp.float32(0.0), jnp.float32(-1e30))
    residual = lax.dynamic_slice_in_dim(tokens, tp_index * piece_width, piece_width, 1)
    return attend_and_reduce(
        query_heads.reshape(tok_rows, heads_local * HEAD_WIDTH),
        k_pad,
        v_pad,
        k_prompt,
        v_prompt,
        bias,
        output_matrix,
        residual,
        tp_count,
    )


def solution(mesh):
    return jax.shard_map(
        per_device,
        mesh=mesh,
        in_specs=(
            P("req", None),
            P(),
            P(None, "tp"),
            P(None, "tp"),
            P(None, "tp"),
            P("tp", None),
            P("req", "tp", None),
            P("req", None, "tp"),
            P("req", None),
            P("req", None),
            P("req", None),
            P(),
        ),
        out_specs=P("req", "tp"),
        check_vma=False,
    )
```

```python
import jax
import jax.numpy as jnp
import functools
from jax import lax
from jax.experimental import pallas as pl
from jax.experimental.pallas import tpu as pltpu
from jax.sharding import PartitionSpec as P

HEAD_WIDTH = 128
REQ_DEV = 32
LMAX = 40


def apply_rotary(vectors, token_positions):
    head_size = vectors.shape[-1]
    half_dim = head_size // 2
    inverse = 1000000.0 ** (-(jnp.arange(half_dim, dtype=jnp.float32) * 2.0 / head_size))
    angles = token_positions[:, None] * inverse[None, :]
    cosine = jnp.cos(angles)[:, None, :]
    sine_part = jnp.sin(angles)[:, None, :]
    first_half = vectors[..., :half_dim]
    second = vectors[..., half_dim:]
    return jnp.concatenate(
        [first_half * cosine - second * sine_part, second * cosine + first_half * sine_part], -1
    )


def layout(lengths, groups, tok_rows):
    req_slots = lengths.shape[0]
    row_ids = jnp.arange(tok_rows, dtype=jnp.int32)
    row_ends = jnp.cumsum(lengths)
    starts = row_ends - lengths
    request_row = jnp.sum((row_ids[:, None] >= row_ends[None, :]).astype(jnp.int32), 1)
    request_hot = (request_row[:, None] == jnp.arange(req_slots, dtype=jnp.int32)[None, :]).astype(
        jnp.int32
    )
    previous = jnp.concatenate([jnp.full((1,), -1, jnp.int32), groups[:-1]])
    is_prompt = (groups != previous).astype(jnp.int32)
    prompt_len = jnp.sum(
        lengths[None, :]
        * is_prompt[None, :]
        * (groups[None, :] == groups[:, None]).astype(jnp.int32),
        1,
    )
    offset_req = (1 - is_prompt) * prompt_len - starts
    group_row = jnp.sum(request_hot * groups[None, :], 1)
    prompt_row = jnp.sum(request_hot * is_prompt[None, :], 1)
    offset_row = jnp.sum(request_hot * offset_req[None, :], 1)
    token_positions = (row_ids + offset_row).astype(jnp.float32)
    group_ids = jnp.arange(3, dtype=jnp.int32)
    group_hot = (groups[None, :] == group_ids[:, None]).astype(jnp.int32)
    prompt_start = jnp.sum((starts * is_prompt)[None, :] * group_hot, 1)
    prompt_len = jnp.sum((lengths * is_prompt)[None, :] * group_hot, 1)
    rows = (request_row, group_row, prompt_row, prompt_start, prompt_len)
    return (request_hot, starts, rows, token_positions, row_ids)


BLOCK = 128


def attend_kernel(
    qb_ref, spread_ref, up_ref, cs_ref, sn_ref, k_ref, v_ref, kp_ref, vp_ref, bias_ref, wo_ref,
    tok_ref, out_ref,
    send_buf, recv_buf, send_sems, recv_sems, *, tp_count, heads, kv_heads, n_blocks
):
    me = lax.axis_index("tp")
    row_dev = lax.axis_index("req")
    piece = out_ref.shape[1]
    barrier = pltpu.get_barrier_semaphore()
    for k in range(1, tp_count):
        peer = lax.rem(me + k, tp_count)
        pl.semaphore_signal(
            barrier, inc=1, device_id=(row_dev, peer), device_id_type=pl.DeviceIdType.MESH
        )
    pl.semaphore_wait(barrier, tp_count - 1)
    rep = heads // kv_heads

    def copy_of(b, k, source):
        peer = lax.rem(me + k, tp_count)
        col = pl.multiple_of(peer * piece, piece)
        row = pl.multiple_of(b * BLOCK, BLOCK)
        return pltpu.make_async_remote_copy(
            src_ref=send_buf.at[b, :, pl.ds(col, piece)],
            dst_ref=recv_buf.at[source, pl.ds(row, BLOCK)],
            send_sem=send_sems.at[b * tp_count + k],
            recv_sem=recv_sems.at[source * n_blocks + b],
            device_id=(row_dev, peer),
            device_id_type=pl.DeviceIdType.MESH,
        )

    def block_body(b, carry):
        row = pl.multiple_of(b * BLOCK, BLOCK)
        first = pl.multiple_of(jnp.maximum(b - 1, 0) * BLOCK, BLOCK)
        bias = bias_ref[b]
        delta = (
            2.0
            * jnp.dot(
                spread_ref[pl.ds(row, BLOCK), :], up_ref[...], preferred_element_type=jnp.float32
            )
        ).astype(jnp.bfloat16).astype(jnp.float32)
        cs = cs_ref[pl.ds(row, BLOCK), :]
        sn = sn_ref[pl.ds(row, BLOCK), :]
        outs = []
        for h in range(heads):
            g = h // rep
            dh = delta[:, h * 128 : (h + 1) * 128]
            qh = (
                qb_ref[pl.ds(row, BLOCK), pl.ds(h * 128, 128)]
                + (dh * cs + pltpu.roll(dh, 64, 1) * sn)
            ).astype(jnp.bfloat16)
            kw = k_ref[pl.ds(first, 2 * BLOCK), pl.ds(g * 128, 128)]
            vw = v_ref[pl.ds(first, 2 * BLOCK), pl.ds(g * 128, 128)]
            kp = kp_ref[:, pl.ds(g * 128, 128)]
            vp = vp_ref[:, pl.ds(g * 128, 128)]
            keys = jnp.concatenate([kw, kp], 0)
            vals = jnp.concatenate([vw, vp], 0)
            s = lax.dot_general(
                qh, keys, (((1,), (1,)), ((), ())), preferred_element_type=jnp.float32
            ) / HEAD_WIDTH**0.5
            s = s + bias
            m = jnp.max(s, -1, keepdims=True)
            w = jnp.exp(s - m)
            p = (w / jnp.sum(w, -1, keepdims=True)).astype(jnp.bfloat16)
            outs.append(
                jnp.dot(p, vals, preferred_element_type=jnp.float32).astype(jnp.bfloat16)
            )
        att = jnp.concatenate(outs, 1)
        part = jnp.dot(att, wo_ref[...], preferred_element_type=jnp.float32)
        send_buf[b] = part.astype(jnp.bfloat16)
        for k in range(1, tp_count):
            copy_of(b, k, me).start()
        return carry

    lax.fori_loop(0, n_blocks, block_body, 0)

    def wait_body(b, carry):
        for k in range(1, tp_count):
            copy_of(b, k, me).wait_send()
            source = lax.rem(me + tp_count - k, tp_count)
            copy_of(b, k, source).wait_recv()
        return carry

    lax.fori_loop(0, n_blocks, wait_body, 0)
    own = pl.multiple_of(me * piece, piece)

    def finish_body(b, carry):
        row = pl.multiple_of(b * BLOCK, BLOCK)
        total = tok_ref[pl.ds(row, BLOCK), pl.ds(own, piece)].astype(jnp.float32)
        total = total + send_buf[b, :, pl.ds(own, piece)].astype(jnp.float32)
        for k in range(1, tp_count):
            source = lax.rem(me + tp_count - k, tp_count)
            total = total + recv_buf[source, pl.ds(row, BLOCK), :].astype(jnp.float32)
        out_ref[pl.ds(row, BLOCK), :] = total.astype(out_ref.dtype)
        return carry

    lax.fori_loop(0, n_blocks, finish_body, 0)


def attend_and_reduce(qb, spread, up, cs, sn, keys, values, k_prompt, v_prompt, bias, wo, tokens, tp_count):
    rows, q_width = qb.shape
    n_blocks = rows // BLOCK
    width = wo.shape[1]
    piece = width // tp_count
    kernel = functools.partial(
        attend_kernel,
        tp_count=tp_count,
        heads=q_width // HEAD_WIDTH,
        kv_heads=keys.shape[1] // HEAD_WIDTH,
        n_blocks=n_blocks,
    )
    vmem = pltpu.MemorySpace.VMEM
    return pl.pallas_call(
        kernel,
        out_shape=jax.ShapeDtypeStruct((rows, piece), jnp.bfloat16),
        in_specs=[pl.BlockSpec(memory_space=vmem)] * 12,
        out_specs=pl.BlockSpec(memory_space=vmem),
        scratch_shapes=[
            pltpu.VMEM((n_blocks, BLOCK, width), jnp.bfloat16),
            pltpu.VMEM((tp_count, rows, piece), jnp.bfloat16),
            pltpu.SemaphoreType.DMA((n_blocks * tp_count,)),
            pltpu.SemaphoreType.DMA((tp_count * n_blocks,)),
        ],
        compiler_params=pltpu.CompilerParams(
            collective_id=0, has_side_effects=True, vmem_limit_bytes=48 * 1024 * 1024
        ),
    )(qb, spread, up, cs, sn, keys, values, k_prompt, v_prompt, bias, wo, tokens)


def per_device(
    tokens,
    input_norm_gain,
    query_matrix,
    key_matrix,
    value_matrix,
    output_matrix,
    adapter_down_maps,
    adapter_up_maps,
    request_row_counts,
    prompt_group_per_request,
    adapter_per_request,
    adapter_table_slot,
):
    tp_count = lax.axis_size("tp")
    req_count = lax.axis_size("req")
    tp_index = lax.axis_index("tp")
    tok_rows, width = tokens.shape
    piece_width = width // tp_count
    lengths = request_row_counts[0]
    groups = prompt_group_per_request[0]
    adapters = adapter_per_request[0]
    req_slots = lengths.shape[0]
    request_hot, starts, row_info, token_positions, row_ids = layout(lengths, groups, tok_rows)
    adapters_per_part = adapter_down_maps.shape[0]
    rank_extent = adapter_down_maps.shape[2]
    slots = adapter_table_slot[adapters]
    holder = slots // adapters_per_part
    local_slot = slots % adapters_per_part
    holder_ids = jnp.arange(req_count, dtype=jnp.int32)
    holder_hot = (holder[None, :] == holder_ids[:, None]).astype(jnp.int32)
    wanted = jnp.sum(holder_hot * local_slot[None, :], 1)
    wanted_in = lax.all_to_all(
        wanted.reshape(req_count, 1), "req", split_axis=0, concat_axis=0, tiled=True
    ).reshape(req_count)
    down_sel = jnp.transpose(adapter_down_maps[wanted_in], (0, 2, 1))
    up_sel = adapter_up_maps[wanted_in]
    maps_out = jnp.concatenate([down_sel, up_sel], 1)
    maps_in = lax.all_to_all(maps_out, "req", split_axis=0, concat_axis=0, tiled=True)
    down_in = maps_in[:, :rank_extent, :].reshape(req_count * rank_extent, piece_width)
    up_in = maps_in[:, rank_extent:, :].reshape(req_count * rank_extent, piece_width)
    float_tok = tokens.astype(jnp.float32)
    normalized_input = (
        float_tok
        * lax.rsqrt(jnp.mean(float_tok * float_tok, -1, keepdims=True) + 1e-06)
        * input_norm_gain
    ).astype(jnp.bfloat16)
    normed_slice = lax.dynamic_slice_in_dim(
        normalized_input, tp_index * piece_width, piece_width, 1
    )
    holder_row = jnp.sum(request_hot * holder[None, :], 1)
    pick = (holder_row[:, None] == holder_ids[None, :])[:, :, None]
    wide_rank = jnp.dot(
        normed_slice, down_in.T, preferred_element_type=jnp.float32
    ).reshape(tok_rows, req_count, rank_extent)
    partial_rank = jnp.sum(jnp.where(pick, wide_rank, jnp.float32(0.0)), 1)
    for step in (1, 2):
        pairs = [(i, i ^ step) for i in range(tp_count)]
        partial_rank = partial_rank + lax.ppermute(partial_rank, "tp", pairs)
    rank = partial_rank.astype(jnp.bfloat16)
    spread = jnp.where(pick, rank[:, None, :], jnp.zeros((), jnp.bfloat16)).reshape(
        tok_rows, req_count * rank_extent
    )
    heads_local = query_matrix.shape[1] // HEAD_WIDTH
    kv_local = key_matrix.shape[1] // HEAD_WIDTH
    query_base = jnp.dot(normalized_input, query_matrix, preferred_element_type=jnp.float32)
    query_rot = apply_rotary(
        query_base.reshape(tok_rows, heads_local, HEAD_WIDTH), token_positions
    ).reshape(tok_rows, heads_local * HEAD_WIDTH)
    half_dim = HEAD_WIDTH // 2
    inverse = 1000000.0 ** (-(jnp.arange(half_dim, dtype=jnp.float32) * 2.0 / HEAD_WIDTH))
    angles = token_positions[:, None] * inverse[None, :]
    cosine = jnp.cos(angles)
    sine = jnp.sin(angles)
    cos_pair = jnp.concatenate([cosine, cosine], 1)
    sin_pair = jnp.concatenate([-sine, sine], 1)
    key_complete = jnp.dot(normalized_input, key_matrix, preferred_element_type=jnp.float32)
    key_head_rows = apply_rotary(
        key_complete.reshape(tok_rows, kv_local, HEAD_WIDTH), token_positions
    ).astype(jnp.bfloat16)
    value_head_rows = (
        jnp.dot(normalized_input, value_matrix, preferred_element_type=jnp.float32)
        .astype(jnp.bfloat16)
        .reshape(tok_rows, kv_local, HEAD_WIDTH)
    )
    request_row, group_row, prompt_row, prompt_start, prompt_len = row_info
    n_blocks = tok_rows // BLOCK
    group_count = prompt_start.shape[0]
    kv_width = kv_local * HEAD_WIDTH
    key_flat = key_head_rows.reshape(tok_rows, kv_width)
    value_flat = value_head_rows.reshape(tok_rows, kv_width)
    clamp_start = jnp.clip(prompt_start, 0, tok_rows - LMAX)
    extra = BLOCK - group_count * LMAX
    k_prompt = jnp.concatenate(
        [lax.dynamic_slice_in_dim(key_flat, clamp_start[g], LMAX, 0) for g in range(group_count)]
        + [jnp.zeros((extra, kv_width), jnp.bfloat16)],
        0,
    )
    v_prompt = jnp.concatenate(
        [lax.dynamic_slice_in_dim(value_flat, clamp_start[g], LMAX, 0) for g in range(group_count)]
        + [jnp.zeros((extra, kv_width), jnp.bfloat16)],
        0,
    )
    firsts = [max(b - 1, 0) for b in range(n_blocks)]

    def windows(values):
        blocks = values.reshape(n_blocks, BLOCK)
        lo = jnp.stack([blocks[f] for f in firsts])
        hi = jnp.stack([blocks[f + 1] for f in firsts])
        return jnp.concatenate([lo, hi], 1)

    win_row = windows(row_ids)
    win_req = windows(request_row)
    win_grp = windows(group_row)
    win_prm = windows(prompt_row)
    q_row = row_ids.reshape(n_blocks, BLOCK)[:, :, None]
    q_req = request_row.reshape(n_blocks, BLOCK)[:, :, None]
    q_grp = group_row.reshape(n_blocks, BLOCK)[:, :, None]
    win_vis = (
        (win_grp[:, None, :] == q_grp)
        & (win_row[:, None, :] <= q_row)
        & ((win_req[:, None, :] == q_req) | (win_prm[:, None, :] == 1))
    )
    p_row = (clamp_start[:, None] + jnp.arange(LMAX, dtype=jnp.int32)[None, :]).reshape(-1)
    p_lo = jnp.repeat(prompt_start, LMAX)
    p_hi = jnp.repeat(prompt_start + prompt_len, LMAX)
    p_grp = jnp.repeat(jnp.arange(group_count, dtype=jnp.int32), LMAX)
    p_row = jnp.concatenate([p_row, jnp.zeros((extra,), jnp.int32)])
    p_lo = jnp.concatenate([p_lo, jnp.ones((extra,), jnp.int32)])
    p_hi = jnp.concatenate([p_hi, jnp.zeros((extra,), jnp.int32)])
    p_grp = jnp.concatenate([p_grp, jnp.full((extra,), -1, jnp.int32)])
    win_first = win_row[:, :1][:, :, None]
    prompt_vis = (
        (p_grp[None, None, :] == q_grp)
        & (p_row[None, None, :] >= p_lo[None, None, :])
        & (p_row[None, None, :] < p_hi[None, None, :])
        & (p_row[None, None, :] < win_first)
        & (p_row[None, None, :] <= q_row)
    )
    vis = jnp.concatenate([win_vis, prompt_vis], 2)
    bias = jnp.where(vis, jnp.float32(0.0), jnp.float32(-1e30))
    return attend_and_reduce(
        query_rot,
        spread,
        up_in,
        cos_pair,
        sin_pair,
        key_flat,
        value_flat,
        k_prompt,
        v_prompt,
        bias,
        output_matrix,
        tokens,
        tp_count,
    )


def solution(mesh):
    return jax.shard_map(
        per_device,
        mesh=mesh,
        in_specs=(
            P("req", None),
            P(),
            P(None, "tp"),
            P(None, "tp"),
            P(None, "tp"),
            P("tp", None),
            P("req", "tp", None),
            P("req", None, "tp"),
            P("req", None),
            P("req", None),
            P("req", None),
            P(),
        ),
        out_specs=P("req", "tp"),
        check_vma=False,
    )
```

```python
import jax
import jax.numpy as jnp
import functools
from jax import lax
from jax.experimental import pallas as pl
from jax.experimental.pallas import tpu as pltpu
from jax.sharding import PartitionSpec as P

HEAD_WIDTH = 128
REQ_DEV = 32
LMAX = 40


def apply_rotary(vectors, token_positions):
    head_size = vectors.shape[-1]
    half_dim = head_size // 2
    inverse = 1000000.0 ** (-(jnp.arange(half_dim, dtype=jnp.float32) * 2.0 / head_size))
    angles = token_positions[:, None] * inverse[None, :]
    cosine = jnp.cos(angles)[:, None, :]
    sine_part = jnp.sin(angles)[:, None, :]
    first_half = vectors[..., :half_dim]
    second = vectors[..., half_dim:]
    return jnp.concatenate(
        [first_half * cosine - second * sine_part, second * cosine + first_half * sine_part], -1
    )


def layout(lengths, groups, tok_rows):
    req_slots = lengths.shape[0]
    row_ids = jnp.arange(tok_rows, dtype=jnp.int32)
    row_ends = jnp.cumsum(lengths)
    starts = row_ends - lengths
    request_row = jnp.sum((row_ids[:, None] >= row_ends[None, :]).astype(jnp.int32), 1)
    request_hot = (request_row[:, None] == jnp.arange(req_slots, dtype=jnp.int32)[None, :]).astype(
        jnp.int32
    )
    previous = jnp.concatenate([jnp.full((1,), -1, jnp.int32), groups[:-1]])
    is_prompt = (groups != previous).astype(jnp.int32)
    prompt_len = jnp.sum(
        lengths[None, :]
        * is_prompt[None, :]
        * (groups[None, :] == groups[:, None]).astype(jnp.int32),
        1,
    )
    offset_req = (1 - is_prompt) * prompt_len - starts
    group_row = jnp.sum(request_hot * groups[None, :], 1)
    prompt_row = jnp.sum(request_hot * is_prompt[None, :], 1)
    offset_row = jnp.sum(request_hot * offset_req[None, :], 1)
    token_positions = (row_ids + offset_row).astype(jnp.float32)
    group_ids = jnp.arange(3, dtype=jnp.int32)
    group_hot = (groups[None, :] == group_ids[:, None]).astype(jnp.int32)
    prompt_start = jnp.sum((starts * is_prompt)[None, :] * group_hot, 1)
    prompt_len = jnp.sum((lengths * is_prompt)[None, :] * group_hot, 1)
    rows = (request_row, group_row, prompt_row, prompt_start, prompt_len)
    return (request_hot, starts, rows, token_positions, row_ids)


BLOCK = 128


def attend_kernel(
    q_ref, k_ref, v_ref, kp_ref, vp_ref, bias_ref, wo_ref, res_ref, out_ref,
    send_buf, recv_buf, send_sems, recv_sems, *, tp_count, heads, kv_heads, n_blocks
):
    me = lax.axis_index("tp")
    row_dev = lax.axis_index("req")
    piece = out_ref.shape[1]
    barrier = pltpu.get_barrier_semaphore()
    for k in range(1, tp_count):
        peer = lax.rem(me + k, tp_count)
        pl.semaphore_signal(
            barrier, inc=1, device_id=(row_dev, peer), device_id_type=pl.DeviceIdType.MESH
        )
    pl.semaphore_wait(barrier, tp_count - 1)
    rep = heads // kv_heads

    def copy_of(b, k, source):
        peer = lax.rem(me + k, tp_count)
        col = pl.multiple_of(peer * piece, piece)
        row = pl.multiple_of(b * BLOCK, BLOCK)
        return pltpu.make_async_remote_copy(
            src_ref=send_buf.at[b, :, pl.ds(col, piece)],
            dst_ref=recv_buf.at[source, pl.ds(row, BLOCK)],
            send_sem=send_sems.at[b * tp_count + k],
            recv_sem=recv_sems.at[source * n_blocks + b],
            device_id=(row_dev, peer),
            device_id_type=pl.DeviceIdType.MESH,
        )

    def block_body(b, carry):
        row = pl.multiple_of(b * BLOCK, BLOCK)
        bias = bias_ref[b]
        outs = []
        for h in range(heads):
            g = h // rep
            qh = q_ref[pl.ds(row, BLOCK), pl.ds(h * 128, 128)]
            kw = k_ref[pl.ds(row, 2 * BLOCK), pl.ds(g * 128, 128)]
            vw = v_ref[pl.ds(row, 2 * BLOCK), pl.ds(g * 128, 128)]
            kp = kp_ref[:, pl.ds(g * 128, 128)]
            vp = vp_ref[:, pl.ds(g * 128, 128)]
            keys = jnp.concatenate([kw, kp], 0)
            vals = jnp.concatenate([vw, vp], 0)
            s = lax.dot_general(
                qh, keys, (((1,), (1,)), ((), ())), preferred_element_type=jnp.float32
            ) / HEAD_WIDTH**0.5
            s = s + bias
            m = jnp.max(s, -1, keepdims=True)
            w = jnp.exp(s - m)
            p = (w / jnp.sum(w, -1, keepdims=True)).astype(jnp.bfloat16)
            outs.append(
                jnp.dot(p, vals, preferred_element_type=jnp.float32).astype(jnp.bfloat16)
            )
        att = jnp.concatenate(outs, 1)
        part = jnp.dot(att, wo_ref[...], preferred_element_type=jnp.float32)
        send_buf[b] = part.astype(jnp.bfloat16)
        for k in range(1, tp_count):
            copy_of(b, k, me).start()
        return carry

    lax.fori_loop(0, n_blocks, block_body, 0)

    def wait_body(b, carry):
        for k in range(1, tp_count):
            copy_of(b, k, me).wait_send()
            source = lax.rem(me + tp_count - k, tp_count)
            copy_of(b, k, source).wait_recv()
        return carry

    lax.fori_loop(0, n_blocks, wait_body, 0)
    own = pl.multiple_of(me * piece, piece)

    def finish_body(b, carry):
        row = pl.multiple_of(b * BLOCK, BLOCK)
        total = res_ref[pl.ds(row, BLOCK), :].astype(jnp.float32)
        total = total + send_buf[b, :, pl.ds(own, piece)].astype(jnp.float32)
        for k in range(1, tp_count):
            source = lax.rem(me + tp_count - k, tp_count)
            total = total + recv_buf[source, pl.ds(row, BLOCK), :].astype(jnp.float32)
        out_ref[pl.ds(row, BLOCK), :] = total.astype(out_ref.dtype)
        return carry

    lax.fori_loop(0, n_blocks, finish_body, 0)


def attend_and_reduce(q, k_pad, v_pad, k_prompt, v_prompt, bias, wo, residual, tp_count):
    rows, q_width = q.shape
    n_blocks = rows // BLOCK
    piece = residual.shape[1]
    width = wo.shape[1]
    kernel = functools.partial(
        attend_kernel,
        tp_count=tp_count,
        heads=q_width // HEAD_WIDTH,
        kv_heads=k_pad.shape[1] // HEAD_WIDTH,
        n_blocks=n_blocks,
    )
    vmem = pltpu.MemorySpace.VMEM
    return pl.pallas_call(
        kernel,
        out_shape=jax.ShapeDtypeStruct((rows, piece), jnp.bfloat16),
        in_specs=[pl.BlockSpec(memory_space=vmem)] * 8,
        out_specs=pl.BlockSpec(memory_space=vmem),
        scratch_shapes=[
            pltpu.VMEM((n_blocks, BLOCK, width), jnp.bfloat16),
            pltpu.VMEM((tp_count, rows, piece), jnp.bfloat16),
            pltpu.SemaphoreType.DMA((n_blocks * tp_count,)),
            pltpu.SemaphoreType.DMA((tp_count * n_blocks,)),
        ],
        compiler_params=pltpu.CompilerParams(
            collective_id=0, has_side_effects=True, vmem_limit_bytes=48 * 1024 * 1024
        ),
    )(q, k_pad, v_pad, k_prompt, v_prompt, bias, wo, residual)


def per_device(
    tokens,
    input_norm_gain,
    query_matrix,
    key_matrix,
    value_matrix,
    output_matrix,
    adapter_down_maps,
    adapter_up_maps,
    request_row_counts,
    prompt_group_per_request,
    adapter_per_request,
    adapter_table_slot,
):
    tp_count = lax.axis_size("tp")
    req_count = lax.axis_size("req")
    tp_index = lax.axis_index("tp")
    tok_rows, width = tokens.shape
    piece_width = width // tp_count
    lengths = request_row_counts[0]
    groups = prompt_group_per_request[0]
    adapters = adapter_per_request[0]
    req_slots = lengths.shape[0]
    request_hot, starts, row_info, token_positions, row_ids = layout(lengths, groups, tok_rows)
    adapters_per_part = adapter_down_maps.shape[0]
    rank_extent = adapter_down_maps.shape[2]
    slots = adapter_table_slot[adapters]
    holder = slots // adapters_per_part
    local_slot = slots % adapters_per_part
    holder_ids = jnp.arange(req_count, dtype=jnp.int32)
    holder_hot = (holder[None, :] == holder_ids[:, None]).astype(jnp.int32)
    wanted = jnp.sum(holder_hot * local_slot[None, :], 1)
    wanted_in = lax.all_to_all(
        wanted.reshape(req_count, 1), "req", split_axis=0, concat_axis=0, tiled=True
    ).reshape(req_count)
    down_sel = jnp.transpose(adapter_down_maps[wanted_in], (0, 2, 1))
    up_sel = adapter_up_maps[wanted_in]
    maps_out = jnp.concatenate([down_sel, up_sel], 1)
    maps_in = lax.all_to_all(maps_out, "req", split_axis=0, concat_axis=0, tiled=True)
    down_in = maps_in[:, :rank_extent, :].reshape(req_count * rank_extent, piece_width)
    up_in = maps_in[:, rank_extent:, :].reshape(req_count * rank_extent, piece_width)
    float_tok = tokens.astype(jnp.float32)
    normalized_input = (
        float_tok
        * lax.rsqrt(jnp.mean(float_tok * float_tok, -1, keepdims=True) + 1e-06)
        * input_norm_gain
    ).astype(jnp.bfloat16)
    normed_slice = lax.dynamic_slice_in_dim(
        normalized_input, tp_index * piece_width, piece_width, 1
    )
    holder_row = jnp.sum(request_hot * holder[None, :], 1)
    pick = (holder_row[:, None] == holder_ids[None, :])[:, :, None]
    wide_rank = jnp.dot(
        normed_slice, down_in.T, preferred_element_type=jnp.float32
    ).reshape(tok_rows, req_count, rank_extent)
    partial_rank = jnp.sum(jnp.where(pick, wide_rank, jnp.float32(0.0)), 1)
    for step in (1, 2):
        pairs = [(i, i ^ step) for i in range(tp_count)]
        partial_rank = partial_rank + lax.ppermute(partial_rank, "tp", pairs)
    rank = partial_rank.astype(jnp.bfloat16)
    spread = jnp.where(pick, rank[:, None, :], jnp.zeros((), jnp.bfloat16)).reshape(
        tok_rows, req_count * rank_extent
    )
    heads_local = query_matrix.shape[1] // HEAD_WIDTH
    kv_local = key_matrix.shape[1] // HEAD_WIDTH
    half_dim = HEAD_WIDTH // 2
    query_base = jnp.dot(normalized_input, query_matrix, preferred_element_type=jnp.float32)
    query_rot = apply_rotary(
        query_base.reshape(tok_rows, heads_local, HEAD_WIDTH), token_positions
    ).reshape(tok_rows, heads_local * HEAD_WIDTH)
    inverse = 1000000.0 ** (-(jnp.arange(half_dim, dtype=jnp.float32) * 2.0 / HEAD_WIDTH))
    angles = token_positions[:, None] * inverse[None, :]
    cosine = jnp.cos(angles)
    sine = jnp.sin(angles)
    cos_wide = jnp.tile(jnp.concatenate([cosine, cosine], 1), (1, heads_local))
    sin_wide = jnp.tile(jnp.concatenate([sine, sine], 1), (1, heads_local))
    up_halves = up_in.reshape(up_in.shape[0], heads_local, 2, half_dim)
    up_turned = jnp.concatenate([-up_halves[:, :, 1:], up_halves[:, :, :1]], 2).reshape(
        up_in.shape
    )
    both = (
        2.0
        * jnp.dot(
            spread,
            jnp.concatenate([up_in, up_turned], 1),
            preferred_element_type=jnp.float32,
        )
    ).astype(jnp.bfloat16).astype(jnp.float32)
    q_width = heads_local * HEAD_WIDTH
    query_heads = (
        query_rot + both[:, :q_width] * cos_wide + both[:, q_width:] * sin_wide
    ).astype(jnp.bfloat16)
    key_complete = jnp.dot(normalized_input, key_matrix, preferred_element_type=jnp.float32)
    key_head_rows = apply_rotary(
        key_complete.reshape(tok_rows, kv_local, HEAD_WIDTH), token_positions
    ).astype(jnp.bfloat16)
    value_head_rows = (
        jnp.dot(normalized_input, value_matrix, preferred_element_type=jnp.float32)
        .astype(jnp.bfloat16)
        .reshape(tok_rows, kv_local, HEAD_WIDTH)
    )
    request_row, group_row, prompt_row, prompt_start, prompt_len = row_info
    n_blocks = tok_rows // BLOCK
    group_count = prompt_start.shape[0]
    kv_width = kv_local * HEAD_WIDTH
    key_flat = key_head_rows.reshape(tok_rows, kv_width)
    value_flat = value_head_rows.reshape(tok_rows, kv_width)
    front = jnp.zeros((BLOCK, kv_width), jnp.bfloat16)
    k_pad = jnp.concatenate([front, key_flat], 0)
    v_pad = jnp.concatenate([front, value_flat], 0)
    clamp_start = jnp.clip(prompt_start, 0, tok_rows - LMAX)
    extra = BLOCK - group_count * LMAX
    k_prompt = jnp.concatenate(
        [lax.dynamic_slice_in_dim(key_flat, clamp_start[g], LMAX, 0) for g in range(group_count)]
        + [jnp.zeros((extra, kv_width), jnp.bfloat16)],
        0,
    )
    v_prompt = jnp.concatenate(
        [lax.dynamic_slice_in_dim(value_flat, clamp_start[g], LMAX, 0) for g in range(group_count)]
        + [jnp.zeros((extra, kv_width), jnp.bfloat16)],
        0,
    )
    def windows(values, fill):
        padded = jnp.concatenate([jnp.full((BLOCK,), fill, values.dtype), values]).reshape(
            n_blocks + 1, BLOCK
        )
        return jnp.concatenate([padded[:-1], padded[1:]], 1)

    win_row = windows(row_ids, -1)
    win_req = windows(request_row, -1)
    win_grp = windows(group_row, -1)
    win_prm = windows(prompt_row, 0)
    q_row = row_ids.reshape(n_blocks, BLOCK)[:, :, None]
    q_req = request_row.reshape(n_blocks, BLOCK)[:, :, None]
    q_grp = group_row.reshape(n_blocks, BLOCK)[:, :, None]
    win_vis = (
        (win_row[:, None, :] >= 0)
        & (win_grp[:, None, :] == q_grp)
        & (win_row[:, None, :] <= q_row)
        & ((win_req[:, None, :] == q_req) | (win_prm[:, None, :] == 1))
    )
    p_row = (clamp_start[:, None] + jnp.arange(LMAX, dtype=jnp.int32)[None, :]).reshape(-1)
    p_lo = jnp.repeat(prompt_start, LMAX)
    p_hi = jnp.repeat(prompt_start + prompt_len, LMAX)
    p_grp = jnp.repeat(jnp.arange(group_count, dtype=jnp.int32), LMAX)
    p_row = jnp.concatenate([p_row, jnp.zeros((extra,), jnp.int32)])
    p_lo = jnp.concatenate([p_lo, jnp.ones((extra,), jnp.int32)])
    p_hi = jnp.concatenate([p_hi, jnp.zeros((extra,), jnp.int32)])
    p_grp = jnp.concatenate([p_grp, jnp.full((extra,), -1, jnp.int32)])
    win_first = q_row[:, :1, :] - BLOCK
    prompt_vis = (
        (p_grp[None, None, :] == q_grp)
        & (p_row[None, None, :] >= p_lo[None, None, :])
        & (p_row[None, None, :] < p_hi[None, None, :])
        & (p_row[None, None, :] < win_first)
        & (p_row[None, None, :] <= q_row)
    )
    vis = jnp.concatenate([win_vis, prompt_vis], 2)
    bias = jnp.where(vis, jnp.float32(0.0), jnp.float32(-1e30))
    residual = lax.dynamic_slice_in_dim(tokens, tp_index * piece_width, piece_width, 1)
    return attend_and_reduce(
        query_heads,
        k_pad,
        v_pad,
        k_prompt,
        v_prompt,
        bias,
        output_matrix,
        residual,
        tp_count,
    )


def solution(mesh):
    return jax.shard_map(
        per_device,
        mesh=mesh,
        in_specs=(
            P("req", None),
            P(),
            P(None, "tp"),
            P(None, "tp"),
            P(None, "tp"),
            P("tp", None),
            P("req", "tp", None),
            P("req", None, "tp"),
            P("req", None),
            P("req", None),
            P("req", None),
            P(),
        ),
        out_specs=P("req", "tp"),
        check_vma=False,
    )
```

```python
import jax
import jax.numpy as jnp
import functools
from jax import lax
from jax.experimental import pallas as pl
from jax.experimental.pallas import tpu as pltpu
from jax.sharding import PartitionSpec as P

HEAD_WIDTH = 128
REQ_DEV = 32
LMAX = 40


def apply_rotary(vectors, token_positions):
    head_size = vectors.shape[-1]
    half_dim = head_size // 2
    inverse = 1000000.0 ** (-(jnp.arange(half_dim, dtype=jnp.float32) * 2.0 / head_size))
    angles = token_positions[:, None] * inverse[None, :]
    cosine = jnp.cos(angles)[:, None, :]
    sine_part = jnp.sin(angles)[:, None, :]
    first_half = vectors[..., :half_dim]
    second = vectors[..., half_dim:]
    return jnp.concatenate(
        [first_half * cosine - second * sine_part, second * cosine + first_half * sine_part], -1
    )


def layout(lengths, groups, tok_rows):
    req_slots = lengths.shape[0]
    row_ids = jnp.arange(tok_rows, dtype=jnp.int32)
    row_ends = jnp.cumsum(lengths)
    starts = row_ends - lengths
    request_row = jnp.sum((row_ids[:, None] >= row_ends[None, :]).astype(jnp.int32), 1)
    request_hot = (request_row[:, None] == jnp.arange(req_slots, dtype=jnp.int32)[None, :]).astype(
        jnp.int32
    )
    previous = jnp.concatenate([jnp.full((1,), -1, jnp.int32), groups[:-1]])
    is_prompt = (groups != previous).astype(jnp.int32)
    prompt_len = jnp.sum(
        lengths[None, :]
        * is_prompt[None, :]
        * (groups[None, :] == groups[:, None]).astype(jnp.int32),
        1,
    )
    offset_req = (1 - is_prompt) * prompt_len - starts
    group_row = jnp.sum(request_hot * groups[None, :], 1)
    prompt_row = jnp.sum(request_hot * is_prompt[None, :], 1)
    offset_row = jnp.sum(request_hot * offset_req[None, :], 1)
    token_positions = (row_ids + offset_row).astype(jnp.float32)
    group_ids = jnp.arange(3, dtype=jnp.int32)
    group_hot = (groups[None, :] == group_ids[:, None]).astype(jnp.int32)
    prompt_start = jnp.sum((starts * is_prompt)[None, :] * group_hot, 1)
    prompt_len = jnp.sum((lengths * is_prompt)[None, :] * group_hot, 1)
    rows = (request_row, group_row, prompt_row, prompt_start, prompt_len)
    return (request_hot, starts, rows, token_positions, row_ids)


BLOCK = 128


def attend_kernel(
    q_ref, cs_ref, sn_ref, k_ref, v_ref, kp_ref, vp_ref, bias_ref, wo_ref, res_ref, out_ref,
    send_buf, recv_buf, send_sems, recv_sems, *, tp_count, heads, kv_heads, n_blocks
):
    me = lax.axis_index("tp")
    row_dev = lax.axis_index("req")
    piece = out_ref.shape[1]
    barrier = pltpu.get_barrier_semaphore()
    for k in range(1, tp_count):
        peer = lax.rem(me + k, tp_count)
        pl.semaphore_signal(
            barrier, inc=1, device_id=(row_dev, peer), device_id_type=pl.DeviceIdType.MESH
        )
    pl.semaphore_wait(barrier, tp_count - 1)
    rep = heads // kv_heads

    def copy_of(b, k, source):
        peer = lax.rem(me + k, tp_count)
        col = pl.multiple_of(peer * piece, piece)
        row = pl.multiple_of(b * BLOCK, BLOCK)
        return pltpu.make_async_remote_copy(
            src_ref=send_buf.at[b, :, pl.ds(col, piece)],
            dst_ref=recv_buf.at[source, pl.ds(row, BLOCK)],
            send_sem=send_sems.at[b * tp_count + k],
            recv_sem=recv_sems.at[source * n_blocks + b],
            device_id=(row_dev, peer),
            device_id_type=pl.DeviceIdType.MESH,
        )

    def block_body(b, carry):
        row = pl.multiple_of(b * BLOCK, BLOCK)
        bias = bias_ref[b]
        cs = cs_ref[pl.ds(row, BLOCK), :]
        sn = sn_ref[pl.ds(row, BLOCK), :]
        outs = []
        for h in range(heads):
            g = h // rep
            qf = q_ref[pl.ds(row, BLOCK), pl.ds(h * 128, 128)]
            qh = (qf * cs + pltpu.roll(qf, 64, 1) * sn).astype(jnp.bfloat16)
            kw = k_ref[pl.ds(row, 2 * BLOCK), pl.ds(g * 128, 128)]
            vw = v_ref[pl.ds(row, 2 * BLOCK), pl.ds(g * 128, 128)]
            kp = kp_ref[:, pl.ds(g * 128, 128)]
            vp = vp_ref[:, pl.ds(g * 128, 128)]
            keys = jnp.concatenate([kw, kp], 0)
            vals = jnp.concatenate([vw, vp], 0)
            s = lax.dot_general(
                qh, keys, (((1,), (1,)), ((), ())), preferred_element_type=jnp.float32
            ) / HEAD_WIDTH**0.5
            s = s + bias
            m = jnp.max(s, -1, keepdims=True)
            w = jnp.exp(s - m)
            p = (w / jnp.sum(w, -1, keepdims=True)).astype(jnp.bfloat16)
            outs.append(
                jnp.dot(p, vals, preferred_element_type=jnp.float32).astype(jnp.bfloat16)
            )
        att = jnp.concatenate(outs, 1)
        part = jnp.dot(att, wo_ref[...], preferred_element_type=jnp.float32)
        send_buf[b] = part.astype(jnp.bfloat16)
        for k in range(1, tp_count):
            copy_of(b, k, me).start()
        return carry

    lax.fori_loop(0, n_blocks, block_body, 0)

    def wait_body(b, carry):
        for k in range(1, tp_count):
            copy_of(b, k, me).wait_send()
            source = lax.rem(me + tp_count - k, tp_count)
            copy_of(b, k, source).wait_recv()
        return carry

    lax.fori_loop(0, n_blocks, wait_body, 0)
    own = pl.multiple_of(me * piece, piece)

    def finish_body(b, carry):
        row = pl.multiple_of(b * BLOCK, BLOCK)
        total = res_ref[pl.ds(row, BLOCK), :].astype(jnp.float32)
        total = total + send_buf[b, :, pl.ds(own, piece)].astype(jnp.float32)
        for k in range(1, tp_count):
            source = lax.rem(me + tp_count - k, tp_count)
            total = total + recv_buf[source, pl.ds(row, BLOCK), :].astype(jnp.float32)
        out_ref[pl.ds(row, BLOCK), :] = total.astype(out_ref.dtype)
        return carry

    lax.fori_loop(0, n_blocks, finish_body, 0)


def attend_and_reduce(q, cs, sn, k_pad, v_pad, k_prompt, v_prompt, bias, wo, residual, tp_count):
    rows, q_width = q.shape
    n_blocks = rows // BLOCK
    piece = residual.shape[1]
    width = wo.shape[1]
    kernel = functools.partial(
        attend_kernel,
        tp_count=tp_count,
        heads=q_width // HEAD_WIDTH,
        kv_heads=k_pad.shape[1] // HEAD_WIDTH,
        n_blocks=n_blocks,
    )
    vmem = pltpu.MemorySpace.VMEM
    return pl.pallas_call(
        kernel,
        out_shape=jax.ShapeDtypeStruct((rows, piece), jnp.bfloat16),
        in_specs=[pl.BlockSpec(memory_space=vmem)] * 10,
        out_specs=pl.BlockSpec(memory_space=vmem),
        scratch_shapes=[
            pltpu.VMEM((n_blocks, BLOCK, width), jnp.bfloat16),
            pltpu.VMEM((tp_count, rows, piece), jnp.bfloat16),
            pltpu.SemaphoreType.DMA((n_blocks * tp_count,)),
            pltpu.SemaphoreType.DMA((tp_count * n_blocks,)),
        ],
        compiler_params=pltpu.CompilerParams(
            collective_id=0, has_side_effects=True, vmem_limit_bytes=48 * 1024 * 1024
        ),
    )(q, cs, sn, k_pad, v_pad, k_prompt, v_prompt, bias, wo, residual)


def per_device(
    tokens,
    input_norm_gain,
    query_matrix,
    key_matrix,
    value_matrix,
    output_matrix,
    adapter_down_maps,
    adapter_up_maps,
    request_row_counts,
    prompt_group_per_request,
    adapter_per_request,
    adapter_table_slot,
):
    tp_count = lax.axis_size("tp")
    req_count = lax.axis_size("req")
    tp_index = lax.axis_index("tp")
    tok_rows, width = tokens.shape
    piece_width = width // tp_count
    lengths = request_row_counts[0]
    groups = prompt_group_per_request[0]
    adapters = adapter_per_request[0]
    req_slots = lengths.shape[0]
    request_hot, starts, row_info, token_positions, row_ids = layout(lengths, groups, tok_rows)
    adapters_per_part = adapter_down_maps.shape[0]
    rank_extent = adapter_down_maps.shape[2]
    slots = adapter_table_slot[adapters]
    holder = slots // adapters_per_part
    local_slot = slots % adapters_per_part
    holder_ids = jnp.arange(req_count, dtype=jnp.int32)
    holder_hot = (holder[None, :] == holder_ids[:, None]).astype(jnp.int32)
    wanted = jnp.sum(holder_hot * local_slot[None, :], 1)
    wanted_in = lax.all_to_all(
        wanted.reshape(req_count, 1), "req", split_axis=0, concat_axis=0, tiled=True
    ).reshape(req_count)
    down_sel = jnp.transpose(adapter_down_maps[wanted_in], (0, 2, 1))
    up_sel = adapter_up_maps[wanted_in]
    maps_out = jnp.concatenate([down_sel, up_sel], 1)
    maps_in = lax.all_to_all(maps_out, "req", split_axis=0, concat_axis=0, tiled=True)
    down_in = maps_in[:, :rank_extent, :].reshape(req_count * rank_extent, piece_width)
    up_in = maps_in[:, rank_extent:, :].reshape(req_count * rank_extent, piece_width)
    float_tok = tokens.astype(jnp.float32)
    normalized_input = (
        float_tok
        * lax.rsqrt(jnp.mean(float_tok * float_tok, -1, keepdims=True) + 1e-06)
        * input_norm_gain
    ).astype(jnp.bfloat16)
    normed_slice = lax.dynamic_slice_in_dim(
        normalized_input, tp_index * piece_width, piece_width, 1
    )
    holder_row = jnp.sum(request_hot * holder[None, :], 1)
    pick = (holder_row[:, None] == holder_ids[None, :])[:, :, None]
    wide_rank = jnp.dot(
        normed_slice, down_in.T, preferred_element_type=jnp.float32
    ).reshape(tok_rows, req_count, rank_extent)
    partial_rank = jnp.sum(jnp.where(pick, wide_rank, jnp.float32(0.0)), 1)
    for step in (1, 2):
        pairs = [(i, i ^ step) for i in range(tp_count)]
        partial_rank = partial_rank + lax.ppermute(partial_rank, "tp", pairs)
    rank = partial_rank.astype(jnp.bfloat16)
    spread = jnp.where(pick, rank[:, None, :], jnp.zeros((), jnp.bfloat16)).reshape(
        tok_rows, req_count * rank_extent
    )
    query_delta = (
        2.0 * jnp.dot(spread, up_in, preferred_element_type=jnp.float32)
    ).astype(jnp.bfloat16)
    heads_local = query_matrix.shape[1] // HEAD_WIDTH
    kv_local = key_matrix.shape[1] // HEAD_WIDTH
    query_full = jnp.dot(
        normalized_input, query_matrix, preferred_element_type=jnp.float32
    ) + query_delta.astype(jnp.float32)
    half_dim = HEAD_WIDTH // 2
    inverse = 1000000.0 ** (-(jnp.arange(half_dim, dtype=jnp.float32) * 2.0 / HEAD_WIDTH))
    angles = token_positions[:, None] * inverse[None, :]
    cosine = jnp.cos(angles)
    sine = jnp.sin(angles)
    cos_pair = jnp.concatenate([cosine, cosine], 1)
    sin_pair = jnp.concatenate([-sine, sine], 1)
    key_complete = jnp.dot(normalized_input, key_matrix, preferred_element_type=jnp.float32)
    key_head_rows = apply_rotary(
        key_complete.reshape(tok_rows, kv_local, HEAD_WIDTH), token_positions
    ).astype(jnp.bfloat16)
    value_head_rows = (
        jnp.dot(normalized_input, value_matrix, preferred_element_type=jnp.float32)
        .astype(jnp.bfloat16)
        .reshape(tok_rows, kv_local, HEAD_WIDTH)
    )
    request_row, group_row, prompt_row, prompt_start, prompt_len = row_info
    n_blocks = tok_rows // BLOCK
    group_count = prompt_start.shape[0]
    kv_width = kv_local * HEAD_WIDTH
    key_flat = key_head_rows.reshape(tok_rows, kv_width)
    value_flat = value_head_rows.reshape(tok_rows, kv_width)
    front = jnp.zeros((BLOCK, kv_width), jnp.bfloat16)
    k_pad = jnp.concatenate([front, key_flat], 0)
    v_pad = jnp.concatenate([front, value_flat], 0)
    clamp_start = jnp.clip(prompt_start, 0, tok_rows - LMAX)
    extra = BLOCK - group_count * LMAX
    k_prompt = jnp.concatenate(
        [lax.dynamic_slice_in_dim(key_flat, clamp_start[g], LMAX, 0) for g in range(group_count)]
        + [jnp.zeros((extra, kv_width), jnp.bfloat16)],
        0,
    )
    v_prompt = jnp.concatenate(
        [lax.dynamic_slice_in_dim(value_flat, clamp_start[g], LMAX, 0) for g in range(group_count)]
        + [jnp.zeros((extra, kv_width), jnp.bfloat16)],
        0,
    )
    def windows(values, fill):
        padded = jnp.concatenate([jnp.full((BLOCK,), fill, values.dtype), values]).reshape(
            n_blocks + 1, BLOCK
        )
        return jnp.concatenate([padded[:-1], padded[1:]], 1)

    win_row = windows(row_ids, -1)
    win_req = windows(request_row, -1)
    win_grp = windows(group_row, -1)
    win_prm = windows(prompt_row, 0)
    q_row = row_ids.reshape(n_blocks, BLOCK)[:, :, None]
    q_req = request_row.reshape(n_blocks, BLOCK)[:, :, None]
    q_grp = group_row.reshape(n_blocks, BLOCK)[:, :, None]
    win_vis = (
        (win_row[:, None, :] >= 0)
        & (win_grp[:, None, :] == q_grp)
        & (win_row[:, None, :] <= q_row)
        & ((win_req[:, None, :] == q_req) | (win_prm[:, None, :] == 1))
    )
    p_row = (clamp_start[:, None] + jnp.arange(LMAX, dtype=jnp.int32)[None, :]).reshape(-1)
    p_lo = jnp.repeat(prompt_start, LMAX)
    p_hi = jnp.repeat(prompt_start + prompt_len, LMAX)
    p_grp = jnp.repeat(jnp.arange(group_count, dtype=jnp.int32), LMAX)
    p_row = jnp.concatenate([p_row, jnp.zeros((extra,), jnp.int32)])
    p_lo = jnp.concatenate([p_lo, jnp.ones((extra,), jnp.int32)])
    p_hi = jnp.concatenate([p_hi, jnp.zeros((extra,), jnp.int32)])
    p_grp = jnp.concatenate([p_grp, jnp.full((extra,), -1, jnp.int32)])
    win_first = q_row[:, :1, :] - BLOCK
    prompt_vis = (
        (p_grp[None, None, :] == q_grp)
        & (p_row[None, None, :] >= p_lo[None, None, :])
        & (p_row[None, None, :] < p_hi[None, None, :])
        & (p_row[None, None, :] < win_first)
        & (p_row[None, None, :] <= q_row)
    )
    vis = jnp.concatenate([win_vis, prompt_vis], 2)
    bias = jnp.where(vis, jnp.float32(0.0), jnp.float32(-1e30))
    residual = lax.dynamic_slice_in_dim(tokens, tp_index * piece_width, piece_width, 1)
    return attend_and_reduce(
        query_full,
        cos_pair,
        sin_pair,
        k_pad,
        v_pad,
        k_prompt,
        v_prompt,
        bias,
        output_matrix,
        residual,
        tp_count,
    )


def solution(mesh):
    return jax.shard_map(
        per_device,
        mesh=mesh,
        in_specs=(
            P("req", None),
            P(),
            P(None, "tp"),
            P(None, "tp"),
            P(None, "tp"),
            P("tp", None),
            P("req", "tp", None),
            P("req", None, "tp"),
            P("req", None),
            P("req", None),
            P("req", None),
            P(),
        ),
        out_specs=P("req", "tp"),
        check_vma=False,
    )
```

```python
import jax
import jax.numpy as jnp
import functools
from jax import lax
from jax.experimental import pallas as pl
from jax.experimental.pallas import tpu as pltpu
from jax.sharding import PartitionSpec as P

HEAD_WIDTH = 128
REQ_DEV = 32
LMAX = 40


def apply_rotary(vectors, token_positions):
    head_size = vectors.shape[-1]
    half_dim = head_size // 2
    inverse = 1000000.0 ** (-(jnp.arange(half_dim, dtype=jnp.float32) * 2.0 / head_size))
    angles = token_positions[:, None] * inverse[None, :]
    cosine = jnp.cos(angles)[:, None, :]
    sine_part = jnp.sin(angles)[:, None, :]
    first_half = vectors[..., :half_dim]
    second = vectors[..., half_dim:]
    return jnp.concatenate(
        [first_half * cosine - second * sine_part, second * cosine + first_half * sine_part], -1
    )


def layout(lengths, groups, tok_rows):
    req_slots = lengths.shape[0]
    row_ids = jnp.arange(tok_rows, dtype=jnp.int32)
    row_ends = jnp.cumsum(lengths)
    starts = row_ends - lengths
    request_row = jnp.sum((row_ids[:, None] >= row_ends[None, :]).astype(jnp.int32), 1)
    request_hot = (request_row[:, None] == jnp.arange(req_slots, dtype=jnp.int32)[None, :]).astype(
        jnp.int32
    )
    previous = jnp.concatenate([jnp.full((1,), -1, jnp.int32), groups[:-1]])
    is_prompt = (groups != previous).astype(jnp.int32)
    prompt_len = jnp.sum(
        lengths[None, :]
        * is_prompt[None, :]
        * (groups[None, :] == groups[:, None]).astype(jnp.int32),
        1,
    )
    offset_req = (1 - is_prompt) * prompt_len - starts
    group_row = jnp.sum(request_hot * groups[None, :], 1)
    prompt_row = jnp.sum(request_hot * is_prompt[None, :], 1)
    offset_row = jnp.sum(request_hot * offset_req[None, :], 1)
    token_positions = (row_ids + offset_row).astype(jnp.float32)
    group_ids = jnp.arange(3, dtype=jnp.int32)
    group_hot = (groups[None, :] == group_ids[:, None]).astype(jnp.int32)
    prompt_start = jnp.sum((starts * is_prompt)[None, :] * group_hot, 1)
    prompt_len = jnp.sum((lengths * is_prompt)[None, :] * group_hot, 1)
    rows = (request_row, group_row, prompt_row, prompt_start, prompt_len)
    return (request_hot, starts, rows, token_positions, row_ids)


BLOCK = 128


def attend_kernel(
    q_ref, cs_ref, sn_ref, k_ref, v_ref, kp_ref, vp_ref, bias_ref, wo_ref, res_ref, out_ref,
    send_buf, recv_buf, send_sems, recv_sems, *, tp_count, heads, kv_heads, n_blocks
):
    me = lax.axis_index("tp")
    row_dev = lax.axis_index("req")
    piece = out_ref.shape[1]
    barrier = pltpu.get_barrier_semaphore()
    for k in range(1, tp_count):
        peer = lax.rem(me + k, tp_count)
        pl.semaphore_signal(
            barrier, inc=1, device_id=(row_dev, peer), device_id_type=pl.DeviceIdType.MESH
        )
    pl.semaphore_wait(barrier, tp_count - 1)
    rep = heads // kv_heads

    def copy_of(b, k, source):
        peer = lax.rem(me + k, tp_count)
        col = pl.multiple_of(peer * piece, piece)
        row = pl.multiple_of(b * BLOCK, BLOCK)
        return pltpu.make_async_remote_copy(
            src_ref=send_buf.at[b, :, pl.ds(col, piece)],
            dst_ref=recv_buf.at[source, pl.ds(row, BLOCK)],
            send_sem=send_sems.at[b * tp_count + k],
            recv_sem=recv_sems.at[source * n_blocks + b],
            device_id=(row_dev, peer),
            device_id_type=pl.DeviceIdType.MESH,
        )

    def block_body(b, carry):
        row = pl.multiple_of(b * BLOCK, BLOCK)
        bias = bias_ref[b]
        cs = cs_ref[pl.ds(row, BLOCK), :]
        sn = sn_ref[pl.ds(row, BLOCK), :]
        outs = []
        for h in range(heads):
            g = h // rep
            qf = q_ref[pl.ds(row, BLOCK), pl.ds(h * 128, 128)]
            qh = (qf * cs + pltpu.roll(qf, 64, 1) * sn).astype(jnp.bfloat16)
            kw = k_ref[pl.ds(row, 2 * BLOCK), pl.ds(g * 128, 128)]
            vw = v_ref[pl.ds(row, 2 * BLOCK), pl.ds(g * 128, 128)]
            kp = kp_ref[:, pl.ds(g * 128, 128)]
            vp = vp_ref[:, pl.ds(g * 128, 128)]
            keys = jnp.concatenate([kw, kp], 0)
            vals = jnp.concatenate([vw, vp], 0)
            s = lax.dot_general(
                qh, keys, (((1,), (1,)), ((), ())), preferred_element_type=jnp.float32
            ) / HEAD_WIDTH**0.5
            s = s + bias
            m = jnp.max(s, -1, keepdims=True)
            w = jnp.exp(s - m)
            p = (w / jnp.sum(w, -1, keepdims=True)).astype(jnp.bfloat16)
            outs.append(
                jnp.dot(p, vals, preferred_element_type=jnp.float32).astype(jnp.bfloat16)
            )
        att = jnp.concatenate(outs, 1)
        part = jnp.dot(att, wo_ref[...], preferred_element_type=jnp.float32)
        send_buf[b] = part.astype(jnp.bfloat16)
        for k in range(1, tp_count):
            copy_of(b, k, me).start()
        return carry

    lax.fori_loop(0, n_blocks, block_body, 0)

    def wait_body(b, carry):
        for k in range(1, tp_count):
            copy_of(b, k, me).wait_send()
            source = lax.rem(me + tp_count - k, tp_count)
            copy_of(b, k, source).wait_recv()
        return carry

    lax.fori_loop(0, n_blocks, wait_body, 0)
    own = pl.multiple_of(me * piece, piece)

    def finish_body(b, carry):
        row = pl.multiple_of(b * BLOCK, BLOCK)
        total = res_ref[pl.ds(row, BLOCK), :].astype(jnp.float32)
        total = total + send_buf[b, :, pl.ds(own, piece)].astype(jnp.float32)
        for k in range(1, tp_count):
            source = lax.rem(me + tp_count - k, tp_count)
            total = total + recv_buf[source, pl.ds(row, BLOCK), :].astype(jnp.float32)
        out_ref[pl.ds(row, BLOCK), :] = total.astype(out_ref.dtype)
        return carry

    lax.fori_loop(0, n_blocks, finish_body, 0)


def attend_and_reduce(q, cs, sn, k_pad, v_pad, k_prompt, v_prompt, bias, wo, residual, tp_count):
    rows, q_width = q.shape
    n_blocks = rows // BLOCK
    piece = residual.shape[1]
    width = wo.shape[1]
    kernel = functools.partial(
        attend_kernel,
        tp_count=tp_count,
        heads=q_width // HEAD_WIDTH,
        kv_heads=k_pad.shape[1] // HEAD_WIDTH,
        n_blocks=n_blocks,
    )
    vmem = pltpu.MemorySpace.VMEM
    return pl.pallas_call(
        kernel,
        out_shape=jax.ShapeDtypeStruct((rows, piece), jnp.bfloat16),
        in_specs=[pl.BlockSpec(memory_space=vmem)] * 10,
        out_specs=pl.BlockSpec(memory_space=vmem),
        scratch_shapes=[
            pltpu.VMEM((n_blocks, BLOCK, width), jnp.bfloat16),
            pltpu.VMEM((tp_count, rows, piece), jnp.bfloat16),
            pltpu.SemaphoreType.DMA((n_blocks * tp_count,)),
            pltpu.SemaphoreType.DMA((tp_count * n_blocks,)),
        ],
        compiler_params=pltpu.CompilerParams(
            collective_id=0, has_side_effects=True, vmem_limit_bytes=48 * 1024 * 1024
        ),
    )(q, cs, sn, k_pad, v_pad, k_prompt, v_prompt, bias, wo, residual)


def per_device(
    tokens,
    input_norm_gain,
    query_matrix,
    key_matrix,
    value_matrix,
    output_matrix,
    adapter_down_maps,
    adapter_up_maps,
    request_row_counts,
    prompt_group_per_request,
    adapter_per_request,
    adapter_table_slot,
):
    tp_count = lax.axis_size("tp")
    req_count = lax.axis_size("req")
    tp_index = lax.axis_index("tp")
    tok_rows, width = tokens.shape
    piece_width = width // tp_count
    lengths = request_row_counts[0]
    groups = prompt_group_per_request[0]
    adapters = adapter_per_request[0]
    req_slots = lengths.shape[0]
    request_hot, starts, row_info, token_positions, row_ids = layout(lengths, groups, tok_rows)
    adapters_per_part = adapter_down_maps.shape[0]
    rank_extent = adapter_down_maps.shape[2]
    slots = adapter_table_slot[adapters]
    holder = slots // adapters_per_part
    local_slot = slots % adapters_per_part
    holder_ids = jnp.arange(req_count, dtype=jnp.int32)
    holder_hot = (holder[None, :] == holder_ids[:, None]).astype(jnp.int32)
    wanted = jnp.sum(holder_hot * local_slot[None, :], 1)
    wanted_in = lax.all_to_all(
        wanted.reshape(req_count, 1), "req", split_axis=0, concat_axis=0, tiled=True
    ).reshape(req_count)
    down_sel = jnp.transpose(adapter_down_maps[wanted_in], (0, 2, 1))
    up_sel = adapter_up_maps[wanted_in]
    maps_out = jnp.concatenate([down_sel, up_sel], 1)
    maps_in = lax.all_to_all(maps_out, "req", split_axis=0, concat_axis=0, tiled=True)
    down_in = maps_in[:, :rank_extent, :].reshape(req_count * rank_extent, piece_width)
    up_in = maps_in[:, rank_extent:, :].reshape(req_count * rank_extent, piece_width)
    float_tok = tokens.astype(jnp.float32)
    normalized_input = (
        float_tok
        * lax.rsqrt(jnp.mean(float_tok * float_tok, -1, keepdims=True) + 1e-06)
        * input_norm_gain
    ).astype(jnp.bfloat16)
    normed_slice = lax.dynamic_slice_in_dim(
        normalized_input, tp_index * piece_width, piece_width, 1
    )
    holder_row = jnp.sum(request_hot * holder[None, :], 1)
    pick = (holder_row[:, None] == holder_ids[None, :])[:, :, None]
    wide_rank = jnp.dot(
        normed_slice, down_in.T, preferred_element_type=jnp.float32
    ).reshape(tok_rows, req_count, rank_extent)
    partial_rank = jnp.sum(jnp.where(pick, wide_rank, jnp.float32(0.0)), 1)
    arrived = [
        lax.ppermute(partial_rank, "tp", [(i, (i + k) % tp_count) for i in range(tp_count)])
        for k in range(1, tp_count)
    ]
    for piece in arrived:
        partial_rank = partial_rank + piece
    rank = partial_rank.astype(jnp.bfloat16)
    spread = jnp.where(pick, rank[:, None, :], jnp.zeros((), jnp.bfloat16)).reshape(
        tok_rows, req_count * rank_extent
    )
    query_delta = (
        2.0 * jnp.dot(spread, up_in, preferred_element_type=jnp.float32)
    ).astype(jnp.bfloat16)
    heads_local = query_matrix.shape[1] // HEAD_WIDTH
    kv_local = key_matrix.shape[1] // HEAD_WIDTH
    query_full = jnp.dot(
        normalized_input, query_matrix, preferred_element_type=jnp.float32
    ) + query_delta.astype(jnp.float32)
    half_dim = HEAD_WIDTH // 2
    inverse = 1000000.0 ** (-(jnp.arange(half_dim, dtype=jnp.float32) * 2.0 / HEAD_WIDTH))
    angles = token_positions[:, None] * inverse[None, :]
    cosine = jnp.cos(angles)
    sine = jnp.sin(angles)
    cos_pair = jnp.concatenate([cosine, cosine], 1)
    sin_pair = jnp.concatenate([-sine, sine], 1)
    key_complete = jnp.dot(normalized_input, key_matrix, preferred_element_type=jnp.float32)
    key_head_rows = apply_rotary(
        key_complete.reshape(tok_rows, kv_local, HEAD_WIDTH), token_positions
    ).astype(jnp.bfloat16)
    value_head_rows = (
        jnp.dot(normalized_input, value_matrix, preferred_element_type=jnp.float32)
        .astype(jnp.bfloat16)
        .reshape(tok_rows, kv_local, HEAD_WIDTH)
    )
    request_row, group_row, prompt_row, prompt_start, prompt_len = row_info
    n_blocks = tok_rows // BLOCK
    group_count = prompt_start.shape[0]
    kv_width = kv_local * HEAD_WIDTH
    key_flat = key_head_rows.reshape(tok_rows, kv_width)
    value_flat = value_head_rows.reshape(tok_rows, kv_width)
    front = jnp.zeros((BLOCK, kv_width), jnp.bfloat16)
    k_pad = jnp.concatenate([front, key_flat], 0)
    v_pad = jnp.concatenate([front, value_flat], 0)
    clamp_start = jnp.clip(prompt_start, 0, tok_rows - LMAX)
    extra = BLOCK - group_count * LMAX
    k_prompt = jnp.concatenate(
        [lax.dynamic_slice_in_dim(key_flat, clamp_start[g], LMAX, 0) for g in range(group_count)]
        + [jnp.zeros((extra, kv_width), jnp.bfloat16)],
        0,
    )
    v_prompt = jnp.concatenate(
        [lax.dynamic_slice_in_dim(value_flat, clamp_start[g], LMAX, 0) for g in range(group_count)]
        + [jnp.zeros((extra, kv_width), jnp.bfloat16)],
        0,
    )
    def windows(values, fill):
        padded = jnp.concatenate([jnp.full((BLOCK,), fill, values.dtype), values]).reshape(
            n_blocks + 1, BLOCK
        )
        return jnp.concatenate([padded[:-1], padded[1:]], 1)

    win_row = windows(row_ids, -1)
    win_req = windows(request_row, -1)
    win_grp = windows(group_row, -1)
    win_prm = windows(prompt_row, 0)
    q_row = row_ids.reshape(n_blocks, BLOCK)[:, :, None]
    q_req = request_row.reshape(n_blocks, BLOCK)[:, :, None]
    q_grp = group_row.reshape(n_blocks, BLOCK)[:, :, None]
    win_vis = (
        (win_row[:, None, :] >= 0)
        & (win_grp[:, None, :] == q_grp)
        & (win_row[:, None, :] <= q_row)
        & ((win_req[:, None, :] == q_req) | (win_prm[:, None, :] == 1))
    )
    p_row = (clamp_start[:, None] + jnp.arange(LMAX, dtype=jnp.int32)[None, :]).reshape(-1)
    p_lo = jnp.repeat(prompt_start, LMAX)
    p_hi = jnp.repeat(prompt_start + prompt_len, LMAX)
    p_grp = jnp.repeat(jnp.arange(group_count, dtype=jnp.int32), LMAX)
    p_row = jnp.concatenate([p_row, jnp.zeros((extra,), jnp.int32)])
    p_lo = jnp.concatenate([p_lo, jnp.ones((extra,), jnp.int32)])
    p_hi = jnp.concatenate([p_hi, jnp.zeros((extra,), jnp.int32)])
    p_grp = jnp.concatenate([p_grp, jnp.full((extra,), -1, jnp.int32)])
    win_first = q_row[:, :1, :] - BLOCK
    prompt_vis = (
        (p_grp[None, None, :] == q_grp)
        & (p_row[None, None, :] >= p_lo[None, None, :])
        & (p_row[None, None, :] < p_hi[None, None, :])
        & (p_row[None, None, :] < win_first)
        & (p_row[None, None, :] <= q_row)
    )
    vis = jnp.concatenate([win_vis, prompt_vis], 2)
    bias = jnp.where(vis, jnp.float32(0.0), jnp.float32(-1e30))
    residual = lax.dynamic_slice_in_dim(tokens, tp_index * piece_width, piece_width, 1)
    return attend_and_reduce(
        query_full,
        cos_pair,
        sin_pair,
        k_pad,
        v_pad,
        k_prompt,
        v_prompt,
        bias,
        output_matrix,
        residual,
        tp_count,
    )


def solution(mesh):
    return jax.shard_map(
        per_device,
        mesh=mesh,
        in_specs=(
            P("req", None),
            P(),
            P(None, "tp"),
            P(None, "tp"),
            P(None, "tp"),
            P("tp", None),
            P("req", "tp", None),
            P("req", None, "tp"),
            P("req", None),
            P("req", None),
            P("req", None),
            P(),
        ),
        out_specs=P("req", "tp"),
        check_vma=False,
    )
```

```python
import jax
import jax.numpy as jnp
import functools
from jax import lax
from jax.experimental import pallas as pl
from jax.experimental.pallas import tpu as pltpu
from jax.sharding import PartitionSpec as P

HEAD_WIDTH = 128
REQ_DEV = 32
LMAX = 40


def apply_rotary(vectors, token_positions):
    head_size = vectors.shape[-1]
    half_dim = head_size // 2
    inverse = 1000000.0 ** (-(jnp.arange(half_dim, dtype=jnp.float32) * 2.0 / head_size))
    angles = token_positions[:, None] * inverse[None, :]
    cosine = jnp.cos(angles)[:, None, :]
    sine_part = jnp.sin(angles)[:, None, :]
    first_half = vectors[..., :half_dim]
    second = vectors[..., half_dim:]
    return jnp.concatenate(
        [first_half * cosine - second * sine_part, second * cosine + first_half * sine_part], -1
    )


def layout(lengths, groups, tok_rows):
    req_slots = lengths.shape[0]
    row_ids = jnp.arange(tok_rows, dtype=jnp.int32)
    row_ends = jnp.cumsum(lengths)
    starts = row_ends - lengths
    request_row = jnp.sum((row_ids[:, None] >= row_ends[None, :]).astype(jnp.int32), 1)
    request_hot = (request_row[:, None] == jnp.arange(req_slots, dtype=jnp.int32)[None, :]).astype(
        jnp.int32
    )
    previous = jnp.concatenate([jnp.full((1,), -1, jnp.int32), groups[:-1]])
    is_prompt = (groups != previous).astype(jnp.int32)
    prompt_len = jnp.sum(
        lengths[None, :]
        * is_prompt[None, :]
        * (groups[None, :] == groups[:, None]).astype(jnp.int32),
        1,
    )
    offset_req = (1 - is_prompt) * prompt_len - starts
    group_row = jnp.sum(request_hot * groups[None, :], 1)
    prompt_row = jnp.sum(request_hot * is_prompt[None, :], 1)
    offset_row = jnp.sum(request_hot * offset_req[None, :], 1)
    token_positions = (row_ids + offset_row).astype(jnp.float32)
    group_ids = jnp.arange(3, dtype=jnp.int32)
    group_hot = (groups[None, :] == group_ids[:, None]).astype(jnp.int32)
    prompt_start = jnp.sum((starts * is_prompt)[None, :] * group_hot, 1)
    prompt_len = jnp.sum((lengths * is_prompt)[None, :] * group_hot, 1)
    rows = (request_row, group_row, prompt_row, prompt_start, prompt_len)
    return (request_hot, starts, rows, token_positions, row_ids)


BLOCK = 128


def attend_kernel(
    q_ref, cs_ref, sn_ref, k_ref, v_ref, kp_ref, vp_ref, bias_ref, wo_ref, res_ref, out_ref,
    send_buf, relay_in, sum_buf, recv_buf, send_sems, recv_sems, *, tp_count, heads, kv_heads,
    n_blocks
):
    me = lax.axis_index("tp")
    row_dev = lax.axis_index("req")
    piece = out_ref.shape[1]
    half = piece // 2
    up = lax.rem(me + 1, tp_count)
    down = lax.rem(me + tp_count - 1, tp_count)
    across = lax.rem(me + 2, tp_count)
    barrier = pltpu.get_barrier_semaphore()
    for peer in (up, down):
        pl.semaphore_signal(
            barrier, inc=1, device_id=(row_dev, peer), device_id_type=pl.DeviceIdType.MESH
        )
    pl.semaphore_wait(barrier, 2)
    rep = heads // kv_heads

    def raw_copy(b, side):
        col = pl.multiple_of(across * piece + side * half, half)
        return pltpu.make_async_remote_copy(
            src_ref=send_buf.at[b, :, pl.ds(col, half)],
            dst_ref=relay_in.at[b, side],
            send_sem=send_sems.at[b * 4 + side],
            recv_sem=recv_sems.at[b * 4 + side],
            device_id=(row_dev, up if side == 0 else down),
            device_id_type=pl.DeviceIdType.MESH,
        )

    def sum_copy(b, side):
        row = pl.multiple_of(b * BLOCK, BLOCK)
        return pltpu.make_async_remote_copy(
            src_ref=sum_buf.at[b, side],
            dst_ref=recv_buf.at[side, pl.ds(row, BLOCK)],
            send_sem=send_sems.at[b * 4 + 2 + side],
            recv_sem=recv_sems.at[b * 4 + 2 + side],
            device_id=(row_dev, up if side == 0 else down),
            device_id_type=pl.DeviceIdType.MESH,
        )

    def forward(b):
        raw_copy(b, 0).wait_recv()
        raw_copy(b, 1).wait_recv()
        col_up = pl.multiple_of(up * piece, piece)
        col_down = pl.multiple_of(down * piece, piece)
        to_up = send_buf[b, :, pl.ds(col_up, piece)].astype(jnp.float32)
        to_down = send_buf[b, :, pl.ds(col_down, piece)].astype(jnp.float32)
        from_down = relay_in[b, 0].astype(jnp.float32)
        from_up = relay_in[b, 1].astype(jnp.float32)
        sum_buf[b, 0] = jnp.concatenate(
            [to_up[:, :half] + from_down, to_up[:, half:]], 1
        ).astype(sum_buf.dtype)
        sum_buf[b, 1] = jnp.concatenate(
            [to_down[:, :half], to_down[:, half:] + from_up], 1
        ).astype(sum_buf.dtype)
        sum_copy(b, 0).start()
        sum_copy(b, 1).start()

    def block_body(b, carry):
        row = pl.multiple_of(b * BLOCK, BLOCK)
        bias = bias_ref[b]
        cs = cs_ref[pl.ds(row, BLOCK), :]
        sn = sn_ref[pl.ds(row, BLOCK), :]
        outs = []
        for h in range(heads):
            g = h // rep
            qf = q_ref[pl.ds(row, BLOCK), pl.ds(h * 128, 128)]
            qh = (qf * cs + pltpu.roll(qf, 64, 1) * sn).astype(jnp.bfloat16)
            kw = k_ref[pl.ds(row, 2 * BLOCK), pl.ds(g * 128, 128)]
            vw = v_ref[pl.ds(row, 2 * BLOCK), pl.ds(g * 128, 128)]
            kp = kp_ref[:, pl.ds(g * 128, 128)]
            vp = vp_ref[:, pl.ds(g * 128, 128)]
            keys = jnp.concatenate([kw, kp], 0)
            vals = jnp.concatenate([vw, vp], 0)
            s = lax.dot_general(
                qh, keys, (((1,), (1,)), ((), ())), preferred_element_type=jnp.float32
            ) / HEAD_WIDTH**0.5
            s = s + bias
            m = jnp.max(s, -1, keepdims=True)
            w = jnp.exp(s - m)
            p = (w / jnp.sum(w, -1, keepdims=True)).astype(jnp.bfloat16)
            outs.append(
                jnp.dot(p, vals, preferred_element_type=jnp.float32).astype(jnp.bfloat16)
            )
        att = jnp.concatenate(outs, 1)
        part = jnp.dot(att, wo_ref[...], preferred_element_type=jnp.float32)
        send_buf[b] = part.astype(jnp.bfloat16)
        raw_copy(b, 0).start()
        raw_copy(b, 1).start()

        @pl.when(b > 0)
        def _():
            forward(b - 1)

        return carry

    lax.fori_loop(0, n_blocks, block_body, 0)
    forward(n_blocks - 1)

    def wait_body(b, carry):
        for side in (0, 1):
            raw_copy(b, side).wait_send()
            sum_copy(b, side).wait_send()
            sum_copy(b, side).wait_recv()
        return carry

    lax.fori_loop(0, n_blocks, wait_body, 0)
    own = pl.multiple_of(me * piece, piece)

    def finish_body(b, carry):
        row = pl.multiple_of(b * BLOCK, BLOCK)
        total = res_ref[pl.ds(row, BLOCK), :].astype(jnp.float32)
        total = total + send_buf[b, :, pl.ds(own, piece)].astype(jnp.float32)
        for side in (0, 1):
            total = total + recv_buf[side, pl.ds(row, BLOCK), :].astype(jnp.float32)
        out_ref[pl.ds(row, BLOCK), :] = total.astype(out_ref.dtype)
        return carry

    lax.fori_loop(0, n_blocks, finish_body, 0)


def attend_and_reduce(q, cs, sn, k_pad, v_pad, k_prompt, v_prompt, bias, wo, residual, tp_count):
    rows, q_width = q.shape
    n_blocks = rows // BLOCK
    piece = residual.shape[1]
    width = wo.shape[1]
    kernel = functools.partial(
        attend_kernel,
        tp_count=tp_count,
        heads=q_width // HEAD_WIDTH,
        kv_heads=k_pad.shape[1] // HEAD_WIDTH,
        n_blocks=n_blocks,
    )
    vmem = pltpu.MemorySpace.VMEM
    return pl.pallas_call(
        kernel,
        out_shape=jax.ShapeDtypeStruct((rows, piece), jnp.bfloat16),
        in_specs=[pl.BlockSpec(memory_space=vmem)] * 10,
        out_specs=pl.BlockSpec(memory_space=vmem),
        scratch_shapes=[
            pltpu.VMEM((n_blocks, BLOCK, width), jnp.bfloat16),
            pltpu.VMEM((n_blocks, 2, BLOCK, piece // 2), jnp.bfloat16),
            pltpu.VMEM((n_blocks, 2, BLOCK, piece), jnp.bfloat16),
            pltpu.VMEM((2, rows, piece), jnp.bfloat16),
            pltpu.SemaphoreType.DMA((n_blocks * 4,)),
            pltpu.SemaphoreType.DMA((n_blocks * 4,)),
        ],
        compiler_params=pltpu.CompilerParams(
            collective_id=0, has_side_effects=True, vmem_limit_bytes=48 * 1024 * 1024
        ),
    )(q, cs, sn, k_pad, v_pad, k_prompt, v_prompt, bias, wo, residual)


def per_device(
    tokens,
    input_norm_gain,
    query_matrix,
    key_matrix,
    value_matrix,
    output_matrix,
    adapter_down_maps,
    adapter_up_maps,
    request_row_counts,
    prompt_group_per_request,
    adapter_per_request,
    adapter_table_slot,
):
    tp_count = lax.axis_size("tp")
    req_count = lax.axis_size("req")
    tp_index = lax.axis_index("tp")
    tok_rows, width = tokens.shape
    piece_width = width // tp_count
    lengths = request_row_counts[0]
    groups = prompt_group_per_request[0]
    adapters = adapter_per_request[0]
    req_slots = lengths.shape[0]
    request_hot, starts, row_info, token_positions, row_ids = layout(lengths, groups, tok_rows)
    adapters_per_part = adapter_down_maps.shape[0]
    rank_extent = adapter_down_maps.shape[2]
    slots = adapter_table_slot[adapters]
    holder = slots // adapters_per_part
    local_slot = slots % adapters_per_part
    holder_ids = jnp.arange(req_count, dtype=jnp.int32)
    holder_hot = (holder[None, :] == holder_ids[:, None]).astype(jnp.int32)
    wanted = jnp.sum(holder_hot * local_slot[None, :], 1)
    wanted_in = lax.all_to_all(
        wanted.reshape(req_count, 1), "req", split_axis=0, concat_axis=0, tiled=True
    ).reshape(req_count)
    down_sel = jnp.transpose(adapter_down_maps[wanted_in], (0, 2, 1))
    up_sel = adapter_up_maps[wanted_in]
    maps_out = jnp.concatenate([down_sel, up_sel], 1)
    maps_in = lax.all_to_all(maps_out, "req", split_axis=0, concat_axis=0, tiled=True)
    down_in = maps_in[:, :rank_extent, :].reshape(req_count * rank_extent, piece_width)
    up_in = maps_in[:, rank_extent:, :].reshape(req_count * rank_extent, piece_width)
    float_tok = tokens.astype(jnp.float32)
    normalized_input = (
        float_tok
        * lax.rsqrt(jnp.mean(float_tok * float_tok, -1, keepdims=True) + 1e-06)
        * input_norm_gain
    ).astype(jnp.bfloat16)
    normed_slice = lax.dynamic_slice_in_dim(
        normalized_input, tp_index * piece_width, piece_width, 1
    )
    holder_row = jnp.sum(request_hot * holder[None, :], 1)
    pick = (holder_row[:, None] == holder_ids[None, :])[:, :, None]
    wide_rank = jnp.dot(
        normed_slice, down_in.T, preferred_element_type=jnp.float32
    ).reshape(tok_rows, req_count, rank_extent)
    partial_rank = jnp.sum(jnp.where(pick, wide_rank, jnp.float32(0.0)), 1)
    arrived = [
        lax.ppermute(partial_rank, "tp", [(i, (i + k) % tp_count) for i in range(tp_count)])
        for k in range(1, tp_count)
    ]
    for piece in arrived:
        partial_rank = partial_rank + piece
    rank = partial_rank.astype(jnp.bfloat16)
    spread = jnp.where(pick, rank[:, None, :], jnp.zeros((), jnp.bfloat16)).reshape(
        tok_rows, req_count * rank_extent
    )
    query_delta = (
        2.0 * jnp.dot(spread, up_in, preferred_element_type=jnp.float32)
    ).astype(jnp.bfloat16)
    heads_local = query_matrix.shape[1] // HEAD_WIDTH
    kv_local = key_matrix.shape[1] // HEAD_WIDTH
    query_full = jnp.dot(
        normalized_input, query_matrix, preferred_element_type=jnp.float32
    ) + query_delta.astype(jnp.float32)
    half_dim = HEAD_WIDTH // 2
    inverse = 1000000.0 ** (-(jnp.arange(half_dim, dtype=jnp.float32) * 2.0 / HEAD_WIDTH))
    angles = token_positions[:, None] * inverse[None, :]
    cosine = jnp.cos(angles)
    sine = jnp.sin(angles)
    cos_pair = jnp.concatenate([cosine, cosine], 1)
    sin_pair = jnp.concatenate([-sine, sine], 1)
    key_complete = jnp.dot(normalized_input, key_matrix, preferred_element_type=jnp.float32)
    key_head_rows = apply_rotary(
        key_complete.reshape(tok_rows, kv_local, HEAD_WIDTH), token_positions
    ).astype(jnp.bfloat16)
    value_head_rows = (
        jnp.dot(normalized_input, value_matrix, preferred_element_type=jnp.float32)
        .astype(jnp.bfloat16)
        .reshape(tok_rows, kv_local, HEAD_WIDTH)
    )
    request_row, group_row, prompt_row, prompt_start, prompt_len = row_info
    n_blocks = tok_rows // BLOCK
    group_count = prompt_start.shape[0]
    kv_width = kv_local * HEAD_WIDTH
    key_flat = key_head_rows.reshape(tok_rows, kv_width)
    value_flat = value_head_rows.reshape(tok_rows, kv_width)
    front = jnp.zeros((BLOCK, kv_width), jnp.bfloat16)
    k_pad = jnp.concatenate([front, key_flat], 0)
    v_pad = jnp.concatenate([front, value_flat], 0)
    clamp_start = jnp.clip(prompt_start, 0, tok_rows - LMAX)
    extra = BLOCK - group_count * LMAX
    k_prompt = jnp.concatenate(
        [lax.dynamic_slice_in_dim(key_flat, clamp_start[g], LMAX, 0) for g in range(group_count)]
        + [jnp.zeros((extra, kv_width), jnp.bfloat16)],
        0,
    )
    v_prompt = jnp.concatenate(
        [lax.dynamic_slice_in_dim(value_flat, clamp_start[g], LMAX, 0) for g in range(group_count)]
        + [jnp.zeros((extra, kv_width), jnp.bfloat16)],
        0,
    )
    def windows(values, fill):
        padded = jnp.concatenate([jnp.full((BLOCK,), fill, values.dtype), values]).reshape(
            n_blocks + 1, BLOCK
        )
        return jnp.concatenate([padded[:-1], padded[1:]], 1)

    win_row = windows(row_ids, -1)
    win_req = windows(request_row, -1)
    win_grp = windows(group_row, -1)
    win_prm = windows(prompt_row, 0)
    q_row = row_ids.reshape(n_blocks, BLOCK)[:, :, None]
    q_req = request_row.reshape(n_blocks, BLOCK)[:, :, None]
    q_grp = group_row.reshape(n_blocks, BLOCK)[:, :, None]
    win_vis = (
        (win_row[:, None, :] >= 0)
        & (win_grp[:, None, :] == q_grp)
        & (win_row[:, None, :] <= q_row)
        & ((win_req[:, None, :] == q_req) | (win_prm[:, None, :] == 1))
    )
    p_row = (clamp_start[:, None] + jnp.arange(LMAX, dtype=jnp.int32)[None, :]).reshape(-1)
    p_lo = jnp.repeat(prompt_start, LMAX)
    p_hi = jnp.repeat(prompt_start + prompt_len, LMAX)
    p_grp = jnp.repeat(jnp.arange(group_count, dtype=jnp.int32), LMAX)
    p_row = jnp.concatenate([p_row, jnp.zeros((extra,), jnp.int32)])
    p_lo = jnp.concatenate([p_lo, jnp.ones((extra,), jnp.int32)])
    p_hi = jnp.concatenate([p_hi, jnp.zeros((extra,), jnp.int32)])
    p_grp = jnp.concatenate([p_grp, jnp.full((extra,), -1, jnp.int32)])
    win_first = q_row[:, :1, :] - BLOCK
    prompt_vis = (
        (p_grp[None, None, :] == q_grp)
        & (p_row[None, None, :] >= p_lo[None, None, :])
        & (p_row[None, None, :] < p_hi[None, None, :])
        & (p_row[None, None, :] < win_first)
        & (p_row[None, None, :] <= q_row)
    )
    vis = jnp.concatenate([win_vis, prompt_vis], 2)
    bias = jnp.where(vis, jnp.float32(0.0), jnp.float32(-1e30))
    residual = lax.dynamic_slice_in_dim(tokens, tp_index * piece_width, piece_width, 1)
    return attend_and_reduce(
        query_full,
        cos_pair,
        sin_pair,
        k_pad,
        v_pad,
        k_prompt,
        v_prompt,
        bias,
        output_matrix,
        residual,
        tp_count,
    )


def solution(mesh):
    return jax.shard_map(
        per_device,
        mesh=mesh,
        in_specs=(
            P("req", None),
            P(),
            P(None, "tp"),
            P(None, "tp"),
            P(None, "tp"),
            P("tp", None),
            P("req", "tp", None),
            P("req", None, "tp"),
            P("req", None),
            P("req", None),
            P("req", None),
            P(),
        ),
        out_specs=P("req", "tp"),
        check_vma=False,
    )
```

```python
import jax
import jax.numpy as jnp
import functools
from jax import lax
from jax.experimental import pallas as pl
from jax.experimental.pallas import tpu as pltpu
from jax.sharding import PartitionSpec as P

HEAD_WIDTH = 128
REQ_DEV = 32
LMAX = 40


def apply_rotary(vectors, token_positions):
    head_size = vectors.shape[-1]
    half_dim = head_size // 2
    inverse = 1000000.0 ** (-(jnp.arange(half_dim, dtype=jnp.float32) * 2.0 / head_size))
    angles = token_positions[:, None] * inverse[None, :]
    cosine = jnp.cos(angles)[:, None, :]
    sine_part = jnp.sin(angles)[:, None, :]
    first_half = vectors[..., :half_dim]
    second = vectors[..., half_dim:]
    return jnp.concatenate(
        [first_half * cosine - second * sine_part, second * cosine + first_half * sine_part], -1
    )


def layout(lengths, groups, tok_rows):
    req_slots = lengths.shape[0]
    row_ids = jnp.arange(tok_rows, dtype=jnp.int32)
    row_ends = jnp.cumsum(lengths)
    starts = row_ends - lengths
    request_row = jnp.sum((row_ids[:, None] >= row_ends[None, :]).astype(jnp.int32), 1)
    request_hot = (request_row[:, None] == jnp.arange(req_slots, dtype=jnp.int32)[None, :]).astype(
        jnp.int32
    )
    previous = jnp.concatenate([jnp.full((1,), -1, jnp.int32), groups[:-1]])
    is_prompt = (groups != previous).astype(jnp.int32)
    prompt_len = jnp.sum(
        lengths[None, :]
        * is_prompt[None, :]
        * (groups[None, :] == groups[:, None]).astype(jnp.int32),
        1,
    )
    offset_req = (1 - is_prompt) * prompt_len - starts
    group_row = jnp.sum(request_hot * groups[None, :], 1)
    prompt_row = jnp.sum(request_hot * is_prompt[None, :], 1)
    offset_row = jnp.sum(request_hot * offset_req[None, :], 1)
    token_positions = (row_ids + offset_row).astype(jnp.float32)
    group_ids = jnp.arange(3, dtype=jnp.int32)
    group_hot = (groups[None, :] == group_ids[:, None]).astype(jnp.int32)
    prompt_start = jnp.sum((starts * is_prompt)[None, :] * group_hot, 1)
    prompt_len = jnp.sum((lengths * is_prompt)[None, :] * group_hot, 1)
    rows = (request_row, group_row, prompt_row, prompt_start, prompt_len)
    return (request_hot, starts, rows, token_positions, row_ids)


BLOCK = 128


def attend_kernel(
    q_ref, cs_ref, sn_ref, k_ref, v_ref, kp_ref, vp_ref, bias_ref, wo_ref, res_ref, out_ref,
    send_buf, relay_in, sum_buf, recv_buf, send_sems, recv_sems, *, tp_count, heads, kv_heads,
    n_blocks
):
    me = lax.axis_index("tp")
    row_dev = lax.axis_index("req")
    piece = out_ref.shape[1]
    half = piece // 2
    up = lax.rem(me + 1, tp_count)
    down = lax.rem(me + tp_count - 1, tp_count)
    across = lax.rem(me + 2, tp_count)
    barrier = pltpu.get_barrier_semaphore()
    for peer in (up, down):
        pl.semaphore_signal(
            barrier, inc=1, device_id=(row_dev, peer), device_id_type=pl.DeviceIdType.MESH
        )
    pl.semaphore_wait(barrier, 2)
    rep = heads // kv_heads

    def raw_copy(b, side):
        col = pl.multiple_of(across * piece + side * half, half)
        return pltpu.make_async_remote_copy(
            src_ref=send_buf.at[b, :, pl.ds(col, half)],
            dst_ref=relay_in.at[b, side],
            send_sem=send_sems.at[b * 4 + side],
            recv_sem=recv_sems.at[b * 4 + side],
            device_id=(row_dev, up if side == 0 else down),
            device_id_type=pl.DeviceIdType.MESH,
        )

    def sum_copy(b, side):
        row = pl.multiple_of(b * BLOCK, BLOCK)
        return pltpu.make_async_remote_copy(
            src_ref=sum_buf.at[b, side],
            dst_ref=recv_buf.at[side, pl.ds(row, BLOCK)],
            send_sem=send_sems.at[b * 4 + 2 + side],
            recv_sem=recv_sems.at[b * 4 + 2 + side],
            device_id=(row_dev, up if side == 0 else down),
            device_id_type=pl.DeviceIdType.MESH,
        )

    def forward(b):
        raw_copy(b, 0).wait_recv()
        raw_copy(b, 1).wait_recv()
        col_up = pl.multiple_of(up * piece, piece)
        col_down = pl.multiple_of(down * piece, piece)
        to_up = send_buf[b, :, pl.ds(col_up, piece)].astype(jnp.float32)
        to_down = send_buf[b, :, pl.ds(col_down, piece)].astype(jnp.float32)
        from_down = relay_in[b, 0].astype(jnp.float32)
        from_up = relay_in[b, 1].astype(jnp.float32)
        sum_buf[b, 0] = jnp.concatenate(
            [to_up[:, :half] + from_down, to_up[:, half:]], 1
        ).astype(sum_buf.dtype)
        sum_buf[b, 1] = jnp.concatenate(
            [to_down[:, :half], to_down[:, half:] + from_up], 1
        ).astype(sum_buf.dtype)
        sum_copy(b, 0).start()
        sum_copy(b, 1).start()

    def block_body(b, carry):
        row = pl.multiple_of(b * BLOCK, BLOCK)
        bias = bias_ref[b]
        cs = cs_ref[pl.ds(row, BLOCK), :]
        sn = sn_ref[pl.ds(row, BLOCK), :]
        outs = []
        for h in range(heads):
            g = h // rep
            qf = q_ref[pl.ds(row, BLOCK), pl.ds(h * 128, 128)]
            qh = (qf * cs + pltpu.roll(qf, 64, 1) * sn).astype(jnp.bfloat16)
            kw = k_ref[pl.ds(row, 2 * BLOCK), pl.ds(g * 128, 128)]
            vw = v_ref[pl.ds(row, 2 * BLOCK), pl.ds(g * 128, 128)]
            kp = kp_ref[:, pl.ds(g * 128, 128)]
            vp = vp_ref[:, pl.ds(g * 128, 128)]
            keys = jnp.concatenate([kw, kp], 0)
            vals = jnp.concatenate([vw, vp], 0)
            s = lax.dot_general(
                qh, keys, (((1,), (1,)), ((), ())), preferred_element_type=jnp.float32
            ) / HEAD_WIDTH**0.5
            s = s + bias
            m = jnp.max(s, -1, keepdims=True)
            w = jnp.exp(s - m)
            p = (w / jnp.sum(w, -1, keepdims=True)).astype(jnp.bfloat16)
            outs.append(
                jnp.dot(p, vals, preferred_element_type=jnp.float32).astype(jnp.bfloat16)
            )
        att = jnp.concatenate(outs, 1)
        part = jnp.dot(att, wo_ref[...], preferred_element_type=jnp.float32)
        send_buf[b] = part.astype(jnp.bfloat16)
        raw_copy(b, 0).start()
        raw_copy(b, 1).start()

        @pl.when(b > 0)
        def _():
            forward(b - 1)

        return carry

    lax.fori_loop(0, n_blocks, block_body, 0)
    forward(n_blocks - 1)

    def wait_body(b, carry):
        for side in (0, 1):
            raw_copy(b, side).wait_send()
            sum_copy(b, side).wait_send()
            sum_copy(b, side).wait_recv()
        return carry

    lax.fori_loop(0, n_blocks, wait_body, 0)
    own = pl.multiple_of(me * piece, piece)

    def finish_body(b, carry):
        row = pl.multiple_of(b * BLOCK, BLOCK)
        total = res_ref[pl.ds(row, BLOCK), :].astype(jnp.float32)
        total = total + send_buf[b, :, pl.ds(own, piece)].astype(jnp.float32)
        for side in (0, 1):
            total = total + recv_buf[side, pl.ds(row, BLOCK), :].astype(jnp.float32)
        out_ref[pl.ds(row, BLOCK), :] = total.astype(out_ref.dtype)
        return carry

    lax.fori_loop(0, n_blocks, finish_body, 0)


def attend_and_reduce(q, cs, sn, k_pad, v_pad, k_prompt, v_prompt, bias, wo, residual, tp_count):
    rows, q_width = q.shape
    n_blocks = rows // BLOCK
    piece = residual.shape[1]
    width = wo.shape[1]
    kernel = functools.partial(
        attend_kernel,
        tp_count=tp_count,
        heads=q_width // HEAD_WIDTH,
        kv_heads=k_pad.shape[1] // HEAD_WIDTH,
        n_blocks=n_blocks,
    )
    vmem = pltpu.MemorySpace.VMEM
    return pl.pallas_call(
        kernel,
        out_shape=jax.ShapeDtypeStruct((rows, piece), jnp.bfloat16),
        in_specs=[pl.BlockSpec(memory_space=vmem)] * 10,
        out_specs=pl.BlockSpec(memory_space=vmem),
        scratch_shapes=[
            pltpu.VMEM((n_blocks, BLOCK, width), jnp.bfloat16),
            pltpu.VMEM((n_blocks, 2, BLOCK, piece // 2), jnp.bfloat16),
            pltpu.VMEM((n_blocks, 2, BLOCK, piece), jnp.bfloat16),
            pltpu.VMEM((2, rows, piece), jnp.bfloat16),
            pltpu.SemaphoreType.DMA((n_blocks * 4,)),
            pltpu.SemaphoreType.DMA((n_blocks * 4,)),
        ],
        compiler_params=pltpu.CompilerParams(
            collective_id=0, has_side_effects=True, vmem_limit_bytes=48 * 1024 * 1024
        ),
    )(q, cs, sn, k_pad, v_pad, k_prompt, v_prompt, bias, wo, residual)


def per_device(
    tokens,
    input_norm_gain,
    query_matrix,
    key_matrix,
    value_matrix,
    output_matrix,
    adapter_down_maps,
    adapter_up_maps,
    request_row_counts,
    prompt_group_per_request,
    adapter_per_request,
    adapter_table_slot,
):
    tp_count = lax.axis_size("tp")
    req_count = lax.axis_size("req")
    tp_index = lax.axis_index("tp")
    tok_rows, width = tokens.shape
    piece_width = width // tp_count
    lengths = request_row_counts[0]
    groups = prompt_group_per_request[0]
    adapters = adapter_per_request[0]
    req_slots = lengths.shape[0]
    request_hot, starts, row_info, token_positions, row_ids = layout(lengths, groups, tok_rows)
    adapters_per_part = adapter_down_maps.shape[0]
    rank_extent = adapter_down_maps.shape[2]
    slots = adapter_table_slot[adapters]
    holder = slots // adapters_per_part
    local_slot = slots % adapters_per_part
    holder_ids = jnp.arange(req_count, dtype=jnp.int32)
    holder_hot = (holder[None, :] == holder_ids[:, None]).astype(jnp.int32)
    wanted = jnp.sum(holder_hot * local_slot[None, :], 1)
    wanted_in = lax.all_to_all(
        wanted.reshape(req_count, 1), "req", split_axis=0, concat_axis=0, tiled=True
    ).reshape(req_count)
    table = jnp.concatenate([jnp.transpose(adapter_down_maps, (0, 2, 1)), adapter_up_maps], 1)
    float_tok = tokens.astype(jnp.float32)
    normalized_input = (
        float_tok
        * lax.rsqrt(jnp.mean(float_tok * float_tok, -1, keepdims=True) + 1e-06)
        * input_norm_gain
    ).astype(jnp.bfloat16)
    maps_out = table[wanted_in]
    normalized_input, maps_out = lax.optimization_barrier((normalized_input, maps_out))
    maps_in = lax.all_to_all(maps_out, "req", split_axis=0, concat_axis=0, tiled=True)
    down_in = maps_in[:, :rank_extent, :].reshape(req_count * rank_extent, piece_width)
    up_in = maps_in[:, rank_extent:, :].reshape(req_count * rank_extent, piece_width)
    normed_slice = lax.dynamic_slice_in_dim(
        normalized_input, tp_index * piece_width, piece_width, 1
    )
    holder_row = jnp.sum(request_hot * holder[None, :], 1)
    pick = (holder_row[:, None] == holder_ids[None, :])[:, :, None]
    wide_rank = jnp.dot(
        normed_slice, down_in.T, preferred_element_type=jnp.float32
    ).reshape(tok_rows, req_count, rank_extent)
    partial_rank = jnp.sum(jnp.where(pick, wide_rank, jnp.float32(0.0)), 1)
    arrived = [
        lax.ppermute(partial_rank, "tp", [(i, (i + k) % tp_count) for i in range(tp_count)])
        for k in range(1, tp_count)
    ]
    for piece in arrived:
        partial_rank = partial_rank + piece
    rank = partial_rank.astype(jnp.bfloat16)
    spread = jnp.where(pick, rank[:, None, :], jnp.zeros((), jnp.bfloat16)).reshape(
        tok_rows, req_count * rank_extent
    )
    query_delta = (
        2.0 * jnp.dot(spread, up_in, preferred_element_type=jnp.float32)
    ).astype(jnp.bfloat16)
    heads_local = query_matrix.shape[1] // HEAD_WIDTH
    kv_local = key_matrix.shape[1] // HEAD_WIDTH
    query_full = jnp.dot(
        normalized_input, query_matrix, preferred_element_type=jnp.float32
    ) + query_delta.astype(jnp.float32)
    half_dim = HEAD_WIDTH // 2
    inverse = 1000000.0 ** (-(jnp.arange(half_dim, dtype=jnp.float32) * 2.0 / HEAD_WIDTH))
    angles = token_positions[:, None] * inverse[None, :]
    cosine = jnp.cos(angles)
    sine = jnp.sin(angles)
    cos_pair = jnp.concatenate([cosine, cosine], 1)
    sin_pair = jnp.concatenate([-sine, sine], 1)
    key_complete = jnp.dot(normalized_input, key_matrix, preferred_element_type=jnp.float32)
    key_head_rows = apply_rotary(
        key_complete.reshape(tok_rows, kv_local, HEAD_WIDTH), token_positions
    ).astype(jnp.bfloat16)
    value_head_rows = (
        jnp.dot(normalized_input, value_matrix, preferred_element_type=jnp.float32)
        .astype(jnp.bfloat16)
        .reshape(tok_rows, kv_local, HEAD_WIDTH)
    )
    request_row, group_row, prompt_row, prompt_start, prompt_len = row_info
    n_blocks = tok_rows // BLOCK
    group_count = prompt_start.shape[0]
    kv_width = kv_local * HEAD_WIDTH
    key_flat = key_head_rows.reshape(tok_rows, kv_width)
    value_flat = value_head_rows.reshape(tok_rows, kv_width)
    front = jnp.zeros((BLOCK, kv_width), jnp.bfloat16)
    k_pad = jnp.concatenate([front, key_flat], 0)
    v_pad = jnp.concatenate([front, value_flat], 0)
    clamp_start = jnp.clip(prompt_start, 0, tok_rows - LMAX)
    extra = BLOCK - group_count * LMAX
    k_prompt = jnp.concatenate(
        [lax.dynamic_slice_in_dim(key_flat, clamp_start[g], LMAX, 0) for g in range(group_count)]
        + [jnp.zeros((extra, kv_width), jnp.bfloat16)],
        0,
    )
    v_prompt = jnp.concatenate(
        [lax.dynamic_slice_in_dim(value_flat, clamp_start[g], LMAX, 0) for g in range(group_count)]
        + [jnp.zeros((extra, kv_width), jnp.bfloat16)],
        0,
    )
    def windows(values, fill):
        padded = jnp.concatenate([jnp.full((BLOCK,), fill, values.dtype), values]).reshape(
            n_blocks + 1, BLOCK
        )
        return jnp.concatenate([padded[:-1], padded[1:]], 1)

    win_row = windows(row_ids, -1)
    win_req = windows(request_row, -1)
    win_grp = windows(group_row, -1)
    win_prm = windows(prompt_row, 0)
    q_row = row_ids.reshape(n_blocks, BLOCK)[:, :, None]
    q_req = request_row.reshape(n_blocks, BLOCK)[:, :, None]
    q_grp = group_row.reshape(n_blocks, BLOCK)[:, :, None]
    win_vis = (
        (win_row[:, None, :] >= 0)
        & (win_grp[:, None, :] == q_grp)
        & (win_row[:, None, :] <= q_row)
        & ((win_req[:, None, :] == q_req) | (win_prm[:, None, :] == 1))
    )
    p_row = (clamp_start[:, None] + jnp.arange(LMAX, dtype=jnp.int32)[None, :]).reshape(-1)
    p_lo = jnp.repeat(prompt_start, LMAX)
    p_hi = jnp.repeat(prompt_start + prompt_len, LMAX)
    p_grp = jnp.repeat(jnp.arange(group_count, dtype=jnp.int32), LMAX)
    p_row = jnp.concatenate([p_row, jnp.zeros((extra,), jnp.int32)])
    p_lo = jnp.concatenate([p_lo, jnp.ones((extra,), jnp.int32)])
    p_hi = jnp.concatenate([p_hi, jnp.zeros((extra,), jnp.int32)])
    p_grp = jnp.concatenate([p_grp, jnp.full((extra,), -1, jnp.int32)])
    win_first = q_row[:, :1, :] - BLOCK
    prompt_vis = (
        (p_grp[None, None, :] == q_grp)
        & (p_row[None, None, :] >= p_lo[None, None, :])
        & (p_row[None, None, :] < p_hi[None, None, :])
        & (p_row[None, None, :] < win_first)
        & (p_row[None, None, :] <= q_row)
    )
    vis = jnp.concatenate([win_vis, prompt_vis], 2)
    bias = jnp.where(vis, jnp.float32(0.0), jnp.float32(-1e30))
    residual = lax.dynamic_slice_in_dim(tokens, tp_index * piece_width, piece_width, 1)
    return attend_and_reduce(
        query_full,
        cos_pair,
        sin_pair,
        k_pad,
        v_pad,
        k_prompt,
        v_prompt,
        bias,
        output_matrix,
        residual,
        tp_count,
    )


def solution(mesh):
    return jax.shard_map(
        per_device,
        mesh=mesh,
        in_specs=(
            P("req", None),
            P(),
            P(None, "tp"),
            P(None, "tp"),
            P(None, "tp"),
            P("tp", None),
            P("req", "tp", None),
            P("req", None, "tp"),
            P("req", None),
            P("req", None),
            P("req", None),
            P(),
        ),
        out_specs=P("req", "tp"),
        check_vma=False,
    )
```

```python
import jax
import jax.numpy as jnp
import functools
from jax import lax
from jax.experimental import pallas as pl
from jax.experimental.pallas import tpu as pltpu
from jax.sharding import PartitionSpec as P

HEAD_WIDTH = 128
REQ_DEV = 32
LMAX = 40


def apply_rotary(vectors, token_positions):
    head_size = vectors.shape[-1]
    half_dim = head_size // 2
    inverse = 1000000.0 ** (-(jnp.arange(half_dim, dtype=jnp.float32) * 2.0 / head_size))
    angles = token_positions[:, None] * inverse[None, :]
    cosine = jnp.cos(angles)[:, None, :]
    sine_part = jnp.sin(angles)[:, None, :]
    first_half = vectors[..., :half_dim]
    second = vectors[..., half_dim:]
    return jnp.concatenate(
        [first_half * cosine - second * sine_part, second * cosine + first_half * sine_part], -1
    )


def layout(lengths, groups, tok_rows):
    req_slots = lengths.shape[0]
    row_ids = jnp.arange(tok_rows, dtype=jnp.int32)
    row_ends = jnp.cumsum(lengths)
    starts = row_ends - lengths
    request_row = jnp.sum((row_ids[:, None] >= row_ends[None, :]).astype(jnp.int32), 1)
    request_hot = (request_row[:, None] == jnp.arange(req_slots, dtype=jnp.int32)[None, :]).astype(
        jnp.int32
    )
    previous = jnp.concatenate([jnp.full((1,), -1, jnp.int32), groups[:-1]])
    is_prompt = (groups != previous).astype(jnp.int32)
    prompt_len = jnp.sum(
        lengths[None, :]
        * is_prompt[None, :]
        * (groups[None, :] == groups[:, None]).astype(jnp.int32),
        1,
    )
    offset_req = (1 - is_prompt) * prompt_len - starts
    group_row = jnp.sum(request_hot * groups[None, :], 1)
    prompt_row = jnp.sum(request_hot * is_prompt[None, :], 1)
    offset_row = jnp.sum(request_hot * offset_req[None, :], 1)
    token_positions = (row_ids + offset_row).astype(jnp.float32)
    group_ids = jnp.arange(3, dtype=jnp.int32)
    group_hot = (groups[None, :] == group_ids[:, None]).astype(jnp.int32)
    prompt_start = jnp.sum((starts * is_prompt)[None, :] * group_hot, 1)
    prompt_len = jnp.sum((lengths * is_prompt)[None, :] * group_hot, 1)
    rows = (request_row, group_row, prompt_row, prompt_start, prompt_len)
    return (request_hot, starts, rows, token_positions, row_ids)


BLOCK = 128


def attend_kernel(
    q_ref, cs_ref, sn_ref, k_ref, v_ref, kp_ref, vp_ref, bias_ref, wo_ref, res_ref, out_ref,
    send_buf, relay_in, sum_buf, recv_buf, send_sems, recv_sems, *, tp_count, heads, kv_heads,
    n_blocks
):
    me = lax.axis_index("tp")
    row_dev = lax.axis_index("req")
    piece = out_ref.shape[1]
    half = piece // 2
    up = lax.rem(me + 1, tp_count)
    down = lax.rem(me + tp_count - 1, tp_count)
    across = lax.rem(me + 2, tp_count)
    barrier = pltpu.get_barrier_semaphore()
    for peer in (up, down):
        pl.semaphore_signal(
            barrier, inc=1, device_id=(row_dev, peer), device_id_type=pl.DeviceIdType.MESH
        )
    pl.semaphore_wait(barrier, 2)
    rep = heads // kv_heads

    def raw_copy(b, side):
        col = pl.multiple_of(across * piece + side * half, half)
        return pltpu.make_async_remote_copy(
            src_ref=send_buf.at[b, :, pl.ds(col, half)],
            dst_ref=relay_in.at[b, side],
            send_sem=send_sems.at[b * 4 + side],
            recv_sem=recv_sems.at[b * 4 + side],
            device_id=(row_dev, up if side == 0 else down),
            device_id_type=pl.DeviceIdType.MESH,
        )

    def sum_copy(b, side):
        row = pl.multiple_of(b * BLOCK, BLOCK)
        return pltpu.make_async_remote_copy(
            src_ref=sum_buf.at[b, side],
            dst_ref=recv_buf.at[side, pl.ds(row, BLOCK)],
            send_sem=send_sems.at[b * 4 + 2 + side],
            recv_sem=recv_sems.at[b * 4 + 2 + side],
            device_id=(row_dev, up if side == 0 else down),
            device_id_type=pl.DeviceIdType.MESH,
        )

    def forward(b):
        raw_copy(b, 0).wait_recv()
        raw_copy(b, 1).wait_recv()
        col_up = pl.multiple_of(up * piece, piece)
        col_down = pl.multiple_of(down * piece, piece)
        to_up = send_buf[b, :, pl.ds(col_up, piece)].astype(jnp.float32)
        to_down = send_buf[b, :, pl.ds(col_down, piece)].astype(jnp.float32)
        from_down = relay_in[b, 0].astype(jnp.float32)
        from_up = relay_in[b, 1].astype(jnp.float32)
        sum_buf[b, 0] = jnp.concatenate(
            [to_up[:, :half] + from_down, to_up[:, half:]], 1
        ).astype(sum_buf.dtype)
        sum_buf[b, 1] = jnp.concatenate(
            [to_down[:, :half], to_down[:, half:] + from_up], 1
        ).astype(sum_buf.dtype)
        sum_copy(b, 0).start()
        sum_copy(b, 1).start()

    def block_body(b, carry):
        row = pl.multiple_of(b * BLOCK, BLOCK)
        bias = bias_ref[b]
        cs = cs_ref[pl.ds(row, BLOCK), :]
        sn = sn_ref[pl.ds(row, BLOCK), :]
        outs = []
        for h in range(heads):
            g = h // rep
            qf = q_ref[pl.ds(row, BLOCK), pl.ds(h * 128, 128)]
            qh = (qf * cs + pltpu.roll(qf, 64, 1) * sn).astype(jnp.bfloat16)
            kw = k_ref[pl.ds(row, 2 * BLOCK), pl.ds(g * 128, 128)]
            vw = v_ref[pl.ds(row, 2 * BLOCK), pl.ds(g * 128, 128)]
            kp = kp_ref[:, pl.ds(g * 128, 128)]
            vp = vp_ref[:, pl.ds(g * 128, 128)]
            keys = jnp.concatenate([kw, kp], 0)
            vals = jnp.concatenate([vw, vp], 0)
            s = lax.dot_general(
                qh, keys, (((1,), (1,)), ((), ())), preferred_element_type=jnp.float32
            ) / HEAD_WIDTH**0.5
            s = s + bias
            m = jnp.max(s, -1, keepdims=True)
            w = jnp.exp(s - m)
            p = (w / jnp.sum(w, -1, keepdims=True)).astype(jnp.bfloat16)
            outs.append(
                jnp.dot(p, vals, preferred_element_type=jnp.float32).astype(jnp.bfloat16)
            )
        att = jnp.concatenate(outs, 1)
        part = jnp.dot(att, wo_ref[...], preferred_element_type=jnp.float32)
        send_buf[b] = part.astype(jnp.bfloat16)
        raw_copy(b, 0).start()
        raw_copy(b, 1).start()

        @pl.when(b > 0)
        def _():
            forward(b - 1)

        return carry

    lax.fori_loop(0, n_blocks, block_body, 0)
    forward(n_blocks - 1)

    def wait_body(b, carry):
        for side in (0, 1):
            raw_copy(b, side).wait_send()
            sum_copy(b, side).wait_send()
            sum_copy(b, side).wait_recv()
        return carry

    lax.fori_loop(0, n_blocks, wait_body, 0)
    own = pl.multiple_of(me * piece, piece)

    def finish_body(b, carry):
        row = pl.multiple_of(b * BLOCK, BLOCK)
        total = res_ref[pl.ds(row, BLOCK), :].astype(jnp.float32)
        total = total + send_buf[b, :, pl.ds(own, piece)].astype(jnp.float32)
        for side in (0, 1):
            total = total + recv_buf[side, pl.ds(row, BLOCK), :].astype(jnp.float32)
        out_ref[pl.ds(row, BLOCK), :] = total.astype(out_ref.dtype)
        return carry

    lax.fori_loop(0, n_blocks, finish_body, 0)


def attend_and_reduce(q, cs, sn, k_pad, v_pad, k_prompt, v_prompt, bias, wo, residual, tp_count):
    rows, q_width = q.shape
    n_blocks = rows // BLOCK
    piece = residual.shape[1]
    width = wo.shape[1]
    kernel = functools.partial(
        attend_kernel,
        tp_count=tp_count,
        heads=q_width // HEAD_WIDTH,
        kv_heads=k_pad.shape[1] // HEAD_WIDTH,
        n_blocks=n_blocks,
    )
    vmem = pltpu.MemorySpace.VMEM
    return pl.pallas_call(
        kernel,
        out_shape=jax.ShapeDtypeStruct((rows, piece), jnp.bfloat16),
        in_specs=[pl.BlockSpec(memory_space=vmem)] * 10,
        out_specs=pl.BlockSpec(memory_space=vmem),
        scratch_shapes=[
            pltpu.VMEM((n_blocks, BLOCK, width), jnp.bfloat16),
            pltpu.VMEM((n_blocks, 2, BLOCK, piece // 2), jnp.bfloat16),
            pltpu.VMEM((n_blocks, 2, BLOCK, piece), jnp.bfloat16),
            pltpu.VMEM((2, rows, piece), jnp.bfloat16),
            pltpu.SemaphoreType.DMA((n_blocks * 4,)),
            pltpu.SemaphoreType.DMA((n_blocks * 4,)),
        ],
        compiler_params=pltpu.CompilerParams(
            collective_id=0, has_side_effects=True, vmem_limit_bytes=48 * 1024 * 1024
        ),
    )(q, cs, sn, k_pad, v_pad, k_prompt, v_prompt, bias, wo, residual)


def ids_kernel(wanted_ref, out_ref, landing, send_sems, recv_sems):
    me = lax.axis_index("req")
    col = lax.axis_index("tp")
    count = lax.axis_size("req")
    barrier = pltpu.get_barrier_semaphore()

    def greet(k, carry):
        peer = lax.rem(me + k, count)
        pl.semaphore_signal(
            barrier, inc=1, device_id=(peer, col), device_id_type=pl.DeviceIdType.MESH
        )
        return carry

    lax.fori_loop(1, count, greet, 0)
    pl.semaphore_wait(barrier, count - 1)

    def copy_to(k):
        dest = lax.rem(me + k, count)
        return pltpu.make_async_remote_copy(
            src_ref=wanted_ref.at[dest],
            dst_ref=landing.at[me],
            send_sem=send_sems.at[k],
            recv_sem=recv_sems.at[k],
            device_id=(dest, col),
            device_id_type=pl.DeviceIdType.MESH,
        )

    def copy_from(k):
        source = lax.rem(me + count - k, count)
        return pltpu.make_async_remote_copy(
            src_ref=wanted_ref.at[source],
            dst_ref=landing.at[source],
            send_sem=send_sems.at[k],
            recv_sem=recv_sems.at[k],
            device_id=(source, col),
            device_id_type=pl.DeviceIdType.MESH,
        )

    def send(k, carry):
        copy_to(k).start()
        return carry

    lax.fori_loop(1, count, send, 0)
    out_ref[me] = wanted_ref[me]

    def finish(k, carry):
        copy_to(k).wait_send()
        copy_from(k).wait_recv()
        source = lax.rem(me + count - k, count)
        out_ref[source] = landing[source]
        return carry

    lax.fori_loop(1, count, finish, 0)


def exchange_ids(wanted):
    count = wanted.shape[0]
    tiles = jnp.broadcast_to(wanted[:, None, None], (count, 8, 128))
    vmem = pltpu.MemorySpace.VMEM
    got = pl.pallas_call(
        ids_kernel,
        out_shape=jax.ShapeDtypeStruct((count, 8, 128), jnp.int32),
        in_specs=[pl.BlockSpec(memory_space=vmem)],
        out_specs=pl.BlockSpec(memory_space=vmem),
        scratch_shapes=[
            pltpu.VMEM((count, 8, 128), jnp.int32),
            pltpu.SemaphoreType.DMA((count,)),
            pltpu.SemaphoreType.DMA((count,)),
        ],
        compiler_params=pltpu.CompilerParams(collective_id=1, has_side_effects=True),
    )(tiles)
    return got[:, 0, 0]


def per_device(
    tokens,
    input_norm_gain,
    query_matrix,
    key_matrix,
    value_matrix,
    output_matrix,
    adapter_down_maps,
    adapter_up_maps,
    request_row_counts,
    prompt_group_per_request,
    adapter_per_request,
    adapter_table_slot,
):
    tp_count = lax.axis_size("tp")
    req_count = lax.axis_size("req")
    tp_index = lax.axis_index("tp")
    tok_rows, width = tokens.shape
    piece_width = width // tp_count
    lengths = request_row_counts[0]
    groups = prompt_group_per_request[0]
    adapters = adapter_per_request[0]
    req_slots = lengths.shape[0]
    request_hot, starts, row_info, token_positions, row_ids = layout(lengths, groups, tok_rows)
    adapters_per_part = adapter_down_maps.shape[0]
    rank_extent = adapter_down_maps.shape[2]
    slots = adapter_table_slot[adapters]
    holder = slots // adapters_per_part
    local_slot = slots % adapters_per_part
    holder_ids = jnp.arange(req_count, dtype=jnp.int32)
    holder_hot = (holder[None, :] == holder_ids[:, None]).astype(jnp.int32)
    wanted = jnp.sum(holder_hot * local_slot[None, :], 1)
    wanted_in = exchange_ids(wanted)
    table = jnp.concatenate([jnp.transpose(adapter_down_maps, (0, 2, 1)), adapter_up_maps], 1)
    float_tok = tokens.astype(jnp.float32)
    normalized_input = (
        float_tok
        * lax.rsqrt(jnp.mean(float_tok * float_tok, -1, keepdims=True) + 1e-06)
        * input_norm_gain
    ).astype(jnp.bfloat16)
    maps_out = table[wanted_in]
    normalized_input, maps_out = lax.optimization_barrier((normalized_input, maps_out))
    maps_in = lax.all_to_all(maps_out, "req", split_axis=0, concat_axis=0, tiled=True)
    down_in = maps_in[:, :rank_extent, :].reshape(req_count * rank_extent, piece_width)
    up_in = maps_in[:, rank_extent:, :].reshape(req_count * rank_extent, piece_width)
    normed_slice = lax.dynamic_slice_in_dim(
        normalized_input, tp_index * piece_width, piece_width, 1
    )
    holder_row = jnp.sum(request_hot * holder[None, :], 1)
    pick = (holder_row[:, None] == holder_ids[None, :])[:, :, None]
    wide_rank = jnp.dot(
        normed_slice, down_in.T, preferred_element_type=jnp.float32
    ).reshape(tok_rows, req_count, rank_extent)
    partial_rank = jnp.sum(jnp.where(pick, wide_rank, jnp.float32(0.0)), 1)
    arrived = [
        lax.ppermute(partial_rank, "tp", [(i, (i + k) % tp_count) for i in range(tp_count)])
        for k in range(1, tp_count)
    ]
    for piece in arrived:
        partial_rank = partial_rank + piece
    rank = partial_rank.astype(jnp.bfloat16)
    spread = jnp.where(pick, rank[:, None, :], jnp.zeros((), jnp.bfloat16)).reshape(
        tok_rows, req_count * rank_extent
    )
    query_delta = (
        2.0 * jnp.dot(spread, up_in, preferred_element_type=jnp.float32)
    ).astype(jnp.bfloat16)
    heads_local = query_matrix.shape[1] // HEAD_WIDTH
    kv_local = key_matrix.shape[1] // HEAD_WIDTH
    query_full = jnp.dot(
        normalized_input, query_matrix, preferred_element_type=jnp.float32
    ) + query_delta.astype(jnp.float32)
    half_dim = HEAD_WIDTH // 2
    inverse = 1000000.0 ** (-(jnp.arange(half_dim, dtype=jnp.float32) * 2.0 / HEAD_WIDTH))
    angles = token_positions[:, None] * inverse[None, :]
    cosine = jnp.cos(angles)
    sine = jnp.sin(angles)
    cos_pair = jnp.concatenate([cosine, cosine], 1)
    sin_pair = jnp.concatenate([-sine, sine], 1)
    key_complete = jnp.dot(normalized_input, key_matrix, preferred_element_type=jnp.float32)
    key_head_rows = apply_rotary(
        key_complete.reshape(tok_rows, kv_local, HEAD_WIDTH), token_positions
    ).astype(jnp.bfloat16)
    value_head_rows = (
        jnp.dot(normalized_input, value_matrix, preferred_element_type=jnp.float32)
        .astype(jnp.bfloat16)
        .reshape(tok_rows, kv_local, HEAD_WIDTH)
    )
    request_row, group_row, prompt_row, prompt_start, prompt_len = row_info
    n_blocks = tok_rows // BLOCK
    group_count = prompt_start.shape[0]
    kv_width = kv_local * HEAD_WIDTH
    key_flat = key_head_rows.reshape(tok_rows, kv_width)
    value_flat = value_head_rows.reshape(tok_rows, kv_width)
    front = jnp.zeros((BLOCK, kv_width), jnp.bfloat16)
    k_pad = jnp.concatenate([front, key_flat], 0)
    v_pad = jnp.concatenate([front, value_flat], 0)
    clamp_start = jnp.clip(prompt_start, 0, tok_rows - LMAX)
    extra = BLOCK - group_count * LMAX
    k_prompt = jnp.concatenate(
        [lax.dynamic_slice_in_dim(key_flat, clamp_start[g], LMAX, 0) for g in range(group_count)]
        + [jnp.zeros((extra, kv_width), jnp.bfloat16)],
        0,
    )
    v_prompt = jnp.concatenate(
        [lax.dynamic_slice_in_dim(value_flat, clamp_start[g], LMAX, 0) for g in range(group_count)]
        + [jnp.zeros((extra, kv_width), jnp.bfloat16)],
        0,
    )
    def windows(values, fill):
        padded = jnp.concatenate([jnp.full((BLOCK,), fill, values.dtype), values]).reshape(
            n_blocks + 1, BLOCK
        )
        return jnp.concatenate([padded[:-1], padded[1:]], 1)

    win_row = windows(row_ids, -1)
    win_req = windows(request_row, -1)
    win_grp = windows(group_row, -1)
    win_prm = windows(prompt_row, 0)
    q_row = row_ids.reshape(n_blocks, BLOCK)[:, :, None]
    q_req = request_row.reshape(n_blocks, BLOCK)[:, :, None]
    q_grp = group_row.reshape(n_blocks, BLOCK)[:, :, None]
    win_vis = (
        (win_row[:, None, :] >= 0)
        & (win_grp[:, None, :] == q_grp)
        & (win_row[:, None, :] <= q_row)
        & ((win_req[:, None, :] == q_req) | (win_prm[:, None, :] == 1))
    )
    p_row = (clamp_start[:, None] + jnp.arange(LMAX, dtype=jnp.int32)[None, :]).reshape(-1)
    p_lo = jnp.repeat(prompt_start, LMAX)
    p_hi = jnp.repeat(prompt_start + prompt_len, LMAX)
    p_grp = jnp.repeat(jnp.arange(group_count, dtype=jnp.int32), LMAX)
    p_row = jnp.concatenate([p_row, jnp.zeros((extra,), jnp.int32)])
    p_lo = jnp.concatenate([p_lo, jnp.ones((extra,), jnp.int32)])
    p_hi = jnp.concatenate([p_hi, jnp.zeros((extra,), jnp.int32)])
    p_grp = jnp.concatenate([p_grp, jnp.full((extra,), -1, jnp.int32)])
    win_first = q_row[:, :1, :] - BLOCK
    prompt_vis = (
        (p_grp[None, None, :] == q_grp)
        & (p_row[None, None, :] >= p_lo[None, None, :])
        & (p_row[None, None, :] < p_hi[None, None, :])
        & (p_row[None, None, :] < win_first)
        & (p_row[None, None, :] <= q_row)
    )
    vis = jnp.concatenate([win_vis, prompt_vis], 2)
    bias = jnp.where(vis, jnp.float32(0.0), jnp.float32(-1e30))
    residual = lax.dynamic_slice_in_dim(tokens, tp_index * piece_width, piece_width, 1)
    return attend_and_reduce(
        query_full,
        cos_pair,
        sin_pair,
        k_pad,
        v_pad,
        k_prompt,
        v_prompt,
        bias,
        output_matrix,
        residual,
        tp_count,
    )


def solution(mesh):
    return jax.shard_map(
        per_device,
        mesh=mesh,
        in_specs=(
            P("req", None),
            P(),
            P(None, "tp"),
            P(None, "tp"),
            P(None, "tp"),
            P("tp", None),
            P("req", "tp", None),
            P("req", None, "tp"),
            P("req", None),
            P("req", None),
            P("req", None),
            P(),
        ),
        out_specs=P("req", "tp"),
        check_vma=False,
    )
```

```python
import jax
import jax.numpy as jnp
import functools
from jax import lax
from jax.experimental import pallas as pl
from jax.experimental.pallas import tpu as pltpu
from jax.sharding import PartitionSpec as P

HEAD_WIDTH = 128
REQ_DEV = 32
LMAX = 40


def apply_rotary(vectors, token_positions):
    head_size = vectors.shape[-1]
    half_dim = head_size // 2
    inverse = 1000000.0 ** (-(jnp.arange(half_dim, dtype=jnp.float32) * 2.0 / head_size))
    angles = token_positions[:, None] * inverse[None, :]
    cosine = jnp.cos(angles)[:, None, :]
    sine_part = jnp.sin(angles)[:, None, :]
    first_half = vectors[..., :half_dim]
    second = vectors[..., half_dim:]
    return jnp.concatenate(
        [first_half * cosine - second * sine_part, second * cosine + first_half * sine_part], -1
    )


def layout(lengths, groups, tok_rows):
    req_slots = lengths.shape[0]
    row_ids = jnp.arange(tok_rows, dtype=jnp.int32)
    row_ends = jnp.cumsum(lengths)
    starts = row_ends - lengths
    request_row = jnp.sum((row_ids[:, None] >= row_ends[None, :]).astype(jnp.int32), 1)
    request_hot = (request_row[:, None] == jnp.arange(req_slots, dtype=jnp.int32)[None, :]).astype(
        jnp.int32
    )
    previous = jnp.concatenate([jnp.full((1,), -1, jnp.int32), groups[:-1]])
    is_prompt = (groups != previous).astype(jnp.int32)
    prompt_len = jnp.sum(
        lengths[None, :]
        * is_prompt[None, :]
        * (groups[None, :] == groups[:, None]).astype(jnp.int32),
        1,
    )
    offset_req = (1 - is_prompt) * prompt_len - starts
    group_row = jnp.sum(request_hot * groups[None, :], 1)
    prompt_row = jnp.sum(request_hot * is_prompt[None, :], 1)
    offset_row = jnp.sum(request_hot * offset_req[None, :], 1)
    token_positions = (row_ids + offset_row).astype(jnp.float32)
    group_ids = jnp.arange(3, dtype=jnp.int32)
    group_hot = (groups[None, :] == group_ids[:, None]).astype(jnp.int32)
    prompt_start = jnp.sum((starts * is_prompt)[None, :] * group_hot, 1)
    prompt_len = jnp.sum((lengths * is_prompt)[None, :] * group_hot, 1)
    rows = (request_row, group_row, prompt_row, prompt_start, prompt_len)
    return (request_hot, starts, rows, token_positions, row_ids)


BLOCK = 128


def attend_kernel(
    q_ref, cs_ref, sn_ref, k_ref, v_ref, kp_ref, vp_ref, bias_ref, wo_ref, res_ref, out_ref,
    send_buf, relay_in, sum_buf, recv_buf, send_sems, recv_sems, *, tp_count, heads, kv_heads,
    n_blocks
):
    me = lax.axis_index("tp")
    row_dev = lax.axis_index("req")
    piece = out_ref.shape[1]
    half = piece // 2
    up = lax.rem(me + 1, tp_count)
    down = lax.rem(me + tp_count - 1, tp_count)
    across = lax.rem(me + 2, tp_count)
    barrier = pltpu.get_barrier_semaphore()
    for peer in (up, down):
        pl.semaphore_signal(
            barrier, inc=1, device_id=(row_dev, peer), device_id_type=pl.DeviceIdType.MESH
        )
    pl.semaphore_wait(barrier, 2)
    rep = heads // kv_heads

    def raw_copy(b, side):
        col = pl.multiple_of(across * piece + side * half, half)
        return pltpu.make_async_remote_copy(
            src_ref=send_buf.at[b, :, pl.ds(col, half)],
            dst_ref=relay_in.at[b, side],
            send_sem=send_sems.at[b * 4 + side],
            recv_sem=recv_sems.at[b * 4 + side],
            device_id=(row_dev, up if side == 0 else down),
            device_id_type=pl.DeviceIdType.MESH,
        )

    def sum_copy(b, side):
        row = pl.multiple_of(b * BLOCK, BLOCK)
        return pltpu.make_async_remote_copy(
            src_ref=sum_buf.at[b, side],
            dst_ref=recv_buf.at[side, pl.ds(row, BLOCK)],
            send_sem=send_sems.at[b * 4 + 2 + side],
            recv_sem=recv_sems.at[b * 4 + 2 + side],
            device_id=(row_dev, up if side == 0 else down),
            device_id_type=pl.DeviceIdType.MESH,
        )

    def forward(b):
        raw_copy(b, 0).wait_recv()
        raw_copy(b, 1).wait_recv()
        col_up = pl.multiple_of(up * piece, piece)
        col_down = pl.multiple_of(down * piece, piece)
        to_up = send_buf[b, :, pl.ds(col_up, piece)].astype(jnp.float32)
        to_down = send_buf[b, :, pl.ds(col_down, piece)].astype(jnp.float32)
        from_down = relay_in[b, 0].astype(jnp.float32)
        from_up = relay_in[b, 1].astype(jnp.float32)
        sum_buf[b, 0] = jnp.concatenate(
            [to_up[:, :half] + from_down, to_up[:, half:]], 1
        ).astype(sum_buf.dtype)
        sum_buf[b, 1] = jnp.concatenate(
            [to_down[:, :half], to_down[:, half:] + from_up], 1
        ).astype(sum_buf.dtype)
        sum_copy(b, 0).start()
        sum_copy(b, 1).start()

    def block_body(b, carry):
        row = pl.multiple_of(b * BLOCK, BLOCK)
        bias = bias_ref[b]
        cs = cs_ref[pl.ds(row, BLOCK), :]
        sn = sn_ref[pl.ds(row, BLOCK), :]
        outs = []
        for h in range(heads):
            g = h // rep
            qf = q_ref[pl.ds(row, BLOCK), pl.ds(h * 128, 128)]
            qh = (qf * cs + pltpu.roll(qf, 64, 1) * sn).astype(jnp.bfloat16)
            kw = k_ref[pl.ds(row, 2 * BLOCK), pl.ds(g * 128, 128)]
            vw = v_ref[pl.ds(row, 2 * BLOCK), pl.ds(g * 128, 128)]
            kp = kp_ref[:, pl.ds(g * 128, 128)]
            vp = vp_ref[:, pl.ds(g * 128, 128)]
            keys = jnp.concatenate([kw, kp], 0)
            vals = jnp.concatenate([vw, vp], 0)
            s = lax.dot_general(
                qh, keys, (((1,), (1,)), ((), ())), preferred_element_type=jnp.float32
            ) / HEAD_WIDTH**0.5
            s = s + bias
            m = jnp.max(s, -1, keepdims=True)
            w = jnp.exp(s - m)
            p = (w / jnp.sum(w, -1, keepdims=True)).astype(jnp.bfloat16)
            outs.append(
                jnp.dot(p, vals, preferred_element_type=jnp.float32).astype(jnp.bfloat16)
            )
        att = jnp.concatenate(outs, 1)
        part = jnp.dot(att, wo_ref[...], preferred_element_type=jnp.float32)
        send_buf[b] = part.astype(jnp.bfloat16)
        raw_copy(b, 0).start()
        raw_copy(b, 1).start()

        @pl.when(b > 0)
        def _():
            forward(b - 1)

        return carry

    lax.fori_loop(0, n_blocks, block_body, 0)
    forward(n_blocks - 1)

    def wait_body(b, carry):
        for side in (0, 1):
            raw_copy(b, side).wait_send()
            sum_copy(b, side).wait_send()
            sum_copy(b, side).wait_recv()
        return carry

    lax.fori_loop(0, n_blocks, wait_body, 0)
    own = pl.multiple_of(me * piece, piece)

    def finish_body(b, carry):
        row = pl.multiple_of(b * BLOCK, BLOCK)
        total = res_ref[pl.ds(row, BLOCK), :].astype(jnp.float32)
        total = total + send_buf[b, :, pl.ds(own, piece)].astype(jnp.float32)
        for side in (0, 1):
            total = total + recv_buf[side, pl.ds(row, BLOCK), :].astype(jnp.float32)
        out_ref[pl.ds(row, BLOCK), :] = total.astype(out_ref.dtype)
        return carry

    lax.fori_loop(0, n_blocks, finish_body, 0)


def attend_and_reduce(q, cs, sn, k_pad, v_pad, k_prompt, v_prompt, bias, wo, residual, tp_count):
    rows, q_width = q.shape
    n_blocks = rows // BLOCK
    piece = residual.shape[1]
    width = wo.shape[1]
    kernel = functools.partial(
        attend_kernel,
        tp_count=tp_count,
        heads=q_width // HEAD_WIDTH,
        kv_heads=k_pad.shape[1] // HEAD_WIDTH,
        n_blocks=n_blocks,
    )
    vmem = pltpu.MemorySpace.VMEM
    return pl.pallas_call(
        kernel,
        out_shape=jax.ShapeDtypeStruct((rows, piece), jnp.bfloat16),
        in_specs=[pl.BlockSpec(memory_space=vmem)] * 10,
        out_specs=pl.BlockSpec(memory_space=vmem),
        scratch_shapes=[
            pltpu.VMEM((n_blocks, BLOCK, width), jnp.bfloat16),
            pltpu.VMEM((n_blocks, 2, BLOCK, piece // 2), jnp.bfloat16),
            pltpu.VMEM((n_blocks, 2, BLOCK, piece), jnp.bfloat16),
            pltpu.VMEM((2, rows, piece), jnp.bfloat16),
            pltpu.SemaphoreType.DMA((n_blocks * 4,)),
            pltpu.SemaphoreType.DMA((n_blocks * 4,)),
        ],
        compiler_params=pltpu.CompilerParams(
            collective_id=0, has_side_effects=True, vmem_limit_bytes=48 * 1024 * 1024
        ),
    )(q, cs, sn, k_pad, v_pad, k_prompt, v_prompt, bias, wo, residual)


def ids_kernel(wanted_ref, out_ref, landing, send_sems, recv_sems):
    me = lax.axis_index("req")
    col = lax.axis_index("tp")
    count = lax.axis_size("req")
    barrier = pltpu.get_barrier_semaphore()

    def greet(k, carry):
        peer = lax.rem(me + k, count)
        pl.semaphore_signal(
            barrier, inc=1, device_id=(peer, col), device_id_type=pl.DeviceIdType.MESH
        )
        return carry

    lax.fori_loop(1, count, greet, 0)
    pl.semaphore_wait(barrier, count - 1)

    def copy_to(k):
        dest = lax.rem(me + k, count)
        return pltpu.make_async_remote_copy(
            src_ref=wanted_ref.at[dest],
            dst_ref=landing.at[me],
            send_sem=send_sems.at[k],
            recv_sem=recv_sems.at[k],
            device_id=(dest, col),
            device_id_type=pl.DeviceIdType.MESH,
        )

    def copy_from(k):
        source = lax.rem(me + count - k, count)
        return pltpu.make_async_remote_copy(
            src_ref=wanted_ref.at[source],
            dst_ref=landing.at[source],
            send_sem=send_sems.at[k],
            recv_sem=recv_sems.at[k],
            device_id=(source, col),
            device_id_type=pl.DeviceIdType.MESH,
        )

    def send(k, carry):
        copy_to(k).start()
        return carry

    lax.fori_loop(1, count, send, 0)
    out_ref[me] = wanted_ref[me]

    def finish(k, carry):
        copy_to(k).wait_send()
        copy_from(k).wait_recv()
        source = lax.rem(me + count - k, count)
        out_ref[source] = landing[source]
        return carry

    lax.fori_loop(1, count, finish, 0)


def exchange_ids(wanted):
    count = wanted.shape[0]
    tiles = jnp.broadcast_to(wanted[:, None, None], (count, 8, 128))
    vmem = pltpu.MemorySpace.VMEM
    got = pl.pallas_call(
        ids_kernel,
        out_shape=jax.ShapeDtypeStruct((count, 8, 128), jnp.int32),
        in_specs=[pl.BlockSpec(memory_space=vmem)],
        out_specs=pl.BlockSpec(memory_space=vmem),
        scratch_shapes=[
            pltpu.VMEM((count, 8, 128), jnp.int32),
            pltpu.SemaphoreType.DMA((count,)),
            pltpu.SemaphoreType.DMA((count,)),
        ],
        compiler_params=pltpu.CompilerParams(collective_id=1, has_side_effects=True),
    )(tiles)
    return got[:, 0, 0]


def per_device(
    tokens,
    input_norm_gain,
    query_matrix,
    key_matrix,
    value_matrix,
    output_matrix,
    adapter_down_maps,
    adapter_up_maps,
    request_row_counts,
    prompt_group_per_request,
    adapter_per_request,
    adapter_table_slot,
):
    tp_count = lax.axis_size("tp")
    req_count = lax.axis_size("req")
    tp_index = lax.axis_index("tp")
    tok_rows, width = tokens.shape
    piece_width = width // tp_count
    lengths = request_row_counts[0]
    groups = prompt_group_per_request[0]
    adapters = adapter_per_request[0]
    req_slots = lengths.shape[0]
    request_hot, starts, row_info, token_positions, row_ids = layout(lengths, groups, tok_rows)
    adapters_per_part = adapter_down_maps.shape[0]
    rank_extent = adapter_down_maps.shape[2]
    slots = adapter_table_slot[adapters]
    holder = slots // adapters_per_part
    local_slot = slots % adapters_per_part
    holder_ids = jnp.arange(req_count, dtype=jnp.int32)
    holder_hot = (holder[None, :] == holder_ids[:, None]).astype(jnp.int32)
    wanted = jnp.sum(holder_hot * local_slot[None, :], 1)
    wanted_in = exchange_ids(wanted)
    table = jnp.concatenate([jnp.transpose(adapter_down_maps, (0, 2, 1)), adapter_up_maps], 1)
    maps_out = table[wanted_in]
    tokens, maps_out = lax.optimization_barrier((tokens, maps_out))
    float_tok = tokens.astype(jnp.float32)
    normalized_input = (
        float_tok
        * lax.rsqrt(jnp.mean(float_tok * float_tok, -1, keepdims=True) + 1e-06)
        * input_norm_gain
    ).astype(jnp.bfloat16)
    maps_in = lax.all_to_all(maps_out, "req", split_axis=0, concat_axis=0, tiled=True)
    down_in = maps_in[:, :rank_extent, :].reshape(req_count * rank_extent, piece_width)
    up_in = maps_in[:, rank_extent:, :].reshape(req_count * rank_extent, piece_width)
    normed_slice = lax.dynamic_slice_in_dim(
        normalized_input, tp_index * piece_width, piece_width, 1
    )
    holder_row = jnp.sum(request_hot * holder[None, :], 1)
    pick = (holder_row[:, None] == holder_ids[None, :])[:, :, None]
    wide_rank = jnp.dot(
        normed_slice, down_in.T, preferred_element_type=jnp.float32
    ).reshape(tok_rows, req_count, rank_extent)
    partial_rank = jnp.sum(jnp.where(pick, wide_rank, jnp.float32(0.0)), 1)
    arrived = [
        lax.ppermute(partial_rank, "tp", [(i, (i + k) % tp_count) for i in range(tp_count)])
        for k in range(1, tp_count)
    ]
    for piece in arrived:
        partial_rank = partial_rank + piece
    rank = partial_rank.astype(jnp.bfloat16)
    spread = jnp.where(pick, rank[:, None, :], jnp.zeros((), jnp.bfloat16)).reshape(
        tok_rows, req_count * rank_extent
    )
    query_delta = (
        2.0 * jnp.dot(spread, up_in, preferred_element_type=jnp.float32)
    ).astype(jnp.bfloat16)
    heads_local = query_matrix.shape[1] // HEAD_WIDTH
    kv_local = key_matrix.shape[1] // HEAD_WIDTH
    query_full = jnp.dot(
        normalized_input, query_matrix, preferred_element_type=jnp.float32
    ) + query_delta.astype(jnp.float32)
    half_dim = HEAD_WIDTH // 2
    inverse = 1000000.0 ** (-(jnp.arange(half_dim, dtype=jnp.float32) * 2.0 / HEAD_WIDTH))
    angles = token_positions[:, None] * inverse[None, :]
    cosine = jnp.cos(angles)
    sine = jnp.sin(angles)
    cos_pair = jnp.concatenate([cosine, cosine], 1)
    sin_pair = jnp.concatenate([-sine, sine], 1)
    key_complete = jnp.dot(normalized_input, key_matrix, preferred_element_type=jnp.float32)
    key_head_rows = apply_rotary(
        key_complete.reshape(tok_rows, kv_local, HEAD_WIDTH), token_positions
    ).astype(jnp.bfloat16)
    value_head_rows = (
        jnp.dot(normalized_input, value_matrix, preferred_element_type=jnp.float32)
        .astype(jnp.bfloat16)
        .reshape(tok_rows, kv_local, HEAD_WIDTH)
    )
    request_row, group_row, prompt_row, prompt_start, prompt_len = row_info
    n_blocks = tok_rows // BLOCK
    group_count = prompt_start.shape[0]
    kv_width = kv_local * HEAD_WIDTH
    key_flat = key_head_rows.reshape(tok_rows, kv_width)
    value_flat = value_head_rows.reshape(tok_rows, kv_width)
    front = jnp.zeros((BLOCK, kv_width), jnp.bfloat16)
    k_pad = jnp.concatenate([front, key_flat], 0)
    v_pad = jnp.concatenate([front, value_flat], 0)
    clamp_start = jnp.clip(prompt_start, 0, tok_rows - LMAX)
    extra = BLOCK - group_count * LMAX
    k_prompt = jnp.concatenate(
        [lax.dynamic_slice_in_dim(key_flat, clamp_start[g], LMAX, 0) for g in range(group_count)]
        + [jnp.zeros((extra, kv_width), jnp.bfloat16)],
        0,
    )
    v_prompt = jnp.concatenate(
        [lax.dynamic_slice_in_dim(value_flat, clamp_start[g], LMAX, 0) for g in range(group_count)]
        + [jnp.zeros((extra, kv_width), jnp.bfloat16)],
        0,
    )
    def windows(values, fill):
        padded = jnp.concatenate([jnp.full((BLOCK,), fill, values.dtype), values]).reshape(
            n_blocks + 1, BLOCK
        )
        return jnp.concatenate([padded[:-1], padded[1:]], 1)

    win_row = windows(row_ids, -1)
    win_req = windows(request_row, -1)
    win_grp = windows(group_row, -1)
    win_prm = windows(prompt_row, 0)
    q_row = row_ids.reshape(n_blocks, BLOCK)[:, :, None]
    q_req = request_row.reshape(n_blocks, BLOCK)[:, :, None]
    q_grp = group_row.reshape(n_blocks, BLOCK)[:, :, None]
    win_vis = (
        (win_row[:, None, :] >= 0)
        & (win_grp[:, None, :] == q_grp)
        & (win_row[:, None, :] <= q_row)
        & ((win_req[:, None, :] == q_req) | (win_prm[:, None, :] == 1))
    )
    p_row = (clamp_start[:, None] + jnp.arange(LMAX, dtype=jnp.int32)[None, :]).reshape(-1)
    p_lo = jnp.repeat(prompt_start, LMAX)
    p_hi = jnp.repeat(prompt_start + prompt_len, LMAX)
    p_grp = jnp.repeat(jnp.arange(group_count, dtype=jnp.int32), LMAX)
    p_row = jnp.concatenate([p_row, jnp.zeros((extra,), jnp.int32)])
    p_lo = jnp.concatenate([p_lo, jnp.ones((extra,), jnp.int32)])
    p_hi = jnp.concatenate([p_hi, jnp.zeros((extra,), jnp.int32)])
    p_grp = jnp.concatenate([p_grp, jnp.full((extra,), -1, jnp.int32)])
    win_first = q_row[:, :1, :] - BLOCK
    prompt_vis = (
        (p_grp[None, None, :] == q_grp)
        & (p_row[None, None, :] >= p_lo[None, None, :])
        & (p_row[None, None, :] < p_hi[None, None, :])
        & (p_row[None, None, :] < win_first)
        & (p_row[None, None, :] <= q_row)
    )
    vis = jnp.concatenate([win_vis, prompt_vis], 2)
    bias = jnp.where(vis, jnp.float32(0.0), jnp.float32(-1e30))
    residual = lax.dynamic_slice_in_dim(tokens, tp_index * piece_width, piece_width, 1)
    return attend_and_reduce(
        query_full,
        cos_pair,
        sin_pair,
        k_pad,
        v_pad,
        k_prompt,
        v_prompt,
        bias,
        output_matrix,
        residual,
        tp_count,
    )


def solution(mesh):
    return jax.shard_map(
        per_device,
        mesh=mesh,
        in_specs=(
            P("req", None),
            P(),
            P(None, "tp"),
            P(None, "tp"),
            P(None, "tp"),
            P("tp", None),
            P("req", "tp", None),
            P("req", None, "tp"),
            P("req", None),
            P("req", None),
            P("req", None),
            P(),
        ),
        out_specs=P("req", "tp"),
        check_vma=False,
    )
```

```python
import jax
import jax.numpy as jnp
import functools
from jax import lax
from jax.experimental import pallas as pl
from jax.experimental.pallas import tpu as pltpu
from jax.sharding import PartitionSpec as P

HEAD_WIDTH = 128
REQ_DEV = 32
LMAX = 40


def apply_rotary(vectors, token_positions):
    head_size = vectors.shape[-1]
    half_dim = head_size // 2
    inverse = 1000000.0 ** (-(jnp.arange(half_dim, dtype=jnp.float32) * 2.0 / head_size))
    angles = token_positions[:, None] * inverse[None, :]
    cosine = jnp.cos(angles)[:, None, :]
    sine_part = jnp.sin(angles)[:, None, :]
    first_half = vectors[..., :half_dim]
    second = vectors[..., half_dim:]
    return jnp.concatenate(
        [first_half * cosine - second * sine_part, second * cosine + first_half * sine_part], -1
    )


def layout(lengths, groups, tok_rows):
    req_slots = lengths.shape[0]
    row_ids = jnp.arange(tok_rows, dtype=jnp.int32)
    row_ends = jnp.cumsum(lengths)
    starts = row_ends - lengths
    request_row = jnp.sum((row_ids[:, None] >= row_ends[None, :]).astype(jnp.int32), 1)
    request_hot = (request_row[:, None] == jnp.arange(req_slots, dtype=jnp.int32)[None, :]).astype(
        jnp.int32
    )
    previous = jnp.concatenate([jnp.full((1,), -1, jnp.int32), groups[:-1]])
    is_prompt = (groups != previous).astype(jnp.int32)
    prompt_len = jnp.sum(
        lengths[None, :]
        * is_prompt[None, :]
        * (groups[None, :] == groups[:, None]).astype(jnp.int32),
        1,
    )
    offset_req = (1 - is_prompt) * prompt_len - starts
    group_row = jnp.sum(request_hot * groups[None, :], 1)
    prompt_row = jnp.sum(request_hot * is_prompt[None, :], 1)
    offset_row = jnp.sum(request_hot * offset_req[None, :], 1)
    token_positions = (row_ids + offset_row).astype(jnp.float32)
    group_ids = jnp.arange(3, dtype=jnp.int32)
    group_hot = (groups[None, :] == group_ids[:, None]).astype(jnp.int32)
    prompt_start = jnp.sum((starts * is_prompt)[None, :] * group_hot, 1)
    prompt_len = jnp.sum((lengths * is_prompt)[None, :] * group_hot, 1)
    rows = (request_row, group_row, prompt_row, prompt_start, prompt_len)
    return (request_hot, starts, rows, token_positions, row_ids)


BLOCK = 128


def attend_kernel(
    q_ref, cs_ref, sn_ref, k_ref, v_ref, kp_ref, vp_ref, bias_ref, wo_ref, res_ref, out_ref,
    send_buf, relay_in, sum_buf, recv_buf, send_sems, recv_sems, *, tp_count, heads, kv_heads,
    n_blocks
):
    me = lax.axis_index("tp")
    row_dev = lax.axis_index("req")
    piece = out_ref.shape[1]
    half = piece // 2
    up = lax.rem(me + 1, tp_count)
    down = lax.rem(me + tp_count - 1, tp_count)
    across = lax.rem(me + 2, tp_count)
    barrier = pltpu.get_barrier_semaphore()
    for peer in (up, down):
        pl.semaphore_signal(
            barrier, inc=1, device_id=(row_dev, peer), device_id_type=pl.DeviceIdType.MESH
        )
    pl.semaphore_wait(barrier, 2)
    rep = heads // kv_heads

    def raw_copy(b, side):
        col = pl.multiple_of(across * piece + side * half, half)
        return pltpu.make_async_remote_copy(
            src_ref=send_buf.at[b, :, pl.ds(col, half)],
            dst_ref=relay_in.at[b, side],
            send_sem=send_sems.at[b * 4 + side],
            recv_sem=recv_sems.at[b * 4 + side],
            device_id=(row_dev, up if side == 0 else down),
            device_id_type=pl.DeviceIdType.MESH,
        )

    def sum_copy(b, side):
        row = pl.multiple_of(b * BLOCK, BLOCK)
        return pltpu.make_async_remote_copy(
            src_ref=sum_buf.at[b, side],
            dst_ref=recv_buf.at[side, pl.ds(row, BLOCK)],
            send_sem=send_sems.at[b * 4 + 2 + side],
            recv_sem=recv_sems.at[b * 4 + 2 + side],
            device_id=(row_dev, up if side == 0 else down),
            device_id_type=pl.DeviceIdType.MESH,
        )

    def forward(b):
        raw_copy(b, 0).wait_recv()
        raw_copy(b, 1).wait_recv()
        col_up = pl.multiple_of(up * piece, piece)
        col_down = pl.multiple_of(down * piece, piece)
        to_up = send_buf[b, :, pl.ds(col_up, piece)].astype(jnp.float32)
        to_down = send_buf[b, :, pl.ds(col_down, piece)].astype(jnp.float32)
        from_down = relay_in[b, 0].astype(jnp.float32)
        from_up = relay_in[b, 1].astype(jnp.float32)
        sum_buf[b, 0] = jnp.concatenate(
            [to_up[:, :half] + from_down, to_up[:, half:]], 1
        ).astype(sum_buf.dtype)
        sum_buf[b, 1] = jnp.concatenate(
            [to_down[:, :half], to_down[:, half:] + from_up], 1
        ).astype(sum_buf.dtype)
        sum_copy(b, 0).start()
        sum_copy(b, 1).start()

    def block_body(b, carry):
        row = pl.multiple_of(b * BLOCK, BLOCK)
        bias = bias_ref[b]
        cs = cs_ref[pl.ds(row, BLOCK), :]
        sn = sn_ref[pl.ds(row, BLOCK), :]
        outs = []
        for h in range(heads):
            g = h // rep
            qf = q_ref[pl.ds(row, BLOCK), pl.ds(h * 128, 128)]
            qh = (qf * cs + pltpu.roll(qf, 64, 1) * sn).astype(jnp.bfloat16)
            kw = k_ref[pl.ds(row, 2 * BLOCK), pl.ds(g * 128, 128)]
            vw = v_ref[pl.ds(row, 2 * BLOCK), pl.ds(g * 128, 128)]
            kp = kp_ref[:, pl.ds(g * 128, 128)]
            vp = vp_ref[:, pl.ds(g * 128, 128)]
            keys = jnp.concatenate([kw, kp], 0)
            vals = jnp.concatenate([vw, vp], 0)
            s = lax.dot_general(
                qh, keys, (((1,), (1,)), ((), ())), preferred_element_type=jnp.float32
            ) / HEAD_WIDTH**0.5
            s = s + bias
            m = jnp.max(s, -1, keepdims=True)
            w = jnp.exp(s - m)
            p = (w / jnp.sum(w, -1, keepdims=True)).astype(jnp.bfloat16)
            outs.append(
                jnp.dot(p, vals, preferred_element_type=jnp.float32).astype(jnp.bfloat16)
            )
        att = jnp.concatenate(outs, 1)
        part = jnp.dot(att, wo_ref[...], preferred_element_type=jnp.float32)
        send_buf[b] = part.astype(jnp.bfloat16)
        raw_copy(b, 0).start()
        raw_copy(b, 1).start()

        @pl.when(b > 0)
        def _():
            forward(b - 1)

        return carry

    lax.fori_loop(0, n_blocks, block_body, 0)
    forward(n_blocks - 1)

    def wait_body(b, carry):
        for side in (0, 1):
            raw_copy(b, side).wait_send()
            sum_copy(b, side).wait_send()
            sum_copy(b, side).wait_recv()
        return carry

    lax.fori_loop(0, n_blocks, wait_body, 0)
    own = pl.multiple_of(me * piece, piece)

    def finish_body(b, carry):
        row = pl.multiple_of(b * BLOCK, BLOCK)
        total = res_ref[pl.ds(row, BLOCK), :].astype(jnp.float32)
        total = total + send_buf[b, :, pl.ds(own, piece)].astype(jnp.float32)
        for side in (0, 1):
            total = total + recv_buf[side, pl.ds(row, BLOCK), :].astype(jnp.float32)
        out_ref[pl.ds(row, BLOCK), :] = total.astype(out_ref.dtype)
        return carry

    lax.fori_loop(0, n_blocks, finish_body, 0)


def attend_and_reduce(q, cs, sn, k_pad, v_pad, k_prompt, v_prompt, bias, wo, residual, tp_count):
    rows, q_width = q.shape
    n_blocks = rows // BLOCK
    piece = residual.shape[1]
    width = wo.shape[1]
    kernel = functools.partial(
        attend_kernel,
        tp_count=tp_count,
        heads=q_width // HEAD_WIDTH,
        kv_heads=k_pad.shape[1] // HEAD_WIDTH,
        n_blocks=n_blocks,
    )
    vmem = pltpu.MemorySpace.VMEM
    return pl.pallas_call(
        kernel,
        out_shape=jax.ShapeDtypeStruct((rows, piece), jnp.bfloat16),
        in_specs=[pl.BlockSpec(memory_space=vmem)] * 10,
        out_specs=pl.BlockSpec(memory_space=vmem),
        scratch_shapes=[
            pltpu.VMEM((n_blocks, BLOCK, width), jnp.bfloat16),
            pltpu.VMEM((n_blocks, 2, BLOCK, piece // 2), jnp.bfloat16),
            pltpu.VMEM((n_blocks, 2, BLOCK, piece), jnp.bfloat16),
            pltpu.VMEM((2, rows, piece), jnp.bfloat16),
            pltpu.SemaphoreType.DMA((n_blocks * 4,)),
            pltpu.SemaphoreType.DMA((n_blocks * 4,)),
        ],
        compiler_params=pltpu.CompilerParams(
            collective_id=0, has_side_effects=True, vmem_limit_bytes=48 * 1024 * 1024
        ),
    )(q, cs, sn, k_pad, v_pad, k_prompt, v_prompt, bias, wo, residual)


def ids_kernel(wanted_ref, out_ref, landing, send_sems, recv_sems):
    me = lax.axis_index("req")
    col = lax.axis_index("tp")
    count = lax.axis_size("req")
    barrier = pltpu.get_barrier_semaphore()

    def greet(k, carry):
        peer = lax.rem(me + k, count)
        pl.semaphore_signal(
            barrier, inc=1, device_id=(peer, col), device_id_type=pl.DeviceIdType.MESH
        )
        return carry

    lax.fori_loop(1, count, greet, 0)
    pl.semaphore_wait(barrier, count - 1)

    def copy_to(k):
        dest = lax.rem(me + k, count)
        return pltpu.make_async_remote_copy(
            src_ref=wanted_ref.at[dest],
            dst_ref=landing.at[me],
            send_sem=send_sems.at[k],
            recv_sem=recv_sems.at[k],
            device_id=(dest, col),
            device_id_type=pl.DeviceIdType.MESH,
        )

    def copy_from(k):
        source = lax.rem(me + count - k, count)
        return pltpu.make_async_remote_copy(
            src_ref=wanted_ref.at[source],
            dst_ref=landing.at[source],
            send_sem=send_sems.at[k],
            recv_sem=recv_sems.at[k],
            device_id=(source, col),
            device_id_type=pl.DeviceIdType.MESH,
        )

    def send(k, carry):
        copy_to(k).start()
        return carry

    lax.fori_loop(1, count, send, 0)
    out_ref[me] = wanted_ref[me]

    def finish(k, carry):
        copy_to(k).wait_send()
        copy_from(k).wait_recv()
        source = lax.rem(me + count - k, count)
        out_ref[source] = landing[source]
        return carry

    lax.fori_loop(1, count, finish, 0)


def exchange_ids(wanted):
    count = wanted.shape[0]
    tiles = jnp.broadcast_to(wanted[:, None, None], (count, 8, 128))
    vmem = pltpu.MemorySpace.VMEM
    got = pl.pallas_call(
        ids_kernel,
        out_shape=jax.ShapeDtypeStruct((count, 8, 128), jnp.int32),
        in_specs=[pl.BlockSpec(memory_space=vmem)],
        out_specs=pl.BlockSpec(memory_space=vmem),
        scratch_shapes=[
            pltpu.VMEM((count, 8, 128), jnp.int32),
            pltpu.SemaphoreType.DMA((count,)),
            pltpu.SemaphoreType.DMA((count,)),
        ],
        compiler_params=pltpu.CompilerParams(collective_id=1, has_side_effects=True),
    )(tiles)
    return got[:, 0, 0]


def rank_sum_kernel(part_ref, out_ref, landing, send_sems, recv_sems):
    me = lax.axis_index("tp")
    row_dev = lax.axis_index("req")
    count = lax.axis_size("tp")
    barrier = pltpu.get_barrier_semaphore()
    for k in range(1, count):
        pl.semaphore_signal(
            barrier,
            inc=1,
            device_id=(row_dev, lax.rem(me + k, count)),
            device_id_type=pl.DeviceIdType.MESH,
        )
    pl.semaphore_wait(barrier, count - 1)
    copies = [
        pltpu.make_async_remote_copy(
            src_ref=part_ref,
            dst_ref=landing.at[k - 1],
            send_sem=send_sems.at[k - 1],
            recv_sem=recv_sems.at[k - 1],
            device_id=(row_dev, lax.rem(me + k, count)),
            device_id_type=pl.DeviceIdType.MESH,
        )
        for k in range(1, count)
    ]
    for copy in copies:
        copy.start()
    total = part_ref[...]
    for k, copy in enumerate(copies):
        copy.wait()
        total = total + landing[k]
    out_ref[...] = total


def rank_sum(part):
    count = lax.axis_size("tp")
    vmem = pltpu.MemorySpace.VMEM
    return pl.pallas_call(
        rank_sum_kernel,
        out_shape=jax.ShapeDtypeStruct(part.shape, part.dtype),
        in_specs=[pl.BlockSpec(memory_space=vmem)],
        out_specs=pl.BlockSpec(memory_space=vmem),
        scratch_shapes=[
            pltpu.VMEM((count - 1,) + part.shape, part.dtype),
            pltpu.SemaphoreType.DMA((count - 1,)),
            pltpu.SemaphoreType.DMA((count - 1,)),
        ],
        compiler_params=pltpu.CompilerParams(collective_id=2, has_side_effects=True),
    )(part)


def per_device(
    tokens,
    input_norm_gain,
    query_matrix,
    key_matrix,
    value_matrix,
    output_matrix,
    adapter_down_maps,
    adapter_up_maps,
    request_row_counts,
    prompt_group_per_request,
    adapter_per_request,
    adapter_table_slot,
):
    tp_count = lax.axis_size("tp")
    req_count = lax.axis_size("req")
    tp_index = lax.axis_index("tp")
    tok_rows, width = tokens.shape
    piece_width = width // tp_count
    lengths = request_row_counts[0]
    groups = prompt_group_per_request[0]
    adapters = adapter_per_request[0]
    req_slots = lengths.shape[0]
    request_hot, starts, row_info, token_positions, row_ids = layout(lengths, groups, tok_rows)
    adapters_per_part = adapter_down_maps.shape[0]
    rank_extent = adapter_down_maps.shape[2]
    slots = adapter_table_slot[adapters]
    holder = slots // adapters_per_part
    local_slot = slots % adapters_per_part
    holder_ids = jnp.arange(req_count, dtype=jnp.int32)
    holder_hot = (holder[None, :] == holder_ids[:, None]).astype(jnp.int32)
    wanted = jnp.sum(holder_hot * local_slot[None, :], 1)
    wanted_in = exchange_ids(wanted)
    table = jnp.concatenate([jnp.transpose(adapter_down_maps, (0, 2, 1)), adapter_up_maps], 1)
    maps_out = table[wanted_in]
    tokens, maps_out = lax.optimization_barrier((tokens, maps_out))
    float_tok = tokens.astype(jnp.float32)
    normalized_input = (
        float_tok
        * lax.rsqrt(jnp.mean(float_tok * float_tok, -1, keepdims=True) + 1e-06)
        * input_norm_gain
    ).astype(jnp.bfloat16)
    maps_in = lax.all_to_all(maps_out, "req", split_axis=0, concat_axis=0, tiled=True)
    down_in = maps_in[:, :rank_extent, :].reshape(req_count * rank_extent, piece_width)
    up_in = maps_in[:, rank_extent:, :].reshape(req_count * rank_extent, piece_width)
    normed_slice = lax.dynamic_slice_in_dim(
        normalized_input, tp_index * piece_width, piece_width, 1
    )
    holder_row = jnp.sum(request_hot * holder[None, :], 1)
    pick = (holder_row[:, None] == holder_ids[None, :])[:, :, None]
    wide_rank = jnp.dot(
        normed_slice, down_in.T, preferred_element_type=jnp.float32
    ).reshape(tok_rows, req_count, rank_extent)
    partial_rank = jnp.sum(jnp.where(pick, wide_rank, jnp.float32(0.0)), 1)
    partial_rank = rank_sum(partial_rank.T).T
    rank = partial_rank.astype(jnp.bfloat16)
    spread = jnp.where(pick, rank[:, None, :], jnp.zeros((), jnp.bfloat16)).reshape(
        tok_rows, req_count * rank_extent
    )
    query_delta = (
        2.0 * jnp.dot(spread, up_in, preferred_element_type=jnp.float32)
    ).astype(jnp.bfloat16)
    heads_local = query_matrix.shape[1] // HEAD_WIDTH
    kv_local = key_matrix.shape[1] // HEAD_WIDTH
    query_full = jnp.dot(
        normalized_input, query_matrix, preferred_element_type=jnp.float32
    ) + query_delta.astype(jnp.float32)
    half_dim = HEAD_WIDTH // 2
    inverse = 1000000.0 ** (-(jnp.arange(half_dim, dtype=jnp.float32) * 2.0 / HEAD_WIDTH))
    angles = token_positions[:, None] * inverse[None, :]
    cosine = jnp.cos(angles)
    sine = jnp.sin(angles)
    cos_pair = jnp.concatenate([cosine, cosine], 1)
    sin_pair = jnp.concatenate([-sine, sine], 1)
    key_complete = jnp.dot(normalized_input, key_matrix, preferred_element_type=jnp.float32)
    key_head_rows = apply_rotary(
        key_complete.reshape(tok_rows, kv_local, HEAD_WIDTH), token_positions
    ).astype(jnp.bfloat16)
    value_head_rows = (
        jnp.dot(normalized_input, value_matrix, preferred_element_type=jnp.float32)
        .astype(jnp.bfloat16)
        .reshape(tok_rows, kv_local, HEAD_WIDTH)
    )
    request_row, group_row, prompt_row, prompt_start, prompt_len = row_info
    n_blocks = tok_rows // BLOCK
    group_count = prompt_start.shape[0]
    kv_width = kv_local * HEAD_WIDTH
    key_flat = key_head_rows.reshape(tok_rows, kv_width)
    value_flat = value_head_rows.reshape(tok_rows, kv_width)
    front = jnp.zeros((BLOCK, kv_width), jnp.bfloat16)
    k_pad = jnp.concatenate([front, key_flat], 0)
    v_pad = jnp.concatenate([front, value_flat], 0)
    clamp_start = jnp.clip(prompt_start, 0, tok_rows - LMAX)
    extra = BLOCK - group_count * LMAX
    k_prompt = jnp.concatenate(
        [lax.dynamic_slice_in_dim(key_flat, clamp_start[g], LMAX, 0) for g in range(group_count)]
        + [jnp.zeros((extra, kv_width), jnp.bfloat16)],
        0,
    )
    v_prompt = jnp.concatenate(
        [lax.dynamic_slice_in_dim(value_flat, clamp_start[g], LMAX, 0) for g in range(group_count)]
        + [jnp.zeros((extra, kv_width), jnp.bfloat16)],
        0,
    )
    def windows(values, fill):
        padded = jnp.concatenate([jnp.full((BLOCK,), fill, values.dtype), values]).reshape(
            n_blocks + 1, BLOCK
        )
        return jnp.concatenate([padded[:-1], padded[1:]], 1)

    win_row = windows(row_ids, -1)
    win_req = windows(request_row, -1)
    win_grp = windows(group_row, -1)
    win_prm = windows(prompt_row, 0)
    q_row = row_ids.reshape(n_blocks, BLOCK)[:, :, None]
    q_req = request_row.reshape(n_blocks, BLOCK)[:, :, None]
    q_grp = group_row.reshape(n_blocks, BLOCK)[:, :, None]
    win_vis = (
        (win_row[:, None, :] >= 0)
        & (win_grp[:, None, :] == q_grp)
        & (win_row[:, None, :] <= q_row)
        & ((win_req[:, None, :] == q_req) | (win_prm[:, None, :] == 1))
    )
    p_row = (clamp_start[:, None] + jnp.arange(LMAX, dtype=jnp.int32)[None, :]).reshape(-1)
    p_lo = jnp.repeat(prompt_start, LMAX)
    p_hi = jnp.repeat(prompt_start + prompt_len, LMAX)
    p_grp = jnp.repeat(jnp.arange(group_count, dtype=jnp.int32), LMAX)
    p_row = jnp.concatenate([p_row, jnp.zeros((extra,), jnp.int32)])
    p_lo = jnp.concatenate([p_lo, jnp.ones((extra,), jnp.int32)])
    p_hi = jnp.concatenate([p_hi, jnp.zeros((extra,), jnp.int32)])
    p_grp = jnp.concatenate([p_grp, jnp.full((extra,), -1, jnp.int32)])
    win_first = q_row[:, :1, :] - BLOCK
    prompt_vis = (
        (p_grp[None, None, :] == q_grp)
        & (p_row[None, None, :] >= p_lo[None, None, :])
        & (p_row[None, None, :] < p_hi[None, None, :])
        & (p_row[None, None, :] < win_first)
        & (p_row[None, None, :] <= q_row)
    )
    vis = jnp.concatenate([win_vis, prompt_vis], 2)
    bias = jnp.where(vis, jnp.float32(0.0), jnp.float32(-1e30))
    residual = lax.dynamic_slice_in_dim(tokens, tp_index * piece_width, piece_width, 1)
    return attend_and_reduce(
        query_full,
        cos_pair,
        sin_pair,
        k_pad,
        v_pad,
        k_prompt,
        v_prompt,
        bias,
        output_matrix,
        residual,
        tp_count,
    )


def solution(mesh):
    return jax.shard_map(
        per_device,
        mesh=mesh,
        in_specs=(
            P("req", None),
            P(),
            P(None, "tp"),
            P(None, "tp"),
            P(None, "tp"),
            P("tp", None),
            P("req", "tp", None),
            P("req", None, "tp"),
            P("req", None),
            P("req", None),
            P("req", None),
            P(),
        ),
        out_specs=P("req", "tp"),
        check_vma=False,
    )
```

```python
import jax
import jax.numpy as jnp
import functools
from jax import lax
from jax.experimental import pallas as pl
from jax.experimental.pallas import tpu as pltpu
from jax.sharding import PartitionSpec as P

HEAD_WIDTH = 128
REQ_DEV = 32
LMAX = 40


def apply_rotary(vectors, token_positions):
    head_size = vectors.shape[-1]
    half_dim = head_size // 2
    inverse = 1000000.0 ** (-(jnp.arange(half_dim, dtype=jnp.float32) * 2.0 / head_size))
    angles = token_positions[:, None] * inverse[None, :]
    cosine = jnp.cos(angles)[:, None, :]
    sine_part = jnp.sin(angles)[:, None, :]
    first_half = vectors[..., :half_dim]
    second = vectors[..., half_dim:]
    return jnp.concatenate(
        [first_half * cosine - second * sine_part, second * cosine + first_half * sine_part], -1
    )


def layout(lengths, groups, tok_rows):
    req_slots = lengths.shape[0]
    row_ids = jnp.arange(tok_rows, dtype=jnp.int32)
    row_ends = jnp.cumsum(lengths)
    starts = row_ends - lengths
    request_row = jnp.sum((row_ids[:, None] >= row_ends[None, :]).astype(jnp.int32), 1)
    request_hot = (request_row[:, None] == jnp.arange(req_slots, dtype=jnp.int32)[None, :]).astype(
        jnp.int32
    )
    previous = jnp.concatenate([jnp.full((1,), -1, jnp.int32), groups[:-1]])
    is_prompt = (groups != previous).astype(jnp.int32)
    prompt_len = jnp.sum(
        lengths[None, :]
        * is_prompt[None, :]
        * (groups[None, :] == groups[:, None]).astype(jnp.int32),
        1,
    )
    offset_req = (1 - is_prompt) * prompt_len - starts
    group_row = jnp.sum(request_hot * groups[None, :], 1)
    prompt_row = jnp.sum(request_hot * is_prompt[None, :], 1)
    offset_row = jnp.sum(request_hot * offset_req[None, :], 1)
    token_positions = (row_ids + offset_row).astype(jnp.float32)
    group_ids = jnp.arange(3, dtype=jnp.int32)
    group_hot = (groups[None, :] == group_ids[:, None]).astype(jnp.int32)
    prompt_start = jnp.sum((starts * is_prompt)[None, :] * group_hot, 1)
    prompt_len = jnp.sum((lengths * is_prompt)[None, :] * group_hot, 1)
    rows = (request_row, group_row, prompt_row, prompt_start, prompt_len)
    return (request_hot, starts, rows, token_positions, row_ids)


BLOCK = 128


def attend_kernel(
    q_ref, cs_ref, sn_ref, k_ref, v_ref, kp_ref, vp_ref, bias_ref, wo_ref, res_ref, out_ref,
    send_buf, relay_in, sum_buf, recv_buf, send_sems, recv_sems, *, tp_count, heads, kv_heads,
    n_blocks
):
    me = lax.axis_index("tp")
    row_dev = lax.axis_index("req")
    piece = out_ref.shape[1]
    half = piece // 2
    up = lax.rem(me + 1, tp_count)
    down = lax.rem(me + tp_count - 1, tp_count)
    across = lax.rem(me + 2, tp_count)
    barrier = pltpu.get_barrier_semaphore()
    for peer in (up, down):
        pl.semaphore_signal(
            barrier, inc=1, device_id=(row_dev, peer), device_id_type=pl.DeviceIdType.MESH
        )
    pl.semaphore_wait(barrier, 2)
    rep = heads // kv_heads

    def raw_copy(b, side):
        col = pl.multiple_of(across * piece + side * half, half)
        return pltpu.make_async_remote_copy(
            src_ref=send_buf.at[b, :, pl.ds(col, half)],
            dst_ref=relay_in.at[b, side],
            send_sem=send_sems.at[b * 4 + side],
            recv_sem=recv_sems.at[b * 4 + side],
            device_id=(row_dev, up if side == 0 else down),
            device_id_type=pl.DeviceIdType.MESH,
        )

    def sum_copy(b, side):
        row = pl.multiple_of(b * BLOCK, BLOCK)
        return pltpu.make_async_remote_copy(
            src_ref=sum_buf.at[b, side],
            dst_ref=recv_buf.at[side, pl.ds(row, BLOCK)],
            send_sem=send_sems.at[b * 4 + 2 + side],
            recv_sem=recv_sems.at[b * 4 + 2 + side],
            device_id=(row_dev, up if side == 0 else down),
            device_id_type=pl.DeviceIdType.MESH,
        )

    def forward(b):
        raw_copy(b, 0).wait_recv()
        raw_copy(b, 1).wait_recv()
        col_up = pl.multiple_of(up * piece, piece)
        col_down = pl.multiple_of(down * piece, piece)
        to_up = send_buf[b, :, pl.ds(col_up, piece)].astype(jnp.float32)
        to_down = send_buf[b, :, pl.ds(col_down, piece)].astype(jnp.float32)
        from_down = relay_in[b, 0].astype(jnp.float32)
        from_up = relay_in[b, 1].astype(jnp.float32)
        sum_buf[b, 0] = jnp.concatenate(
            [to_up[:, :half] + from_down, to_up[:, half:]], 1
        ).astype(sum_buf.dtype)
        sum_buf[b, 1] = jnp.concatenate(
            [to_down[:, :half], to_down[:, half:] + from_up], 1
        ).astype(sum_buf.dtype)
        sum_copy(b, 0).start()
        sum_copy(b, 1).start()

    def block_body(b, carry):
        row = pl.multiple_of(b * BLOCK, BLOCK)
        bias = bias_ref[b]
        cs = cs_ref[pl.ds(row, BLOCK), :]
        sn = sn_ref[pl.ds(row, BLOCK), :]
        outs = []
        for h in range(heads):
            g = h // rep
            qf = q_ref[pl.ds(row, BLOCK), pl.ds(h * 128, 128)]
            qh = (qf * cs + pltpu.roll(qf, 64, 1) * sn).astype(jnp.bfloat16)
            kw = k_ref[pl.ds(row, 2 * BLOCK), pl.ds(g * 128, 128)]
            vw = v_ref[pl.ds(row, 2 * BLOCK), pl.ds(g * 128, 128)]
            kp = kp_ref[:, pl.ds(g * 128, 128)]
            vp = vp_ref[:, pl.ds(g * 128, 128)]
            keys = jnp.concatenate([kw, kp], 0)
            vals = jnp.concatenate([vw, vp], 0)
            s = lax.dot_general(
                qh, keys, (((1,), (1,)), ((), ())), preferred_element_type=jnp.float32
            ) / HEAD_WIDTH**0.5
            s = s + bias
            m = jnp.max(s, -1, keepdims=True)
            w = jnp.exp(s - m)
            p = (w / jnp.sum(w, -1, keepdims=True)).astype(jnp.bfloat16)
            outs.append(
                jnp.dot(p, vals, preferred_element_type=jnp.float32).astype(jnp.bfloat16)
            )
        att = jnp.concatenate(outs, 1)
        part = jnp.dot(att, wo_ref[...], preferred_element_type=jnp.float32)
        send_buf[b] = part.astype(jnp.bfloat16)
        raw_copy(b, 0).start()
        raw_copy(b, 1).start()

        @pl.when(b > 0)
        def _():
            forward(b - 1)

        return carry

    lax.fori_loop(0, n_blocks, block_body, 0)
    forward(n_blocks - 1)

    own = pl.multiple_of(me * piece, piece)

    def finish_body(b, carry):
        for side in (0, 1):
            raw_copy(b, side).wait_send()
            sum_copy(b, side).wait_send()
            sum_copy(b, side).wait_recv()
        row = pl.multiple_of(b * BLOCK, BLOCK)
        total = res_ref[pl.ds(row, BLOCK), :].astype(jnp.float32)
        total = total + send_buf[b, :, pl.ds(own, piece)].astype(jnp.float32)
        for side in (0, 1):
            total = total + recv_buf[side, pl.ds(row, BLOCK), :].astype(jnp.float32)
        out_ref[pl.ds(row, BLOCK), :] = total.astype(out_ref.dtype)
        return carry

    lax.fori_loop(0, n_blocks, finish_body, 0)


def attend_and_reduce(q, cs, sn, k_pad, v_pad, k_prompt, v_prompt, bias, wo, residual, tp_count):
    rows, q_width = q.shape
    n_blocks = rows // BLOCK
    piece = residual.shape[1]
    width = wo.shape[1]
    kernel = functools.partial(
        attend_kernel,
        tp_count=tp_count,
        heads=q_width // HEAD_WIDTH,
        kv_heads=k_pad.shape[1] // HEAD_WIDTH,
        n_blocks=n_blocks,
    )
    vmem = pltpu.MemorySpace.VMEM
    return pl.pallas_call(
        kernel,
        out_shape=jax.ShapeDtypeStruct((rows, piece), jnp.bfloat16),
        in_specs=[pl.BlockSpec(memory_space=vmem)] * 10,
        out_specs=pl.BlockSpec(memory_space=vmem),
        scratch_shapes=[
            pltpu.VMEM((n_blocks, BLOCK, width), jnp.bfloat16),
            pltpu.VMEM((n_blocks, 2, BLOCK, piece // 2), jnp.bfloat16),
            pltpu.VMEM((n_blocks, 2, BLOCK, piece), jnp.bfloat16),
            pltpu.VMEM((2, rows, piece), jnp.bfloat16),
            pltpu.SemaphoreType.DMA((n_blocks * 4,)),
            pltpu.SemaphoreType.DMA((n_blocks * 4,)),
        ],
        compiler_params=pltpu.CompilerParams(
            collective_id=0, has_side_effects=True, vmem_limit_bytes=48 * 1024 * 1024
        ),
    )(q, cs, sn, k_pad, v_pad, k_prompt, v_prompt, bias, wo, residual)


def ids_kernel(wanted_ref, out_ref, landing, send_sems, recv_sems):
    me = lax.axis_index("req")
    col = lax.axis_index("tp")
    count = lax.axis_size("req")
    barrier = pltpu.get_barrier_semaphore()

    def greet(k, carry):
        peer = lax.rem(me + k, count)
        pl.semaphore_signal(
            barrier, inc=1, device_id=(peer, col), device_id_type=pl.DeviceIdType.MESH
        )
        return carry

    lax.fori_loop(1, count, greet, 0)
    pl.semaphore_wait(barrier, count - 1)

    def copy_to(k):
        dest = lax.rem(me + k, count)
        return pltpu.make_async_remote_copy(
            src_ref=wanted_ref.at[dest],
            dst_ref=landing.at[me],
            send_sem=send_sems.at[k],
            recv_sem=recv_sems.at[k],
            device_id=(dest, col),
            device_id_type=pl.DeviceIdType.MESH,
        )

    def copy_from(k):
        source = lax.rem(me + count - k, count)
        return pltpu.make_async_remote_copy(
            src_ref=wanted_ref.at[source],
            dst_ref=landing.at[source],
            send_sem=send_sems.at[k],
            recv_sem=recv_sems.at[k],
            device_id=(source, col),
            device_id_type=pl.DeviceIdType.MESH,
        )

    def send(k, carry):
        copy_to(k).start()
        return carry

    lax.fori_loop(1, count, send, 0)
    out_ref[me] = wanted_ref[me]

    def finish(k, carry):
        copy_to(k).wait_send()
        copy_from(k).wait_recv()
        source = lax.rem(me + count - k, count)
        out_ref[source] = landing[source]
        return carry

    lax.fori_loop(1, count, finish, 0)


def exchange_ids(wanted):
    count = wanted.shape[0]
    tiles = jnp.broadcast_to(wanted[:, None, None], (count, 8, 128))
    vmem = pltpu.MemorySpace.VMEM
    got = pl.pallas_call(
        ids_kernel,
        out_shape=jax.ShapeDtypeStruct((count, 8, 128), jnp.int32),
        in_specs=[pl.BlockSpec(memory_space=vmem)],
        out_specs=pl.BlockSpec(memory_space=vmem),
        scratch_shapes=[
            pltpu.VMEM((count, 8, 128), jnp.int32),
            pltpu.SemaphoreType.DMA((count,)),
            pltpu.SemaphoreType.DMA((count,)),
        ],
        compiler_params=pltpu.CompilerParams(collective_id=1, has_side_effects=True),
    )(tiles)
    return got[:, 0, 0]


def per_device(
    tokens,
    input_norm_gain,
    query_matrix,
    key_matrix,
    value_matrix,
    output_matrix,
    adapter_down_maps,
    adapter_up_maps,
    request_row_counts,
    prompt_group_per_request,
    adapter_per_request,
    adapter_table_slot,
):
    tp_count = lax.axis_size("tp")
    req_count = lax.axis_size("req")
    tp_index = lax.axis_index("tp")
    tok_rows, width = tokens.shape
    piece_width = width // tp_count
    lengths = request_row_counts[0]
    groups = prompt_group_per_request[0]
    adapters = adapter_per_request[0]
    req_slots = lengths.shape[0]
    request_hot, starts, row_info, token_positions, row_ids = layout(lengths, groups, tok_rows)
    adapters_per_part = adapter_down_maps.shape[0]
    rank_extent = adapter_down_maps.shape[2]
    slots = adapter_table_slot[adapters]
    holder = slots // adapters_per_part
    local_slot = slots % adapters_per_part
    holder_ids = jnp.arange(req_count, dtype=jnp.int32)
    holder_hot = (holder[None, :] == holder_ids[:, None]).astype(jnp.int32)
    wanted = jnp.sum(holder_hot * local_slot[None, :], 1)
    wanted_in = exchange_ids(wanted)
    table = jnp.concatenate([jnp.transpose(adapter_down_maps, (0, 2, 1)), adapter_up_maps], 1)
    maps_out = table[wanted_in]
    tokens, maps_out = lax.optimization_barrier((tokens, maps_out))
    float_tok = tokens.astype(jnp.float32)
    normalized_input = (
        float_tok
        * lax.rsqrt(jnp.mean(float_tok * float_tok, -1, keepdims=True) + 1e-06)
        * input_norm_gain
    ).astype(jnp.bfloat16)
    maps_in = lax.all_to_all(maps_out, "req", split_axis=0, concat_axis=0, tiled=True)
    down_in = maps_in[:, :rank_extent, :].reshape(req_count * rank_extent, piece_width)
    up_in = maps_in[:, rank_extent:, :].reshape(req_count * rank_extent, piece_width)
    normed_slice = lax.dynamic_slice_in_dim(
        normalized_input, tp_index * piece_width, piece_width, 1
    )
    holder_row = jnp.sum(request_hot * holder[None, :], 1)
    pick = (holder_row[:, None] == holder_ids[None, :])[:, :, None]
    wide_rank = jnp.dot(
        normed_slice, down_in.T, preferred_element_type=jnp.float32
    ).reshape(tok_rows, req_count, rank_extent)
    partial_rank = jnp.sum(jnp.where(pick, wide_rank, jnp.float32(0.0)), 1)
    arrived = [
        lax.ppermute(partial_rank, "tp", [(i, (i + k) % tp_count) for i in range(tp_count)])
        for k in range(1, tp_count)
    ]
    for piece in arrived:
        partial_rank = partial_rank + piece
    rank = partial_rank.astype(jnp.bfloat16)
    spread = jnp.where(pick, rank[:, None, :], jnp.zeros((), jnp.bfloat16)).reshape(
        tok_rows, req_count * rank_extent
    )
    query_delta = (
        2.0 * jnp.dot(spread, up_in, preferred_element_type=jnp.float32)
    ).astype(jnp.bfloat16)
    heads_local = query_matrix.shape[1] // HEAD_WIDTH
    kv_local = key_matrix.shape[1] // HEAD_WIDTH
    query_full = jnp.dot(
        normalized_input, query_matrix, preferred_element_type=jnp.float32
    ) + query_delta.astype(jnp.float32)
    half_dim = HEAD_WIDTH // 2
    inverse = 1000000.0 ** (-(jnp.arange(half_dim, dtype=jnp.float32) * 2.0 / HEAD_WIDTH))
    angles = token_positions[:, None] * inverse[None, :]
    cosine = jnp.cos(angles)
    sine = jnp.sin(angles)
    cos_pair = jnp.concatenate([cosine, cosine], 1)
    sin_pair = jnp.concatenate([-sine, sine], 1)
    key_complete = jnp.dot(normalized_input, key_matrix, preferred_element_type=jnp.float32)
    key_head_rows = apply_rotary(
        key_complete.reshape(tok_rows, kv_local, HEAD_WIDTH), token_positions
    ).astype(jnp.bfloat16)
    value_head_rows = (
        jnp.dot(normalized_input, value_matrix, preferred_element_type=jnp.float32)
        .astype(jnp.bfloat16)
        .reshape(tok_rows, kv_local, HEAD_WIDTH)
    )
    request_row, group_row, prompt_row, prompt_start, prompt_len = row_info
    n_blocks = tok_rows // BLOCK
    group_count = prompt_start.shape[0]
    kv_width = kv_local * HEAD_WIDTH
    key_flat = key_head_rows.reshape(tok_rows, kv_width)
    value_flat = value_head_rows.reshape(tok_rows, kv_width)
    front = jnp.zeros((BLOCK, kv_width), jnp.bfloat16)
    k_pad = jnp.concatenate([front, key_flat], 0)
    v_pad = jnp.concatenate([front, value_flat], 0)
    clamp_start = jnp.clip(prompt_start, 0, tok_rows - LMAX)
    extra = BLOCK - group_count * LMAX
    k_prompt = jnp.concatenate(
        [lax.dynamic_slice_in_dim(key_flat, clamp_start[g], LMAX, 0) for g in range(group_count)]
        + [jnp.zeros((extra, kv_width), jnp.bfloat16)],
        0,
    )
    v_prompt = jnp.concatenate(
        [lax.dynamic_slice_in_dim(value_flat, clamp_start[g], LMAX, 0) for g in range(group_count)]
        + [jnp.zeros((extra, kv_width), jnp.bfloat16)],
        0,
    )
    def windows(values, fill):
        padded = jnp.concatenate([jnp.full((BLOCK,), fill, values.dtype), values]).reshape(
            n_blocks + 1, BLOCK
        )
        return jnp.concatenate([padded[:-1], padded[1:]], 1)

    win_row = windows(row_ids, -1)
    win_req = windows(request_row, -1)
    win_grp = windows(group_row, -1)
    win_prm = windows(prompt_row, 0)
    q_row = row_ids.reshape(n_blocks, BLOCK)[:, :, None]
    q_req = request_row.reshape(n_blocks, BLOCK)[:, :, None]
    q_grp = group_row.reshape(n_blocks, BLOCK)[:, :, None]
    win_vis = (
        (win_row[:, None, :] >= 0)
        & (win_grp[:, None, :] == q_grp)
        & (win_row[:, None, :] <= q_row)
        & ((win_req[:, None, :] == q_req) | (win_prm[:, None, :] == 1))
    )
    p_row = (clamp_start[:, None] + jnp.arange(LMAX, dtype=jnp.int32)[None, :]).reshape(-1)
    p_lo = jnp.repeat(prompt_start, LMAX)
    p_hi = jnp.repeat(prompt_start + prompt_len, LMAX)
    p_grp = jnp.repeat(jnp.arange(group_count, dtype=jnp.int32), LMAX)
    p_row = jnp.concatenate([p_row, jnp.zeros((extra,), jnp.int32)])
    p_lo = jnp.concatenate([p_lo, jnp.ones((extra,), jnp.int32)])
    p_hi = jnp.concatenate([p_hi, jnp.zeros((extra,), jnp.int32)])
    p_grp = jnp.concatenate([p_grp, jnp.full((extra,), -1, jnp.int32)])
    win_first = q_row[:, :1, :] - BLOCK
    prompt_vis = (
        (p_grp[None, None, :] == q_grp)
        & (p_row[None, None, :] >= p_lo[None, None, :])
        & (p_row[None, None, :] < p_hi[None, None, :])
        & (p_row[None, None, :] < win_first)
        & (p_row[None, None, :] <= q_row)
    )
    vis = jnp.concatenate([win_vis, prompt_vis], 2)
    bias = jnp.where(vis, jnp.float32(0.0), jnp.float32(-1e30))
    residual = lax.dynamic_slice_in_dim(tokens, tp_index * piece_width, piece_width, 1)
    return attend_and_reduce(
        query_full,
        cos_pair,
        sin_pair,
        k_pad,
        v_pad,
        k_prompt,
        v_prompt,
        bias,
        output_matrix,
        residual,
        tp_count,
    )


def solution(mesh):
    return jax.shard_map(
        per_device,
        mesh=mesh,
        in_specs=(
            P("req", None),
            P(),
            P(None, "tp"),
            P(None, "tp"),
            P(None, "tp"),
            P("tp", None),
            P("req", "tp", None),
            P("req", None, "tp"),
            P("req", None),
            P("req", None),
            P("req", None),
            P(),
        ),
        out_specs=P("req", "tp"),
        check_vma=False,
    )
```

```python
import jax
import jax.numpy as jnp
import functools
from jax import lax
from jax.experimental import pallas as pl
from jax.experimental.pallas import tpu as pltpu
from jax.sharding import PartitionSpec as P

HEAD_WIDTH = 128
REQ_DEV = 32
LMAX = 40


def apply_rotary(vectors, token_positions):
    head_size = vectors.shape[-1]
    half_dim = head_size // 2
    inverse = 1000000.0 ** (-(jnp.arange(half_dim, dtype=jnp.float32) * 2.0 / head_size))
    angles = token_positions[:, None] * inverse[None, :]
    cosine = jnp.cos(angles)[:, None, :]
    sine_part = jnp.sin(angles)[:, None, :]
    first_half = vectors[..., :half_dim]
    second = vectors[..., half_dim:]
    return jnp.concatenate(
        [first_half * cosine - second * sine_part, second * cosine + first_half * sine_part], -1
    )


def layout(lengths, groups, tok_rows):
    req_slots = lengths.shape[0]
    row_ids = jnp.arange(tok_rows, dtype=jnp.int32)
    row_ends = jnp.cumsum(lengths)
    starts = row_ends - lengths
    request_row = jnp.sum((row_ids[:, None] >= row_ends[None, :]).astype(jnp.int32), 1)
    request_hot = (request_row[:, None] == jnp.arange(req_slots, dtype=jnp.int32)[None, :]).astype(
        jnp.int32
    )
    previous = jnp.concatenate([jnp.full((1,), -1, jnp.int32), groups[:-1]])
    is_prompt = (groups != previous).astype(jnp.int32)
    prompt_len = jnp.sum(
        lengths[None, :]
        * is_prompt[None, :]
        * (groups[None, :] == groups[:, None]).astype(jnp.int32),
        1,
    )
    offset_req = (1 - is_prompt) * prompt_len - starts
    group_row = jnp.sum(request_hot * groups[None, :], 1)
    prompt_row = jnp.sum(request_hot * is_prompt[None, :], 1)
    offset_row = jnp.sum(request_hot * offset_req[None, :], 1)
    token_positions = (row_ids + offset_row).astype(jnp.float32)
    group_ids = jnp.arange(3, dtype=jnp.int32)
    group_hot = (groups[None, :] == group_ids[:, None]).astype(jnp.int32)
    prompt_start = jnp.sum((starts * is_prompt)[None, :] * group_hot, 1)
    prompt_len = jnp.sum((lengths * is_prompt)[None, :] * group_hot, 1)
    rows = (request_row, group_row, prompt_row, prompt_start, prompt_len)
    return (request_hot, starts, rows, token_positions, row_ids)


BLOCK = 64
PROMPT_ROWS = 128


def attend_kernel(
    q_ref, cs_ref, sn_ref, k_ref, v_ref, kp_ref, vp_ref, bias_ref, wo_ref, res_ref, out_ref,
    send_buf, relay_in, sum_buf, recv_buf, send_sems, recv_sems, *, tp_count, heads, kv_heads,
    n_blocks
):
    me = lax.axis_index("tp")
    row_dev = lax.axis_index("req")
    piece = out_ref.shape[1]
    half = piece // 2
    up = lax.rem(me + 1, tp_count)
    down = lax.rem(me + tp_count - 1, tp_count)
    across = lax.rem(me + 2, tp_count)
    barrier = pltpu.get_barrier_semaphore()
    for peer in (up, down):
        pl.semaphore_signal(
            barrier, inc=1, device_id=(row_dev, peer), device_id_type=pl.DeviceIdType.MESH
        )
    pl.semaphore_wait(barrier, 2)
    rep = heads // kv_heads

    def raw_copy(b, side):
        col = pl.multiple_of(across * piece + side * half, half)
        return pltpu.make_async_remote_copy(
            src_ref=send_buf.at[b, :, pl.ds(col, half)],
            dst_ref=relay_in.at[b, side],
            send_sem=send_sems.at[b * 4 + side],
            recv_sem=recv_sems.at[b * 4 + side],
            device_id=(row_dev, up if side == 0 else down),
            device_id_type=pl.DeviceIdType.MESH,
        )

    def sum_copy(b, side):
        row = pl.multiple_of(b * BLOCK, BLOCK)
        return pltpu.make_async_remote_copy(
            src_ref=sum_buf.at[b, side],
            dst_ref=recv_buf.at[side, pl.ds(row, BLOCK)],
            send_sem=send_sems.at[b * 4 + 2 + side],
            recv_sem=recv_sems.at[b * 4 + 2 + side],
            device_id=(row_dev, up if side == 0 else down),
            device_id_type=pl.DeviceIdType.MESH,
        )

    def forward(b):
        raw_copy(b, 0).wait_recv()
        raw_copy(b, 1).wait_recv()
        col_up = pl.multiple_of(up * piece, piece)
        col_down = pl.multiple_of(down * piece, piece)
        to_up = send_buf[b, :, pl.ds(col_up, piece)].astype(jnp.float32)
        to_down = send_buf[b, :, pl.ds(col_down, piece)].astype(jnp.float32)
        from_down = relay_in[b, 0].astype(jnp.float32)
        from_up = relay_in[b, 1].astype(jnp.float32)
        sum_buf[b, 0] = jnp.concatenate(
            [to_up[:, :half] + from_down, to_up[:, half:]], 1
        ).astype(sum_buf.dtype)
        sum_buf[b, 1] = jnp.concatenate(
            [to_down[:, :half], to_down[:, half:] + from_up], 1
        ).astype(sum_buf.dtype)
        sum_copy(b, 0).start()
        sum_copy(b, 1).start()

    def block_body(b, carry):
        row = pl.multiple_of(b * BLOCK, BLOCK)
        bias = bias_ref[b]
        cs = cs_ref[pl.ds(row, BLOCK), :]
        sn = sn_ref[pl.ds(row, BLOCK), :]
        outs = []
        for h in range(heads):
            g = h // rep
            qf = q_ref[pl.ds(row, BLOCK), pl.ds(h * 128, 128)]
            qh = (qf * cs + pltpu.roll(qf, 64, 1) * sn).astype(jnp.bfloat16)
            kw = k_ref[pl.ds(row, 2 * BLOCK), pl.ds(g * 128, 128)]
            vw = v_ref[pl.ds(row, 2 * BLOCK), pl.ds(g * 128, 128)]
            kp = kp_ref[:, pl.ds(g * 128, 128)]
            vp = vp_ref[:, pl.ds(g * 128, 128)]
            keys = jnp.concatenate([kw, kp], 0)
            vals = jnp.concatenate([vw, vp], 0)
            s = lax.dot_general(
                qh, keys, (((1,), (1,)), ((), ())), preferred_element_type=jnp.float32
            ) / HEAD_WIDTH**0.5
            s = s + bias
            m = jnp.max(s, -1, keepdims=True)
            w = jnp.exp(s - m)
            p = (w / jnp.sum(w, -1, keepdims=True)).astype(jnp.bfloat16)
            outs.append(
                jnp.dot(p, vals, preferred_element_type=jnp.float32).astype(jnp.bfloat16)
            )
        att = jnp.concatenate(outs, 1)
        part = jnp.dot(att, wo_ref[...], preferred_element_type=jnp.float32)
        send_buf[b] = part.astype(jnp.bfloat16)
        raw_copy(b, 0).start()
        raw_copy(b, 1).start()

        @pl.when(b > 0)
        def _():
            forward(b - 1)

        return carry

    lax.fori_loop(0, n_blocks, block_body, 0)
    forward(n_blocks - 1)

    own = pl.multiple_of(me * piece, piece)

    def finish_body(b, carry):
        for side in (0, 1):
            raw_copy(b, side).wait_send()
            sum_copy(b, side).wait_send()
            sum_copy(b, side).wait_recv()
        row = pl.multiple_of(b * BLOCK, BLOCK)
        total = res_ref[pl.ds(row, BLOCK), :].astype(jnp.float32)
        total = total + send_buf[b, :, pl.ds(own, piece)].astype(jnp.float32)
        for side in (0, 1):
            total = total + recv_buf[side, pl.ds(row, BLOCK), :].astype(jnp.float32)
        out_ref[pl.ds(row, BLOCK), :] = total.astype(out_ref.dtype)
        return carry

    lax.fori_loop(0, n_blocks, finish_body, 0)


def attend_and_reduce(q, cs, sn, k_pad, v_pad, k_prompt, v_prompt, bias, wo, residual, tp_count):
    rows, q_width = q.shape
    n_blocks = rows // BLOCK
    piece = residual.shape[1]
    width = wo.shape[1]
    kernel = functools.partial(
        attend_kernel,
        tp_count=tp_count,
        heads=q_width // HEAD_WIDTH,
        kv_heads=k_pad.shape[1] // HEAD_WIDTH,
        n_blocks=n_blocks,
    )
    vmem = pltpu.MemorySpace.VMEM
    return pl.pallas_call(
        kernel,
        out_shape=jax.ShapeDtypeStruct((rows, piece), jnp.bfloat16),
        in_specs=[pl.BlockSpec(memory_space=vmem)] * 10,
        out_specs=pl.BlockSpec(memory_space=vmem),
        scratch_shapes=[
            pltpu.VMEM((n_blocks, BLOCK, width), jnp.bfloat16),
            pltpu.VMEM((n_blocks, 2, BLOCK, piece // 2), jnp.bfloat16),
            pltpu.VMEM((n_blocks, 2, BLOCK, piece), jnp.bfloat16),
            pltpu.VMEM((2, rows, piece), jnp.bfloat16),
            pltpu.SemaphoreType.DMA((n_blocks * 4,)),
            pltpu.SemaphoreType.DMA((n_blocks * 4,)),
        ],
        compiler_params=pltpu.CompilerParams(
            collective_id=0, has_side_effects=True, vmem_limit_bytes=48 * 1024 * 1024
        ),
    )(q, cs, sn, k_pad, v_pad, k_prompt, v_prompt, bias, wo, residual)


def ids_kernel(wanted_ref, out_ref, landing, send_sems, recv_sems):
    me = lax.axis_index("req")
    col = lax.axis_index("tp")
    count = lax.axis_size("req")
    barrier = pltpu.get_barrier_semaphore()

    def greet(k, carry):
        peer = lax.rem(me + k, count)
        pl.semaphore_signal(
            barrier, inc=1, device_id=(peer, col), device_id_type=pl.DeviceIdType.MESH
        )
        return carry

    lax.fori_loop(1, count, greet, 0)
    pl.semaphore_wait(barrier, count - 1)

    def copy_to(k):
        dest = lax.rem(me + k, count)
        return pltpu.make_async_remote_copy(
            src_ref=wanted_ref.at[dest],
            dst_ref=landing.at[me],
            send_sem=send_sems.at[k],
            recv_sem=recv_sems.at[k],
            device_id=(dest, col),
            device_id_type=pl.DeviceIdType.MESH,
        )

    def copy_from(k):
        source = lax.rem(me + count - k, count)
        return pltpu.make_async_remote_copy(
            src_ref=wanted_ref.at[source],
            dst_ref=landing.at[source],
            send_sem=send_sems.at[k],
            recv_sem=recv_sems.at[k],
            device_id=(source, col),
            device_id_type=pl.DeviceIdType.MESH,
        )

    def send(k, carry):
        copy_to(k).start()
        return carry

    lax.fori_loop(1, count, send, 0)
    out_ref[me] = wanted_ref[me]

    def finish(k, carry):
        copy_to(k).wait_send()
        copy_from(k).wait_recv()
        source = lax.rem(me + count - k, count)
        out_ref[source] = landing[source]
        return carry

    lax.fori_loop(1, count, finish, 0)


def exchange_ids(wanted):
    count = wanted.shape[0]
    tiles = jnp.broadcast_to(wanted[:, None, None], (count, 8, 128))
    vmem = pltpu.MemorySpace.VMEM
    got = pl.pallas_call(
        ids_kernel,
        out_shape=jax.ShapeDtypeStruct((count, 8, 128), jnp.int32),
        in_specs=[pl.BlockSpec(memory_space=vmem)],
        out_specs=pl.BlockSpec(memory_space=vmem),
        scratch_shapes=[
            pltpu.VMEM((count, 8, 128), jnp.int32),
            pltpu.SemaphoreType.DMA((count,)),
            pltpu.SemaphoreType.DMA((count,)),
        ],
        compiler_params=pltpu.CompilerParams(collective_id=1, has_side_effects=True),
    )(tiles)
    return got[:, 0, 0]


def per_device(
    tokens,
    input_norm_gain,
    query_matrix,
    key_matrix,
    value_matrix,
    output_matrix,
    adapter_down_maps,
    adapter_up_maps,
    request_row_counts,
    prompt_group_per_request,
    adapter_per_request,
    adapter_table_slot,
):
    tp_count = lax.axis_size("tp")
    req_count = lax.axis_size("req")
    tp_index = lax.axis_index("tp")
    tok_rows, width = tokens.shape
    piece_width = width // tp_count
    lengths = request_row_counts[0]
    groups = prompt_group_per_request[0]
    adapters = adapter_per_request[0]
    req_slots = lengths.shape[0]
    request_hot, starts, row_info, token_positions, row_ids = layout(lengths, groups, tok_rows)
    adapters_per_part = adapter_down_maps.shape[0]
    rank_extent = adapter_down_maps.shape[2]
    slots = adapter_table_slot[adapters]
    holder = slots // adapters_per_part
    local_slot = slots % adapters_per_part
    holder_ids = jnp.arange(req_count, dtype=jnp.int32)
    holder_hot = (holder[None, :] == holder_ids[:, None]).astype(jnp.int32)
    wanted = jnp.sum(holder_hot * local_slot[None, :], 1)
    wanted_in = exchange_ids(wanted)
    table = jnp.concatenate([jnp.transpose(adapter_down_maps, (0, 2, 1)), adapter_up_maps], 1)
    maps_out = table[wanted_in]
    tokens, maps_out = lax.optimization_barrier((tokens, maps_out))
    float_tok = tokens.astype(jnp.float32)
    normalized_input = (
        float_tok
        * lax.rsqrt(jnp.mean(float_tok * float_tok, -1, keepdims=True) + 1e-06)
        * input_norm_gain
    ).astype(jnp.bfloat16)
    maps_in = lax.all_to_all(maps_out, "req", split_axis=0, concat_axis=0, tiled=True)
    down_in = maps_in[:, :rank_extent, :].reshape(req_count * rank_extent, piece_width)
    up_in = maps_in[:, rank_extent:, :].reshape(req_count * rank_extent, piece_width)
    normed_slice = lax.dynamic_slice_in_dim(
        normalized_input, tp_index * piece_width, piece_width, 1
    )
    holder_row = jnp.sum(request_hot * holder[None, :], 1)
    pick = (holder_row[:, None] == holder_ids[None, :])[:, :, None]
    wide_rank = jnp.dot(
        normed_slice, down_in.T, preferred_element_type=jnp.float32
    ).reshape(tok_rows, req_count, rank_extent)
    partial_rank = jnp.sum(jnp.where(pick, wide_rank, jnp.float32(0.0)), 1)
    arrived = [
        lax.ppermute(partial_rank, "tp", [(i, (i + k) % tp_count) for i in range(tp_count)])
        for k in range(1, tp_count)
    ]
    for piece in arrived:
        partial_rank = partial_rank + piece
    rank = partial_rank.astype(jnp.bfloat16)
    spread = jnp.where(pick, rank[:, None, :], jnp.zeros((), jnp.bfloat16)).reshape(
        tok_rows, req_count * rank_extent
    )
    query_delta = (
        2.0 * jnp.dot(spread, up_in, preferred_element_type=jnp.float32)
    ).astype(jnp.bfloat16)
    heads_local = query_matrix.shape[1] // HEAD_WIDTH
    kv_local = key_matrix.shape[1] // HEAD_WIDTH
    query_full = jnp.dot(
        normalized_input, query_matrix, preferred_element_type=jnp.float32
    ) + query_delta.astype(jnp.float32)
    half_dim = HEAD_WIDTH // 2
    inverse = 1000000.0 ** (-(jnp.arange(half_dim, dtype=jnp.float32) * 2.0 / HEAD_WIDTH))
    angles = token_positions[:, None] * inverse[None, :]
    cosine = jnp.cos(angles)
    sine = jnp.sin(angles)
    cos_pair = jnp.concatenate([cosine, cosine], 1)
    sin_pair = jnp.concatenate([-sine, sine], 1)
    key_complete = jnp.dot(normalized_input, key_matrix, preferred_element_type=jnp.float32)
    key_head_rows = apply_rotary(
        key_complete.reshape(tok_rows, kv_local, HEAD_WIDTH), token_positions
    ).astype(jnp.bfloat16)
    value_head_rows = (
        jnp.dot(normalized_input, value_matrix, preferred_element_type=jnp.float32)
        .astype(jnp.bfloat16)
        .reshape(tok_rows, kv_local, HEAD_WIDTH)
    )
    request_row, group_row, prompt_row, prompt_start, prompt_len = row_info
    n_blocks = tok_rows // BLOCK
    group_count = prompt_start.shape[0]
    kv_width = kv_local * HEAD_WIDTH
    key_flat = key_head_rows.reshape(tok_rows, kv_width)
    value_flat = value_head_rows.reshape(tok_rows, kv_width)
    front = jnp.zeros((BLOCK, kv_width), jnp.bfloat16)
    k_pad = jnp.concatenate([front, key_flat], 0)
    v_pad = jnp.concatenate([front, value_flat], 0)
    clamp_start = jnp.clip(prompt_start, 0, tok_rows - LMAX)
    extra = PROMPT_ROWS - group_count * LMAX
    k_prompt = jnp.concatenate(
        [lax.dynamic_slice_in_dim(key_flat, clamp_start[g], LMAX, 0) for g in range(group_count)]
        + [jnp.zeros((extra, kv_width), jnp.bfloat16)],
        0,
    )
    v_prompt = jnp.concatenate(
        [lax.dynamic_slice_in_dim(value_flat, clamp_start[g], LMAX, 0) for g in range(group_count)]
        + [jnp.zeros((extra, kv_width), jnp.bfloat16)],
        0,
    )
    def windows(values, fill):
        padded = jnp.concatenate([jnp.full((BLOCK,), fill, values.dtype), values]).reshape(
            n_blocks + 1, BLOCK
        )
        return jnp.concatenate([padded[:-1], padded[1:]], 1)

    win_row = windows(row_ids, -1)
    win_req = windows(request_row, -1)
    win_grp = windows(group_row, -1)
    win_prm = windows(prompt_row, 0)
    q_row = row_ids.reshape(n_blocks, BLOCK)[:, :, None]
    q_req = request_row.reshape(n_blocks, BLOCK)[:, :, None]
    q_grp = group_row.reshape(n_blocks, BLOCK)[:, :, None]
    win_vis = (
        (win_row[:, None, :] >= 0)
        & (win_grp[:, None, :] == q_grp)
        & (win_row[:, None, :] <= q_row)
        & ((win_req[:, None, :] == q_req) | (win_prm[:, None, :] == 1))
    )
    p_row = (clamp_start[:, None] + jnp.arange(LMAX, dtype=jnp.int32)[None, :]).reshape(-1)
    p_lo = jnp.repeat(prompt_start, LMAX)
    p_hi = jnp.repeat(prompt_start + prompt_len, LMAX)
    p_grp = jnp.repeat(jnp.arange(group_count, dtype=jnp.int32), LMAX)
    p_row = jnp.concatenate([p_row, jnp.zeros((extra,), jnp.int32)])
    p_lo = jnp.concatenate([p_lo, jnp.ones((extra,), jnp.int32)])
    p_hi = jnp.concatenate([p_hi, jnp.zeros((extra,), jnp.int32)])
    p_grp = jnp.concatenate([p_grp, jnp.full((extra,), -1, jnp.int32)])
    win_first = q_row[:, :1, :] - BLOCK
    prompt_vis = (
        (p_grp[None, None, :] == q_grp)
        & (p_row[None, None, :] >= p_lo[None, None, :])
        & (p_row[None, None, :] < p_hi[None, None, :])
        & (p_row[None, None, :] < win_first)
        & (p_row[None, None, :] <= q_row)
    )
    vis = jnp.concatenate([win_vis, prompt_vis], 2)
    bias = jnp.where(vis, jnp.float32(0.0), jnp.float32(-1e30))
    residual = lax.dynamic_slice_in_dim(tokens, tp_index * piece_width, piece_width, 1)
    return attend_and_reduce(
        query_full,
        cos_pair,
        sin_pair,
        k_pad,
        v_pad,
        k_prompt,
        v_prompt,
        bias,
        output_matrix,
        residual,
        tp_count,
    )


def solution(mesh):
    return jax.shard_map(
        per_device,
        mesh=mesh,
        in_specs=(
            P("req", None),
            P(),
            P(None, "tp"),
            P(None, "tp"),
            P(None, "tp"),
            P("tp", None),
            P("req", "tp", None),
            P("req", None, "tp"),
            P("req", None),
            P("req", None),
            P("req", None),
            P(),
        ),
        out_specs=P("req", "tp"),
        check_vma=False,
    )
```

```python
import jax
import jax.numpy as jnp
import functools
from jax import lax
from jax.experimental import pallas as pl
from jax.experimental.pallas import tpu as pltpu
from jax.sharding import PartitionSpec as P

HEAD_WIDTH = 128
REQ_DEV = 32
LMAX = 40


def apply_rotary(vectors, token_positions):
    head_size = vectors.shape[-1]
    half_dim = head_size // 2
    inverse = 1000000.0 ** (-(jnp.arange(half_dim, dtype=jnp.float32) * 2.0 / head_size))
    angles = token_positions[:, None] * inverse[None, :]
    cosine = jnp.cos(angles)[:, None, :]
    sine_part = jnp.sin(angles)[:, None, :]
    first_half = vectors[..., :half_dim]
    second = vectors[..., half_dim:]
    return jnp.concatenate(
        [first_half * cosine - second * sine_part, second * cosine + first_half * sine_part], -1
    )


def layout(lengths, groups, tok_rows):
    req_slots = lengths.shape[0]
    row_ids = jnp.arange(tok_rows, dtype=jnp.int32)
    row_ends = jnp.cumsum(lengths)
    starts = row_ends - lengths
    request_row = jnp.sum((row_ids[:, None] >= row_ends[None, :]).astype(jnp.int32), 1)
    request_hot = (request_row[:, None] == jnp.arange(req_slots, dtype=jnp.int32)[None, :]).astype(
        jnp.int32
    )
    previous = jnp.concatenate([jnp.full((1,), -1, jnp.int32), groups[:-1]])
    is_prompt = (groups != previous).astype(jnp.int32)
    prompt_len = jnp.sum(
        lengths[None, :]
        * is_prompt[None, :]
        * (groups[None, :] == groups[:, None]).astype(jnp.int32),
        1,
    )
    offset_req = (1 - is_prompt) * prompt_len - starts
    group_row = jnp.sum(request_hot * groups[None, :], 1)
    prompt_row = jnp.sum(request_hot * is_prompt[None, :], 1)
    offset_row = jnp.sum(request_hot * offset_req[None, :], 1)
    token_positions = (row_ids + offset_row).astype(jnp.float32)
    group_ids = jnp.arange(3, dtype=jnp.int32)
    group_hot = (groups[None, :] == group_ids[:, None]).astype(jnp.int32)
    prompt_start = jnp.sum((starts * is_prompt)[None, :] * group_hot, 1)
    prompt_len = jnp.sum((lengths * is_prompt)[None, :] * group_hot, 1)
    rows = (request_row, group_row, prompt_row, prompt_start, prompt_len)
    return (request_hot, starts, rows, token_positions, row_ids)


BLOCK = 256
PROMPT_ROWS = 128


def attend_kernel(
    q_ref, cs_ref, sn_ref, k_ref, v_ref, kp_ref, vp_ref, bias_ref, wo_ref, res_ref, out_ref,
    send_buf, relay_in, sum_buf, recv_buf, send_sems, recv_sems, *, tp_count, heads, kv_heads,
    n_blocks
):
    me = lax.axis_index("tp")
    row_dev = lax.axis_index("req")
    piece = out_ref.shape[1]
    half = piece // 2
    up = lax.rem(me + 1, tp_count)
    down = lax.rem(me + tp_count - 1, tp_count)
    across = lax.rem(me + 2, tp_count)
    barrier = pltpu.get_barrier_semaphore()
    for peer in (up, down):
        pl.semaphore_signal(
            barrier, inc=1, device_id=(row_dev, peer), device_id_type=pl.DeviceIdType.MESH
        )
    pl.semaphore_wait(barrier, 2)
    rep = heads // kv_heads

    def raw_copy(b, side):
        col = pl.multiple_of(across * piece + side * half, half)
        return pltpu.make_async_remote_copy(
            src_ref=send_buf.at[b, :, pl.ds(col, half)],
            dst_ref=relay_in.at[b, side],
            send_sem=send_sems.at[b * 4 + side],
            recv_sem=recv_sems.at[b * 4 + side],
            device_id=(row_dev, up if side == 0 else down),
            device_id_type=pl.DeviceIdType.MESH,
        )

    def sum_copy(b, side):
        row = pl.multiple_of(b * BLOCK, BLOCK)
        return pltpu.make_async_remote_copy(
            src_ref=sum_buf.at[b, side],
            dst_ref=recv_buf.at[side, pl.ds(row, BLOCK)],
            send_sem=send_sems.at[b * 4 + 2 + side],
            recv_sem=recv_sems.at[b * 4 + 2 + side],
            device_id=(row_dev, up if side == 0 else down),
            device_id_type=pl.DeviceIdType.MESH,
        )

    def forward(b):
        raw_copy(b, 0).wait_recv()
        raw_copy(b, 1).wait_recv()
        col_up = pl.multiple_of(up * piece, piece)
        col_down = pl.multiple_of(down * piece, piece)
        to_up = send_buf[b, :, pl.ds(col_up, piece)].astype(jnp.float32)
        to_down = send_buf[b, :, pl.ds(col_down, piece)].astype(jnp.float32)
        from_down = relay_in[b, 0].astype(jnp.float32)
        from_up = relay_in[b, 1].astype(jnp.float32)
        sum_buf[b, 0] = jnp.concatenate(
            [to_up[:, :half] + from_down, to_up[:, half:]], 1
        ).astype(sum_buf.dtype)
        sum_buf[b, 1] = jnp.concatenate(
            [to_down[:, :half], to_down[:, half:] + from_up], 1
        ).astype(sum_buf.dtype)
        sum_copy(b, 0).start()
        sum_copy(b, 1).start()

    def block_body(b, carry):
        row = pl.multiple_of(b * BLOCK, BLOCK)
        bias = bias_ref[b]
        cs = cs_ref[pl.ds(row, BLOCK), :]
        sn = sn_ref[pl.ds(row, BLOCK), :]
        outs = []
        for h in range(heads):
            g = h // rep
            qf = q_ref[pl.ds(row, BLOCK), pl.ds(h * 128, 128)]
            qh = (qf * cs + pltpu.roll(qf, 64, 1) * sn).astype(jnp.bfloat16)
            kw = k_ref[pl.ds(row, 2 * BLOCK), pl.ds(g * 128, 128)]
            vw = v_ref[pl.ds(row, 2 * BLOCK), pl.ds(g * 128, 128)]
            kp = kp_ref[:, pl.ds(g * 128, 128)]
            vp = vp_ref[:, pl.ds(g * 128, 128)]
            keys = jnp.concatenate([kw, kp], 0)
            vals = jnp.concatenate([vw, vp], 0)
            s = lax.dot_general(
                qh, keys, (((1,), (1,)), ((), ())), preferred_element_type=jnp.float32
            ) / HEAD_WIDTH**0.5
            s = s + bias
            m = jnp.max(s, -1, keepdims=True)
            w = jnp.exp(s - m)
            p = (w / jnp.sum(w, -1, keepdims=True)).astype(jnp.bfloat16)
            outs.append(
                jnp.dot(p, vals, preferred_element_type=jnp.float32).astype(jnp.bfloat16)
            )
        att = jnp.concatenate(outs, 1)
        part = jnp.dot(att, wo_ref[...], preferred_element_type=jnp.float32)
        send_buf[b] = part.astype(jnp.bfloat16)
        raw_copy(b, 0).start()
        raw_copy(b, 1).start()

        @pl.when(b > 0)
        def _():
            forward(b - 1)

        return carry

    lax.fori_loop(0, n_blocks, block_body, 0)
    forward(n_blocks - 1)

    own = pl.multiple_of(me * piece, piece)

    def finish_body(b, carry):
        for side in (0, 1):
            raw_copy(b, side).wait_send()
            sum_copy(b, side).wait_send()
            sum_copy(b, side).wait_recv()
        row = pl.multiple_of(b * BLOCK, BLOCK)
        total = res_ref[pl.ds(row, BLOCK), :].astype(jnp.float32)
        total = total + send_buf[b, :, pl.ds(own, piece)].astype(jnp.float32)
        for side in (0, 1):
            total = total + recv_buf[side, pl.ds(row, BLOCK), :].astype(jnp.float32)
        out_ref[pl.ds(row, BLOCK), :] = total.astype(out_ref.dtype)
        return carry

    lax.fori_loop(0, n_blocks, finish_body, 0)


def attend_and_reduce(q, cs, sn, k_pad, v_pad, k_prompt, v_prompt, bias, wo, residual, tp_count):
    rows, q_width = q.shape
    n_blocks = rows // BLOCK
    piece = residual.shape[1]
    width = wo.shape[1]
    kernel = functools.partial(
        attend_kernel,
        tp_count=tp_count,
        heads=q_width // HEAD_WIDTH,
        kv_heads=k_pad.shape[1] // HEAD_WIDTH,
        n_blocks=n_blocks,
    )
    vmem = pltpu.MemorySpace.VMEM
    return pl.pallas_call(
        kernel,
        out_shape=jax.ShapeDtypeStruct((rows, piece), jnp.bfloat16),
        in_specs=[pl.BlockSpec(memory_space=vmem)] * 10,
        out_specs=pl.BlockSpec(memory_space=vmem),
        scratch_shapes=[
            pltpu.VMEM((n_blocks, BLOCK, width), jnp.bfloat16),
            pltpu.VMEM((n_blocks, 2, BLOCK, piece // 2), jnp.bfloat16),
            pltpu.VMEM((n_blocks, 2, BLOCK, piece), jnp.bfloat16),
            pltpu.VMEM((2, rows, piece), jnp.bfloat16),
            pltpu.SemaphoreType.DMA((n_blocks * 4,)),
            pltpu.SemaphoreType.DMA((n_blocks * 4,)),
        ],
        compiler_params=pltpu.CompilerParams(
            collective_id=0, has_side_effects=True, vmem_limit_bytes=48 * 1024 * 1024
        ),
    )(q, cs, sn, k_pad, v_pad, k_prompt, v_prompt, bias, wo, residual)


def ids_kernel(wanted_ref, out_ref, landing, send_sems, recv_sems):
    me = lax.axis_index("req")
    col = lax.axis_index("tp")
    count = lax.axis_size("req")
    barrier = pltpu.get_barrier_semaphore()

    def greet(k, carry):
        peer = lax.rem(me + k, count)
        pl.semaphore_signal(
            barrier, inc=1, device_id=(peer, col), device_id_type=pl.DeviceIdType.MESH
        )
        return carry

    lax.fori_loop(1, count, greet, 0)
    pl.semaphore_wait(barrier, count - 1)

    def copy_to(k):
        dest = lax.rem(me + k, count)
        return pltpu.make_async_remote_copy(
            src_ref=wanted_ref.at[dest],
            dst_ref=landing.at[me],
            send_sem=send_sems.at[k],
            recv_sem=recv_sems.at[k],
            device_id=(dest, col),
            device_id_type=pl.DeviceIdType.MESH,
        )

    def copy_from(k):
        source = lax.rem(me + count - k, count)
        return pltpu.make_async_remote_copy(
            src_ref=wanted_ref.at[source],
            dst_ref=landing.at[source],
            send_sem=send_sems.at[k],
            recv_sem=recv_sems.at[k],
            device_id=(source, col),
            device_id_type=pl.DeviceIdType.MESH,
        )

    def send(k, carry):
        copy_to(k).start()
        return carry

    lax.fori_loop(1, count, send, 0)
    out_ref[me] = wanted_ref[me]

    def finish(k, carry):
        copy_to(k).wait_send()
        copy_from(k).wait_recv()
        source = lax.rem(me + count - k, count)
        out_ref[source] = landing[source]
        return carry

    lax.fori_loop(1, count, finish, 0)


def exchange_ids(wanted):
    count = wanted.shape[0]
    tiles = jnp.broadcast_to(wanted[:, None, None], (count, 8, 128))
    vmem = pltpu.MemorySpace.VMEM
    got = pl.pallas_call(
        ids_kernel,
        out_shape=jax.ShapeDtypeStruct((count, 8, 128), jnp.int32),
        in_specs=[pl.BlockSpec(memory_space=vmem)],
        out_specs=pl.BlockSpec(memory_space=vmem),
        scratch_shapes=[
            pltpu.VMEM((count, 8, 128), jnp.int32),
            pltpu.SemaphoreType.DMA((count,)),
            pltpu.SemaphoreType.DMA((count,)),
        ],
        compiler_params=pltpu.CompilerParams(collective_id=1, has_side_effects=True),
    )(tiles)
    return got[:, 0, 0]


def per_device(
    tokens,
    input_norm_gain,
    query_matrix,
    key_matrix,
    value_matrix,
    output_matrix,
    adapter_down_maps,
    adapter_up_maps,
    request_row_counts,
    prompt_group_per_request,
    adapter_per_request,
    adapter_table_slot,
):
    tp_count = lax.axis_size("tp")
    req_count = lax.axis_size("req")
    tp_index = lax.axis_index("tp")
    tok_rows, width = tokens.shape
    piece_width = width // tp_count
    lengths = request_row_counts[0]
    groups = prompt_group_per_request[0]
    adapters = adapter_per_request[0]
    req_slots = lengths.shape[0]
    request_hot, starts, row_info, token_positions, row_ids = layout(lengths, groups, tok_rows)
    adapters_per_part = adapter_down_maps.shape[0]
    rank_extent = adapter_down_maps.shape[2]
    slots = adapter_table_slot[adapters]
    holder = slots // adapters_per_part
    local_slot = slots % adapters_per_part
    holder_ids = jnp.arange(req_count, dtype=jnp.int32)
    holder_hot = (holder[None, :] == holder_ids[:, None]).astype(jnp.int32)
    wanted = jnp.sum(holder_hot * local_slot[None, :], 1)
    wanted_in = exchange_ids(wanted)
    table = jnp.concatenate([jnp.transpose(adapter_down_maps, (0, 2, 1)), adapter_up_maps], 1)
    maps_out = table[wanted_in]
    tokens, maps_out = lax.optimization_barrier((tokens, maps_out))
    float_tok = tokens.astype(jnp.float32)
    normalized_input = (
        float_tok
        * lax.rsqrt(jnp.mean(float_tok * float_tok, -1, keepdims=True) + 1e-06)
        * input_norm_gain
    ).astype(jnp.bfloat16)
    maps_in = lax.all_to_all(maps_out, "req", split_axis=0, concat_axis=0, tiled=True)
    down_in = maps_in[:, :rank_extent, :].reshape(req_count * rank_extent, piece_width)
    up_in = maps_in[:, rank_extent:, :].reshape(req_count * rank_extent, piece_width)
    normed_slice = lax.dynamic_slice_in_dim(
        normalized_input, tp_index * piece_width, piece_width, 1
    )
    holder_row = jnp.sum(request_hot * holder[None, :], 1)
    pick = (holder_row[:, None] == holder_ids[None, :])[:, :, None]
    wide_rank = jnp.dot(
        normed_slice, down_in.T, preferred_element_type=jnp.float32
    ).reshape(tok_rows, req_count, rank_extent)
    partial_rank = jnp.sum(jnp.where(pick, wide_rank, jnp.float32(0.0)), 1)
    arrived = [
        lax.ppermute(partial_rank, "tp", [(i, (i + k) % tp_count) for i in range(tp_count)])
        for k in range(1, tp_count)
    ]
    for piece in arrived:
        partial_rank = partial_rank + piece
    rank = partial_rank.astype(jnp.bfloat16)
    spread = jnp.where(pick, rank[:, None, :], jnp.zeros((), jnp.bfloat16)).reshape(
        tok_rows, req_count * rank_extent
    )
    query_delta = (
        2.0 * jnp.dot(spread, up_in, preferred_element_type=jnp.float32)
    ).astype(jnp.bfloat16)
    heads_local = query_matrix.shape[1] // HEAD_WIDTH
    kv_local = key_matrix.shape[1] // HEAD_WIDTH
    query_full = jnp.dot(
        normalized_input, query_matrix, preferred_element_type=jnp.float32
    ) + query_delta.astype(jnp.float32)
    half_dim = HEAD_WIDTH // 2
    inverse = 1000000.0 ** (-(jnp.arange(half_dim, dtype=jnp.float32) * 2.0 / HEAD_WIDTH))
    angles = token_positions[:, None] * inverse[None, :]
    cosine = jnp.cos(angles)
    sine = jnp.sin(angles)
    cos_pair = jnp.concatenate([cosine, cosine], 1)
    sin_pair = jnp.concatenate([-sine, sine], 1)
    key_complete = jnp.dot(normalized_input, key_matrix, preferred_element_type=jnp.float32)
    key_head_rows = apply_rotary(
        key_complete.reshape(tok_rows, kv_local, HEAD_WIDTH), token_positions
    ).astype(jnp.bfloat16)
    value_head_rows = (
        jnp.dot(normalized_input, value_matrix, preferred_element_type=jnp.float32)
        .astype(jnp.bfloat16)
        .reshape(tok_rows, kv_local, HEAD_WIDTH)
    )
    request_row, group_row, prompt_row, prompt_start, prompt_len = row_info
    n_blocks = tok_rows // BLOCK
    group_count = prompt_start.shape[0]
    kv_width = kv_local * HEAD_WIDTH
    key_flat = key_head_rows.reshape(tok_rows, kv_width)
    value_flat = value_head_rows.reshape(tok_rows, kv_width)
    front = jnp.zeros((BLOCK, kv_width), jnp.bfloat16)
    k_pad = jnp.concatenate([front, key_flat], 0)
    v_pad = jnp.concatenate([front, value_flat], 0)
    clamp_start = jnp.clip(prompt_start, 0, tok_rows - LMAX)
    extra = PROMPT_ROWS - group_count * LMAX
    k_prompt = jnp.concatenate(
        [lax.dynamic_slice_in_dim(key_flat, clamp_start[g], LMAX, 0) for g in range(group_count)]
        + [jnp.zeros((extra, kv_width), jnp.bfloat16)],
        0,
    )
    v_prompt = jnp.concatenate(
        [lax.dynamic_slice_in_dim(value_flat, clamp_start[g], LMAX, 0) for g in range(group_count)]
        + [jnp.zeros((extra, kv_width), jnp.bfloat16)],
        0,
    )
    def windows(values, fill):
        padded = jnp.concatenate([jnp.full((BLOCK,), fill, values.dtype), values]).reshape(
            n_blocks + 1, BLOCK
        )
        return jnp.concatenate([padded[:-1], padded[1:]], 1)

    win_row = windows(row_ids, -1)
    win_req = windows(request_row, -1)
    win_grp = windows(group_row, -1)
    win_prm = windows(prompt_row, 0)
    q_row = row_ids.reshape(n_blocks, BLOCK)[:, :, None]
    q_req = request_row.reshape(n_blocks, BLOCK)[:, :, None]
    q_grp = group_row.reshape(n_blocks, BLOCK)[:, :, None]
    win_vis = (
        (win_row[:, None, :] >= 0)
        & (win_grp[:, None, :] == q_grp)
        & (win_row[:, None, :] <= q_row)
        & ((win_req[:, None, :] == q_req) | (win_prm[:, None, :] == 1))
    )
    p_row = (clamp_start[:, None] + jnp.arange(LMAX, dtype=jnp.int32)[None, :]).reshape(-1)
    p_lo = jnp.repeat(prompt_start, LMAX)
    p_hi = jnp.repeat(prompt_start + prompt_len, LMAX)
    p_grp = jnp.repeat(jnp.arange(group_count, dtype=jnp.int32), LMAX)
    p_row = jnp.concatenate([p_row, jnp.zeros((extra,), jnp.int32)])
    p_lo = jnp.concatenate([p_lo, jnp.ones((extra,), jnp.int32)])
    p_hi = jnp.concatenate([p_hi, jnp.zeros((extra,), jnp.int32)])
    p_grp = jnp.concatenate([p_grp, jnp.full((extra,), -1, jnp.int32)])
    win_first = q_row[:, :1, :] - BLOCK
    prompt_vis = (
        (p_grp[None, None, :] == q_grp)
        & (p_row[None, None, :] >= p_lo[None, None, :])
        & (p_row[None, None, :] < p_hi[None, None, :])
        & (p_row[None, None, :] < win_first)
        & (p_row[None, None, :] <= q_row)
    )
    vis = jnp.concatenate([win_vis, prompt_vis], 2)
    bias = jnp.where(vis, jnp.float32(0.0), jnp.float32(-1e30))
    residual = lax.dynamic_slice_in_dim(tokens, tp_index * piece_width, piece_width, 1)
    return attend_and_reduce(
        query_full,
        cos_pair,
        sin_pair,
        k_pad,
        v_pad,
        k_prompt,
        v_prompt,
        bias,
        output_matrix,
        residual,
        tp_count,
    )


def solution(mesh):
    return jax.shard_map(
        per_device,
        mesh=mesh,
        in_specs=(
            P("req", None),
            P(),
            P(None, "tp"),
            P(None, "tp"),
            P(None, "tp"),
            P("tp", None),
            P("req", "tp", None),
            P("req", None, "tp"),
            P("req", None),
            P("req", None),
            P("req", None),
            P(),
        ),
        out_specs=P("req", "tp"),
        check_vma=False,
    )
```

```python
import jax
import jax.numpy as jnp
import functools
from jax import lax
from jax.experimental import pallas as pl
from jax.experimental.pallas import tpu as pltpu
from jax.sharding import PartitionSpec as P

HEAD_WIDTH = 128
REQ_DEV = 32
LMAX = 40


def apply_rotary(vectors, token_positions):
    head_size = vectors.shape[-1]
    half_dim = head_size // 2
    inverse = 1000000.0 ** (-(jnp.arange(half_dim, dtype=jnp.float32) * 2.0 / head_size))
    angles = token_positions[:, None] * inverse[None, :]
    cosine = jnp.cos(angles)[:, None, :]
    sine_part = jnp.sin(angles)[:, None, :]
    first_half = vectors[..., :half_dim]
    second = vectors[..., half_dim:]
    return jnp.concatenate(
        [first_half * cosine - second * sine_part, second * cosine + first_half * sine_part], -1
    )


def layout(lengths, groups, tok_rows):
    req_slots = lengths.shape[0]
    row_ids = jnp.arange(tok_rows, dtype=jnp.int32)
    row_ends = jnp.cumsum(lengths)
    starts = row_ends - lengths
    request_row = jnp.sum((row_ids[:, None] >= row_ends[None, :]).astype(jnp.int32), 1)
    request_hot = (request_row[:, None] == jnp.arange(req_slots, dtype=jnp.int32)[None, :]).astype(
        jnp.int32
    )
    previous = jnp.concatenate([jnp.full((1,), -1, jnp.int32), groups[:-1]])
    is_prompt = (groups != previous).astype(jnp.int32)
    prompt_len = jnp.sum(
        lengths[None, :]
        * is_prompt[None, :]
        * (groups[None, :] == groups[:, None]).astype(jnp.int32),
        1,
    )
    offset_req = (1 - is_prompt) * prompt_len - starts
    group_row = jnp.sum(request_hot * groups[None, :], 1)
    prompt_row = jnp.sum(request_hot * is_prompt[None, :], 1)
    offset_row = jnp.sum(request_hot * offset_req[None, :], 1)
    token_positions = (row_ids + offset_row).astype(jnp.float32)
    group_ids = jnp.arange(3, dtype=jnp.int32)
    group_hot = (groups[None, :] == group_ids[:, None]).astype(jnp.int32)
    prompt_start = jnp.sum((starts * is_prompt)[None, :] * group_hot, 1)
    prompt_len = jnp.sum((lengths * is_prompt)[None, :] * group_hot, 1)
    rows = (request_row, group_row, prompt_row, prompt_start, prompt_len)
    return (request_hot, starts, rows, token_positions, row_ids)


BLOCK = 128


def attend_kernel(
    q_ref, cs_ref, sn_ref, k_ref, v_ref, kp_ref, vp_ref, bias_ref, wo_ref, res_ref, out_ref,
    send_buf, relay_in, sum_buf, recv_buf, send_sems, recv_sems, *, tp_count, heads, kv_heads,
    n_blocks
):
    me = lax.axis_index("tp")
    row_dev = lax.axis_index("req")
    piece = out_ref.shape[1]
    half = piece // 2
    up = lax.rem(me + 1, tp_count)
    down = lax.rem(me + tp_count - 1, tp_count)
    across = lax.rem(me + 2, tp_count)
    barrier = pltpu.get_barrier_semaphore()
    for peer in (up, down):
        pl.semaphore_signal(
            barrier, inc=1, device_id=(row_dev, peer), device_id_type=pl.DeviceIdType.MESH
        )
    pl.semaphore_wait(barrier, 2)
    rep = heads // kv_heads

    def raw_copy(b, side):
        col = pl.multiple_of(across * piece + side * half, half)
        return pltpu.make_async_remote_copy(
            src_ref=send_buf.at[b, :, pl.ds(col, half)],
            dst_ref=relay_in.at[b, side],
            send_sem=send_sems.at[b * 4 + side],
            recv_sem=recv_sems.at[b * 4 + side],
            device_id=(row_dev, up if side == 0 else down),
            device_id_type=pl.DeviceIdType.MESH,
        )

    def sum_copy(b, side):
        row = pl.multiple_of(b * BLOCK, BLOCK)
        return pltpu.make_async_remote_copy(
            src_ref=sum_buf.at[b, side],
            dst_ref=recv_buf.at[side, pl.ds(row, BLOCK)],
            send_sem=send_sems.at[b * 4 + 2 + side],
            recv_sem=recv_sems.at[b * 4 + 2 + side],
            device_id=(row_dev, up if side == 0 else down),
            device_id_type=pl.DeviceIdType.MESH,
        )

    def forward(b):
        raw_copy(b, 0).wait_recv()
        raw_copy(b, 1).wait_recv()
        col_up = pl.multiple_of(up * piece, piece)
        col_down = pl.multiple_of(down * piece, piece)
        to_up = send_buf[b, :, pl.ds(col_up, piece)].astype(jnp.float32)
        to_down = send_buf[b, :, pl.ds(col_down, piece)].astype(jnp.float32)
        from_down = relay_in[b, 0].astype(jnp.float32)
        from_up = relay_in[b, 1].astype(jnp.float32)
        sum_buf[b, 0] = jnp.concatenate(
            [to_up[:, :half] + from_down, to_up[:, half:]], 1
        ).astype(sum_buf.dtype)
        sum_buf[b, 1] = jnp.concatenate(
            [to_down[:, :half], to_down[:, half:] + from_up], 1
        ).astype(sum_buf.dtype)
        sum_copy(b, 0).start()
        sum_copy(b, 1).start()

    def block_body(b, carry):
        row = pl.multiple_of(b * BLOCK, BLOCK)
        bias = bias_ref[b]
        cs = cs_ref[pl.ds(row, BLOCK), :]
        sn = sn_ref[pl.ds(row, BLOCK), :]
        outs = []
        for h in range(heads):
            g = h // rep
            qf = q_ref[pl.ds(row, BLOCK), pl.ds(h * 128, 128)]
            qh = (qf * cs + pltpu.roll(qf, 64, 1) * sn).astype(jnp.bfloat16)
            kw = k_ref[pl.ds(row, 2 * BLOCK), pl.ds(g * 128, 128)]
            vw = v_ref[pl.ds(row, 2 * BLOCK), pl.ds(g * 128, 128)]
            kp = kp_ref[:, pl.ds(g * 128, 128)]
            vp = vp_ref[:, pl.ds(g * 128, 128)]
            keys = jnp.concatenate([kw, kp], 0)
            vals = jnp.concatenate([vw, vp], 0)
            s = lax.dot_general(
                qh, keys, (((1,), (1,)), ((), ())), preferred_element_type=jnp.float32
            ) / HEAD_WIDTH**0.5
            s = s + bias
            m = jnp.max(s, -1, keepdims=True)
            w = jnp.exp(s - m)
            p = (w / jnp.sum(w, -1, keepdims=True)).astype(jnp.bfloat16)
            outs.append(
                jnp.dot(p, vals, preferred_element_type=jnp.float32).astype(jnp.bfloat16)
            )
        att = jnp.concatenate(outs, 1)
        part = jnp.dot(att, wo_ref[...], preferred_element_type=jnp.float32)
        send_buf[b] = part.astype(jnp.bfloat16)
        raw_copy(b, 0).start()
        raw_copy(b, 1).start()

        @pl.when(b > 0)
        def _():
            forward(b - 1)

        return carry

    lax.fori_loop(0, n_blocks, block_body, 0)
    forward(n_blocks - 1)

    own = pl.multiple_of(me * piece, piece)

    def finish_body(b, carry):
        for side in (0, 1):
            raw_copy(b, side).wait_send()
            sum_copy(b, side).wait_send()
            sum_copy(b, side).wait_recv()
        row = pl.multiple_of(b * BLOCK, BLOCK)
        total = res_ref[pl.ds(row, BLOCK), :].astype(jnp.float32)
        total = total + send_buf[b, :, pl.ds(own, piece)].astype(jnp.float32)
        for side in (0, 1):
            total = total + recv_buf[side, pl.ds(row, BLOCK), :].astype(jnp.float32)
        out_ref[pl.ds(row, BLOCK), :] = total.astype(out_ref.dtype)
        return carry

    lax.fori_loop(0, n_blocks, finish_body, 0)


def attend_and_reduce(q, cs, sn, k_pad, v_pad, k_prompt, v_prompt, bias, wo, residual, tp_count):
    rows, q_width = q.shape
    n_blocks = rows // BLOCK
    piece = residual.shape[1]
    width = wo.shape[1]
    kernel = functools.partial(
        attend_kernel,
        tp_count=tp_count,
        heads=q_width // HEAD_WIDTH,
        kv_heads=k_pad.shape[1] // HEAD_WIDTH,
        n_blocks=n_blocks,
    )
    vmem = pltpu.MemorySpace.VMEM
    return pl.pallas_call(
        kernel,
        out_shape=jax.ShapeDtypeStruct((rows, piece), jnp.bfloat16),
        in_specs=[pl.BlockSpec(memory_space=vmem)] * 10,
        out_specs=pl.BlockSpec(memory_space=vmem),
        scratch_shapes=[
            pltpu.VMEM((n_blocks, BLOCK, width), jnp.bfloat16),
            pltpu.VMEM((n_blocks, 2, BLOCK, piece // 2), jnp.bfloat16),
            pltpu.VMEM((n_blocks, 2, BLOCK, piece), jnp.bfloat16),
            pltpu.VMEM((2, rows, piece), jnp.bfloat16),
            pltpu.SemaphoreType.DMA((n_blocks * 4,)),
            pltpu.SemaphoreType.DMA((n_blocks * 4,)),
        ],
        compiler_params=pltpu.CompilerParams(
            collective_id=0, has_side_effects=True, vmem_limit_bytes=48 * 1024 * 1024
        ),
    )(q, cs, sn, k_pad, v_pad, k_prompt, v_prompt, bias, wo, residual)


def ids_kernel(wanted_ref, out_ref, landing, send_sems, recv_sems):
    me = lax.axis_index("req")
    col = lax.axis_index("tp")
    count = lax.axis_size("req")

    def copy_to(k):
        dest = lax.rem(me + k, count)
        return pltpu.make_async_remote_copy(
            src_ref=wanted_ref.at[dest],
            dst_ref=landing.at[me],
            send_sem=send_sems.at[k],
            recv_sem=recv_sems.at[k],
            device_id=(dest, col),
            device_id_type=pl.DeviceIdType.MESH,
        )

    def copy_from(k):
        source = lax.rem(me + count - k, count)
        return pltpu.make_async_remote_copy(
            src_ref=wanted_ref.at[source],
            dst_ref=landing.at[source],
            send_sem=send_sems.at[k],
            recv_sem=recv_sems.at[k],
            device_id=(source, col),
            device_id_type=pl.DeviceIdType.MESH,
        )

    def send(k, carry):
        copy_to(k).start()
        return carry

    lax.fori_loop(1, count, send, 0)
    out_ref[me] = wanted_ref[me]

    def finish(k, carry):
        copy_to(k).wait_send()
        copy_from(k).wait_recv()
        source = lax.rem(me + count - k, count)
        out_ref[source] = landing[source]
        return carry

    lax.fori_loop(1, count, finish, 0)


def exchange_ids(wanted):
    count = wanted.shape[0]
    tiles = jnp.broadcast_to(wanted[:, None, None], (count, 8, 128))
    vmem = pltpu.MemorySpace.VMEM
    got = pl.pallas_call(
        ids_kernel,
        out_shape=jax.ShapeDtypeStruct((count, 8, 128), jnp.int32),
        in_specs=[pl.BlockSpec(memory_space=vmem)],
        out_specs=pl.BlockSpec(memory_space=vmem),
        scratch_shapes=[
            pltpu.VMEM((count, 8, 128), jnp.int32),
            pltpu.SemaphoreType.DMA((count,)),
            pltpu.SemaphoreType.DMA((count,)),
        ],
        compiler_params=pltpu.CompilerParams(has_side_effects=True),
    )(tiles)
    return got[:, 0, 0]


def per_device(
    tokens,
    input_norm_gain,
    query_matrix,
    key_matrix,
    value_matrix,
    output_matrix,
    adapter_down_maps,
    adapter_up_maps,
    request_row_counts,
    prompt_group_per_request,
    adapter_per_request,
    adapter_table_slot,
):
    tp_count = lax.axis_size("tp")
    req_count = lax.axis_size("req")
    tp_index = lax.axis_index("tp")
    tok_rows, width = tokens.shape
    piece_width = width // tp_count
    lengths = request_row_counts[0]
    groups = prompt_group_per_request[0]
    adapters = adapter_per_request[0]
    req_slots = lengths.shape[0]
    request_hot, starts, row_info, token_positions, row_ids = layout(lengths, groups, tok_rows)
    adapters_per_part = adapter_down_maps.shape[0]
    rank_extent = adapter_down_maps.shape[2]
    slots = adapter_table_slot[adapters]
    holder = slots // adapters_per_part
    local_slot = slots % adapters_per_part
    holder_ids = jnp.arange(req_count, dtype=jnp.int32)
    holder_hot = (holder[None, :] == holder_ids[:, None]).astype(jnp.int32)
    wanted = jnp.sum(holder_hot * local_slot[None, :], 1)
    wanted_in = exchange_ids(wanted)
    table = jnp.concatenate([jnp.transpose(adapter_down_maps, (0, 2, 1)), adapter_up_maps], 1)
    maps_out = table[wanted_in]
    tokens, maps_out = lax.optimization_barrier((tokens, maps_out))
    float_tok = tokens.astype(jnp.float32)
    normalized_input = (
        float_tok
        * lax.rsqrt(jnp.mean(float_tok * float_tok, -1, keepdims=True) + 1e-06)
        * input_norm_gain
    ).astype(jnp.bfloat16)
    maps_in = lax.all_to_all(maps_out, "req", split_axis=0, concat_axis=0, tiled=True)
    down_in = maps_in[:, :rank_extent, :].reshape(req_count * rank_extent, piece_width)
    up_in = maps_in[:, rank_extent:, :].reshape(req_count * rank_extent, piece_width)
    normed_slice = lax.dynamic_slice_in_dim(
        normalized_input, tp_index * piece_width, piece_width, 1
    )
    holder_row = jnp.sum(request_hot * holder[None, :], 1)
    pick = (holder_row[:, None] == holder_ids[None, :])[:, :, None]
    wide_rank = jnp.dot(
        normed_slice, down_in.T, preferred_element_type=jnp.float32
    ).reshape(tok_rows, req_count, rank_extent)
    partial_rank = jnp.sum(jnp.where(pick, wide_rank, jnp.float32(0.0)), 1)
    arrived = [
        lax.ppermute(partial_rank, "tp", [(i, (i + k) % tp_count) for i in range(tp_count)])
        for k in range(1, tp_count)
    ]
    for piece in arrived:
        partial_rank = partial_rank + piece
    rank = partial_rank.astype(jnp.bfloat16)
    spread = jnp.where(pick, rank[:, None, :], jnp.zeros((), jnp.bfloat16)).reshape(
        tok_rows, req_count * rank_extent
    )
    query_delta = (
        2.0 * jnp.dot(spread, up_in, preferred_element_type=jnp.float32)
    ).astype(jnp.bfloat16)
    heads_local = query_matrix.shape[1] // HEAD_WIDTH
    kv_local = key_matrix.shape[1] // HEAD_WIDTH
    query_full = jnp.dot(
        normalized_input, query_matrix, preferred_element_type=jnp.float32
    ) + query_delta.astype(jnp.float32)
    half_dim = HEAD_WIDTH // 2
    inverse = 1000000.0 ** (-(jnp.arange(half_dim, dtype=jnp.float32) * 2.0 / HEAD_WIDTH))
    angles = token_positions[:, None] * inverse[None, :]
    cosine = jnp.cos(angles)
    sine = jnp.sin(angles)
    cos_pair = jnp.concatenate([cosine, cosine], 1)
    sin_pair = jnp.concatenate([-sine, sine], 1)
    key_complete = jnp.dot(normalized_input, key_matrix, preferred_element_type=jnp.float32)
    key_head_rows = apply_rotary(
        key_complete.reshape(tok_rows, kv_local, HEAD_WIDTH), token_positions
    ).astype(jnp.bfloat16)
    value_head_rows = (
        jnp.dot(normalized_input, value_matrix, preferred_element_type=jnp.float32)
        .astype(jnp.bfloat16)
        .reshape(tok_rows, kv_local, HEAD_WIDTH)
    )
    request_row, group_row, prompt_row, prompt_start, prompt_len = row_info
    n_blocks = tok_rows // BLOCK
    group_count = prompt_start.shape[0]
    kv_width = kv_local * HEAD_WIDTH
    key_flat = key_head_rows.reshape(tok_rows, kv_width)
    value_flat = value_head_rows.reshape(tok_rows, kv_width)
    front = jnp.zeros((BLOCK, kv_width), jnp.bfloat16)
    k_pad = jnp.concatenate([front, key_flat], 0)
    v_pad = jnp.concatenate([front, value_flat], 0)
    clamp_start = jnp.clip(prompt_start, 0, tok_rows - LMAX)
    extra = BLOCK - group_count * LMAX
    k_prompt = jnp.concatenate(
        [lax.dynamic_slice_in_dim(key_flat, clamp_start[g], LMAX, 0) for g in range(group_count)]
        + [jnp.zeros((extra, kv_width), jnp.bfloat16)],
        0,
    )
    v_prompt = jnp.concatenate(
        [lax.dynamic_slice_in_dim(value_flat, clamp_start[g], LMAX, 0) for g in range(group_count)]
        + [jnp.zeros((extra, kv_width), jnp.bfloat16)],
        0,
    )
    def windows(values, fill):
        padded = jnp.concatenate([jnp.full((BLOCK,), fill, values.dtype), values]).reshape(
            n_blocks + 1, BLOCK
        )
        return jnp.concatenate([padded[:-1], padded[1:]], 1)

    win_row = windows(row_ids, -1)
    win_req = windows(request_row, -1)
    win_grp = windows(group_row, -1)
    win_prm = windows(prompt_row, 0)
    q_row = row_ids.reshape(n_blocks, BLOCK)[:, :, None]
    q_req = request_row.reshape(n_blocks, BLOCK)[:, :, None]
    q_grp = group_row.reshape(n_blocks, BLOCK)[:, :, None]
    win_vis = (
        (win_row[:, None, :] >= 0)
        & (win_grp[:, None, :] == q_grp)
        & (win_row[:, None, :] <= q_row)
        & ((win_req[:, None, :] == q_req) | (win_prm[:, None, :] == 1))
    )
    p_row = (clamp_start[:, None] + jnp.arange(LMAX, dtype=jnp.int32)[None, :]).reshape(-1)
    p_lo = jnp.repeat(prompt_start, LMAX)
    p_hi = jnp.repeat(prompt_start + prompt_len, LMAX)
    p_grp = jnp.repeat(jnp.arange(group_count, dtype=jnp.int32), LMAX)
    p_row = jnp.concatenate([p_row, jnp.zeros((extra,), jnp.int32)])
    p_lo = jnp.concatenate([p_lo, jnp.ones((extra,), jnp.int32)])
    p_hi = jnp.concatenate([p_hi, jnp.zeros((extra,), jnp.int32)])
    p_grp = jnp.concatenate([p_grp, jnp.full((extra,), -1, jnp.int32)])
    win_first = q_row[:, :1, :] - BLOCK
    prompt_vis = (
        (p_grp[None, None, :] == q_grp)
        & (p_row[None, None, :] >= p_lo[None, None, :])
        & (p_row[None, None, :] < p_hi[None, None, :])
        & (p_row[None, None, :] < win_first)
        & (p_row[None, None, :] <= q_row)
    )
    vis = jnp.concatenate([win_vis, prompt_vis], 2)
    bias = jnp.where(vis, jnp.float32(0.0), jnp.float32(-1e30))
    residual = lax.dynamic_slice_in_dim(tokens, tp_index * piece_width, piece_width, 1)
    return attend_and_reduce(
        query_full,
        cos_pair,
        sin_pair,
        k_pad,
        v_pad,
        k_prompt,
        v_prompt,
        bias,
        output_matrix,
        residual,
        tp_count,
    )


def solution(mesh):
    return jax.shard_map(
        per_device,
        mesh=mesh,
        in_specs=(
            P("req", None),
            P(),
            P(None, "tp"),
            P(None, "tp"),
            P(None, "tp"),
            P("tp", None),
            P("req", "tp", None),
            P("req", None, "tp"),
            P("req", None),
            P("req", None),
            P("req", None),
            P(),
        ),
        out_specs=P("req", "tp"),
        check_vma=False,
    )
```

```python
import jax
import jax.numpy as jnp
import functools
from jax import lax
from jax.experimental import pallas as pl
from jax.experimental.pallas import tpu as pltpu
from jax.sharding import PartitionSpec as P

HEAD_WIDTH = 128
REQ_DEV = 32
LMAX = 40


def apply_rotary(vectors, token_positions):
    head_size = vectors.shape[-1]
    half_dim = head_size // 2
    inverse = 1000000.0 ** (-(jnp.arange(half_dim, dtype=jnp.float32) * 2.0 / head_size))
    angles = token_positions[:, None] * inverse[None, :]
    cosine = jnp.cos(angles)[:, None, :]
    sine_part = jnp.sin(angles)[:, None, :]
    first_half = vectors[..., :half_dim]
    second = vectors[..., half_dim:]
    return jnp.concatenate(
        [first_half * cosine - second * sine_part, second * cosine + first_half * sine_part], -1
    )


def layout(lengths, groups, tok_rows):
    req_slots = lengths.shape[0]
    row_ids = jnp.arange(tok_rows, dtype=jnp.int32)
    row_ends = jnp.cumsum(lengths)
    starts = row_ends - lengths
    request_row = jnp.sum((row_ids[:, None] >= row_ends[None, :]).astype(jnp.int32), 1)
    request_hot = (request_row[:, None] == jnp.arange(req_slots, dtype=jnp.int32)[None, :]).astype(
        jnp.int32
    )
    previous = jnp.concatenate([jnp.full((1,), -1, jnp.int32), groups[:-1]])
    is_prompt = (groups != previous).astype(jnp.int32)
    prompt_len = jnp.sum(
        lengths[None, :]
        * is_prompt[None, :]
        * (groups[None, :] == groups[:, None]).astype(jnp.int32),
        1,
    )
    offset_req = (1 - is_prompt) * prompt_len - starts
    group_row = jnp.sum(request_hot * groups[None, :], 1)
    prompt_row = jnp.sum(request_hot * is_prompt[None, :], 1)
    offset_row = jnp.sum(request_hot * offset_req[None, :], 1)
    token_positions = (row_ids + offset_row).astype(jnp.float32)
    group_ids = jnp.arange(3, dtype=jnp.int32)
    group_hot = (groups[None, :] == group_ids[:, None]).astype(jnp.int32)
    prompt_start = jnp.sum((starts * is_prompt)[None, :] * group_hot, 1)
    prompt_len = jnp.sum((lengths * is_prompt)[None, :] * group_hot, 1)
    rows = (request_row, group_row, prompt_row, prompt_start, prompt_len)
    return (request_hot, starts, rows, token_positions, row_ids)


BLOCK = 128


def attend_kernel(
    q_ref, cs_ref, sn_ref, k_ref, v_ref, kp_ref, vp_ref, bias_ref, wo_ref, res_ref, out_ref,
    send_buf, relay_in, sum_buf, recv_buf, send_sems, recv_sems, *, tp_count, heads, kv_heads,
    n_blocks
):
    me = lax.axis_index("tp")
    row_dev = lax.axis_index("req")
    piece = out_ref.shape[1]
    half = piece // 2
    up = lax.rem(me + 1, tp_count)
    down = lax.rem(me + tp_count - 1, tp_count)
    across = lax.rem(me + 2, tp_count)
    barrier = pltpu.get_barrier_semaphore()
    for peer in (up, down):
        pl.semaphore_signal(
            barrier, inc=1, device_id=(row_dev, peer), device_id_type=pl.DeviceIdType.MESH
        )
    pl.semaphore_wait(barrier, 2)
    rep = heads // kv_heads

    def raw_copy(b, side):
        col = pl.multiple_of(across * piece + side * half, half)
        return pltpu.make_async_remote_copy(
            src_ref=send_buf.at[b, :, pl.ds(col, half)],
            dst_ref=relay_in.at[b, side],
            send_sem=send_sems.at[b * 4 + side],
            recv_sem=recv_sems.at[b * 4 + side],
            device_id=(row_dev, up if side == 0 else down),
            device_id_type=pl.DeviceIdType.MESH,
        )

    def sum_copy(b, side):
        row = pl.multiple_of(b * BLOCK, BLOCK)
        return pltpu.make_async_remote_copy(
            src_ref=sum_buf.at[b, side],
            dst_ref=recv_buf.at[side, pl.ds(row, BLOCK)],
            send_sem=send_sems.at[b * 4 + 2 + side],
            recv_sem=recv_sems.at[b * 4 + 2 + side],
            device_id=(row_dev, up if side == 0 else down),
            device_id_type=pl.DeviceIdType.MESH,
        )

    def forward(b):
        raw_copy(b, 0).wait_recv()
        raw_copy(b, 1).wait_recv()
        col_up = pl.multiple_of(up * piece, piece)
        col_down = pl.multiple_of(down * piece, piece)
        to_up = send_buf[b, :, pl.ds(col_up, piece)].astype(jnp.float32)
        to_down = send_buf[b, :, pl.ds(col_down, piece)].astype(jnp.float32)
        from_down = relay_in[b, 0].astype(jnp.float32)
        from_up = relay_in[b, 1].astype(jnp.float32)
        sum_buf[b, 0] = jnp.concatenate(
            [to_up[:, :half] + from_down, to_up[:, half:]], 1
        ).astype(sum_buf.dtype)
        sum_buf[b, 1] = jnp.concatenate(
            [to_down[:, :half], to_down[:, half:] + from_up], 1
        ).astype(sum_buf.dtype)
        sum_copy(b, 0).start()
        sum_copy(b, 1).start()

    def block_body(b, carry):
        row = pl.multiple_of(b * BLOCK, BLOCK)
        bias = bias_ref[b]
        cs = cs_ref[pl.ds(row, BLOCK), :]
        sn = sn_ref[pl.ds(row, BLOCK), :]
        outs = []
        for h in range(heads):
            g = h // rep
            qf = q_ref[pl.ds(row, BLOCK), pl.ds(h * 128, 128)]
            qh = (qf * cs + pltpu.roll(qf, 64, 1) * sn).astype(jnp.bfloat16)
            kw = k_ref[pl.ds(row, 2 * BLOCK), pl.ds(g * 128, 128)]
            vw = v_ref[pl.ds(row, 2 * BLOCK), pl.ds(g * 128, 128)]
            kp = kp_ref[:, pl.ds(g * 128, 128)]
            vp = vp_ref[:, pl.ds(g * 128, 128)]
            keys = jnp.concatenate([kw, kp], 0)
            vals = jnp.concatenate([vw, vp], 0)
            s = lax.dot_general(
                qh, keys, (((1,), (1,)), ((), ())), preferred_element_type=jnp.float32
            ) / HEAD_WIDTH**0.5
            s = s + bias
            m = jnp.max(s, -1, keepdims=True)
            w = jnp.exp(s - m)
            p = (w / jnp.sum(w, -1, keepdims=True)).astype(jnp.bfloat16)
            outs.append(
                jnp.dot(p, vals, preferred_element_type=jnp.float32).astype(jnp.bfloat16)
            )
        att = jnp.concatenate(outs, 1)
        part = jnp.dot(att, wo_ref[...], preferred_element_type=jnp.float32)
        send_buf[b] = part.astype(jnp.bfloat16)
        raw_copy(b, 0).start()
        raw_copy(b, 1).start()

        @pl.when(b > 0)
        def _():
            forward(b - 1)

        return carry

    lax.fori_loop(0, n_blocks, block_body, 0)
    forward(n_blocks - 1)

    own = pl.multiple_of(me * piece, piece)

    def finish_body(b, carry):
        for side in (0, 1):
            raw_copy(b, side).wait_send()
            sum_copy(b, side).wait_send()
            sum_copy(b, side).wait_recv()
        row = pl.multiple_of(b * BLOCK, BLOCK)
        total = res_ref[pl.ds(row, BLOCK), :].astype(jnp.float32)
        total = total + send_buf[b, :, pl.ds(own, piece)].astype(jnp.float32)
        for side in (0, 1):
            total = total + recv_buf[side, pl.ds(row, BLOCK), :].astype(jnp.float32)
        out_ref[pl.ds(row, BLOCK), :] = total.astype(out_ref.dtype)
        return carry

    lax.fori_loop(0, n_blocks, finish_body, 0)


def attend_and_reduce(q, cs, sn, k_pad, v_pad, k_prompt, v_prompt, bias, wo, residual, tp_count):
    rows, q_width = q.shape
    n_blocks = rows // BLOCK
    piece = residual.shape[1]
    width = wo.shape[1]
    kernel = functools.partial(
        attend_kernel,
        tp_count=tp_count,
        heads=q_width // HEAD_WIDTH,
        kv_heads=k_pad.shape[1] // HEAD_WIDTH,
        n_blocks=n_blocks,
    )
    vmem = pltpu.MemorySpace.VMEM
    return pl.pallas_call(
        kernel,
        out_shape=jax.ShapeDtypeStruct((rows, piece), jnp.bfloat16),
        in_specs=[pl.BlockSpec(memory_space=vmem)] * 10,
        out_specs=pl.BlockSpec(memory_space=vmem),
        scratch_shapes=[
            pltpu.VMEM((n_blocks, BLOCK, width), jnp.bfloat16),
            pltpu.VMEM((n_blocks, 2, BLOCK, piece // 2), jnp.bfloat16),
            pltpu.VMEM((n_blocks, 2, BLOCK, piece), jnp.bfloat16),
            pltpu.VMEM((2, rows, piece), jnp.bfloat16),
            pltpu.SemaphoreType.DMA((n_blocks * 4,)),
            pltpu.SemaphoreType.DMA((n_blocks * 4,)),
        ],
        compiler_params=pltpu.CompilerParams(
            collective_id=0, has_side_effects=True, vmem_limit_bytes=48 * 1024 * 1024
        ),
    )(q, cs, sn, k_pad, v_pad, k_prompt, v_prompt, bias, wo, residual)


def ids_kernel(wanted_ref, out_ref, landing, send_sems, recv_sems):
    me = lax.axis_index("req")
    col = lax.axis_index("tp")
    count = lax.axis_size("req")
    barrier = pltpu.get_barrier_semaphore()

    def greet(k, carry):
        peer = lax.rem(me + k, count)
        pl.semaphore_signal(
            barrier, inc=1, device_id=(peer, col), device_id_type=pl.DeviceIdType.MESH
        )
        return carry

    lax.fori_loop(1, count, greet, 0)
    pl.semaphore_wait(barrier, count - 1)

    def copy_to(k):
        dest = lax.rem(me + k, count)
        return pltpu.make_async_remote_copy(
            src_ref=wanted_ref.at[dest],
            dst_ref=landing.at[me],
            send_sem=send_sems.at[k],
            recv_sem=recv_sems.at[k],
            device_id=(dest, col),
            device_id_type=pl.DeviceIdType.MESH,
        )

    def copy_from(k):
        source = lax.rem(me + count - k, count)
        return pltpu.make_async_remote_copy(
            src_ref=wanted_ref.at[source],
            dst_ref=landing.at[source],
            send_sem=send_sems.at[k],
            recv_sem=recv_sems.at[k],
            device_id=(source, col),
            device_id_type=pl.DeviceIdType.MESH,
        )

    def send(k, carry):
        copy_to(k).start()
        return carry

    lax.fori_loop(1, count, send, 0)
    out_ref[me] = wanted_ref[me]

    def finish(k, carry):
        copy_to(k).wait_send()
        copy_from(k).wait_recv()
        source = lax.rem(me + count - k, count)
        out_ref[source] = landing[source]
        return carry

    lax.fori_loop(1, count, finish, 0)


def exchange_ids(wanted):
    count = wanted.shape[0]
    tiles = jnp.broadcast_to(wanted[:, None, None], (count, 8, 128))
    vmem = pltpu.MemorySpace.VMEM
    got = pl.pallas_call(
        ids_kernel,
        out_shape=jax.ShapeDtypeStruct((count, 8, 128), jnp.int32),
        in_specs=[pl.BlockSpec(memory_space=vmem)],
        out_specs=pl.BlockSpec(memory_space=vmem),
        scratch_shapes=[
            pltpu.VMEM((count, 8, 128), jnp.int32),
            pltpu.SemaphoreType.DMA((count,)),
            pltpu.SemaphoreType.DMA((count,)),
        ],
        compiler_params=pltpu.CompilerParams(collective_id=1, has_side_effects=True),
    )(tiles)
    return got


def per_device(
    tokens,
    input_norm_gain,
    query_matrix,
    key_matrix,
    value_matrix,
    output_matrix,
    adapter_down_maps,
    adapter_up_maps,
    request_row_counts,
    prompt_group_per_request,
    adapter_per_request,
    adapter_table_slot,
):
    tp_count = lax.axis_size("tp")
    req_count = lax.axis_size("req")
    tp_index = lax.axis_index("tp")
    tok_rows, width = tokens.shape
    piece_width = width // tp_count
    lengths = request_row_counts[0]
    groups = prompt_group_per_request[0]
    adapters = adapter_per_request[0]
    req_slots = lengths.shape[0]
    request_hot, starts, row_info, token_positions, row_ids = layout(lengths, groups, tok_rows)
    adapters_per_part = adapter_down_maps.shape[0]
    rank_extent = adapter_down_maps.shape[2]
    slots = adapter_table_slot[adapters]
    holder = slots // adapters_per_part
    local_slot = slots % adapters_per_part
    holder_ids = jnp.arange(req_count, dtype=jnp.int32)
    holder_hot = (holder[None, :] == holder_ids[:, None]).astype(jnp.int32)
    wanted = jnp.sum(holder_hot * local_slot[None, :], 1)
    wanted_in = exchange_ids(wanted)
    table = jnp.concatenate([jnp.transpose(adapter_down_maps, (0, 2, 1)), adapter_up_maps], 1)
    slot_hot = (
        wanted_in[:, 0, :adapters_per_part]
        == jnp.arange(adapters_per_part, dtype=jnp.int32)[None, :]
    ).astype(table.dtype)
    maps_out = (
        jnp.dot(slot_hot, table.reshape(adapters_per_part, -1), preferred_element_type=jnp.float32)
        .astype(table.dtype)
        .reshape((req_count,) + table.shape[1:])
    )
    tokens, maps_out = lax.optimization_barrier((tokens, maps_out))
    float_tok = tokens.astype(jnp.float32)
    normalized_input = (
        float_tok
        * lax.rsqrt(jnp.mean(float_tok * float_tok, -1, keepdims=True) + 1e-06)
        * input_norm_gain
    ).astype(jnp.bfloat16)
    maps_in = lax.all_to_all(maps_out, "req", split_axis=0, concat_axis=0, tiled=True)
    down_in = maps_in[:, :rank_extent, :].reshape(req_count * rank_extent, piece_width)
    up_in = maps_in[:, rank_extent:, :].reshape(req_count * rank_extent, piece_width)
    normed_slice = lax.dynamic_slice_in_dim(
        normalized_input, tp_index * piece_width, piece_width, 1
    )
    holder_row = jnp.sum(request_hot * holder[None, :], 1)
    pick = (holder_row[:, None] == holder_ids[None, :])[:, :, None]
    wide_rank = jnp.dot(
        normed_slice, down_in.T, preferred_element_type=jnp.float32
    ).reshape(tok_rows, req_count, rank_extent)
    partial_rank = jnp.sum(jnp.where(pick, wide_rank, jnp.float32(0.0)), 1)
    arrived = [
        lax.ppermute(partial_rank, "tp", [(i, (i + k) % tp_count) for i in range(tp_count)])
        for k in range(1, tp_count)
    ]
    for piece in arrived:
        partial_rank = partial_rank + piece
    rank = partial_rank.astype(jnp.bfloat16)
    spread = jnp.where(pick, rank[:, None, :], jnp.zeros((), jnp.bfloat16)).reshape(
        tok_rows, req_count * rank_extent
    )
    query_delta = (
        2.0 * jnp.dot(spread, up_in, preferred_element_type=jnp.float32)
    ).astype(jnp.bfloat16)
    heads_local = query_matrix.shape[1] // HEAD_WIDTH
    kv_local = key_matrix.shape[1] // HEAD_WIDTH
    query_full = jnp.dot(
        normalized_input, query_matrix, preferred_element_type=jnp.float32
    ) + query_delta.astype(jnp.float32)
    half_dim = HEAD_WIDTH // 2
    inverse = 1000000.0 ** (-(jnp.arange(half_dim, dtype=jnp.float32) * 2.0 / HEAD_WIDTH))
    angles = token_positions[:, None] * inverse[None, :]
    cosine = jnp.cos(angles)
    sine = jnp.sin(angles)
    cos_pair = jnp.concatenate([cosine, cosine], 1)
    sin_pair = jnp.concatenate([-sine, sine], 1)
    key_complete = jnp.dot(normalized_input, key_matrix, preferred_element_type=jnp.float32)
    key_head_rows = apply_rotary(
        key_complete.reshape(tok_rows, kv_local, HEAD_WIDTH), token_positions
    ).astype(jnp.bfloat16)
    value_head_rows = (
        jnp.dot(normalized_input, value_matrix, preferred_element_type=jnp.float32)
        .astype(jnp.bfloat16)
        .reshape(tok_rows, kv_local, HEAD_WIDTH)
    )
    request_row, group_row, prompt_row, prompt_start, prompt_len = row_info
    n_blocks = tok_rows // BLOCK
    group_count = prompt_start.shape[0]
    kv_width = kv_local * HEAD_WIDTH
    key_flat = key_head_rows.reshape(tok_rows, kv_width)
    value_flat = value_head_rows.reshape(tok_rows, kv_width)
    front = jnp.zeros((BLOCK, kv_width), jnp.bfloat16)
    k_pad = jnp.concatenate([front, key_flat], 0)
    v_pad = jnp.concatenate([front, value_flat], 0)
    clamp_start = jnp.clip(prompt_start, 0, tok_rows - LMAX)
    extra = BLOCK - group_count * LMAX
    k_prompt = jnp.concatenate(
        [lax.dynamic_slice_in_dim(key_flat, clamp_start[g], LMAX, 0) for g in range(group_count)]
        + [jnp.zeros((extra, kv_width), jnp.bfloat16)],
        0,
    )
    v_prompt = jnp.concatenate(
        [lax.dynamic_slice_in_dim(value_flat, clamp_start[g], LMAX, 0) for g in range(group_count)]
        + [jnp.zeros((extra, kv_width), jnp.bfloat16)],
        0,
    )
    def windows(values, fill):
        padded = jnp.concatenate([jnp.full((BLOCK,), fill, values.dtype), values]).reshape(
            n_blocks + 1, BLOCK
        )
        return jnp.concatenate([padded[:-1], padded[1:]], 1)

    win_row = windows(row_ids, -1)
    win_req = windows(request_row, -1)
    win_grp = windows(group_row, -1)
    win_prm = windows(prompt_row, 0)
    q_row = row_ids.reshape(n_blocks, BLOCK)[:, :, None]
    q_req = request_row.reshape(n_blocks, BLOCK)[:, :, None]
    q_grp = group_row.reshape(n_blocks, BLOCK)[:, :, None]
    win_vis = (
        (win_row[:, None, :] >= 0)
        & (win_grp[:, None, :] == q_grp)
        & (win_row[:, None, :] <= q_row)
        & ((win_req[:, None, :] == q_req) | (win_prm[:, None, :] == 1))
    )
    p_row = (clamp_start[:, None] + jnp.arange(LMAX, dtype=jnp.int32)[None, :]).reshape(-1)
    p_lo = jnp.repeat(prompt_start, LMAX)
    p_hi = jnp.repeat(prompt_start + prompt_len, LMAX)
    p_grp = jnp.repeat(jnp.arange(group_count, dtype=jnp.int32), LMAX)
    p_row = jnp.concatenate([p_row, jnp.zeros((extra,), jnp.int32)])
    p_lo = jnp.concatenate([p_lo, jnp.ones((extra,), jnp.int32)])
    p_hi = jnp.concatenate([p_hi, jnp.zeros((extra,), jnp.int32)])
    p_grp = jnp.concatenate([p_grp, jnp.full((extra,), -1, jnp.int32)])
    win_first = q_row[:, :1, :] - BLOCK
    prompt_vis = (
        (p_grp[None, None, :] == q_grp)
        & (p_row[None, None, :] >= p_lo[None, None, :])
        & (p_row[None, None, :] < p_hi[None, None, :])
        & (p_row[None, None, :] < win_first)
        & (p_row[None, None, :] <= q_row)
    )
    vis = jnp.concatenate([win_vis, prompt_vis], 2)
    bias = jnp.where(vis, jnp.float32(0.0), jnp.float32(-1e30))
    residual = lax.dynamic_slice_in_dim(tokens, tp_index * piece_width, piece_width, 1)
    return attend_and_reduce(
        query_full,
        cos_pair,
        sin_pair,
        k_pad,
        v_pad,
        k_prompt,
        v_prompt,
        bias,
        output_matrix,
        residual,
        tp_count,
    )


def solution(mesh):
    return jax.shard_map(
        per_device,
        mesh=mesh,
        in_specs=(
            P("req", None),
            P(),
            P(None, "tp"),
            P(None, "tp"),
            P(None, "tp"),
            P("tp", None),
            P("req", "tp", None),
            P("req", None, "tp"),
            P("req", None),
            P("req", None),
            P("req", None),
            P(),
        ),
        out_specs=P("req", "tp"),
        check_vma=False,
    )
```

```python
import jax
import jax.numpy as jnp
import functools
from jax import lax
from jax.experimental import pallas as pl
from jax.experimental.pallas import tpu as pltpu
from jax.sharding import PartitionSpec as P

HEAD_WIDTH = 128
REQ_DEV = 32
LMAX = 40


def apply_rotary(vectors, token_positions):
    head_size = vectors.shape[-1]
    half_dim = head_size // 2
    inverse = 1000000.0 ** (-(jnp.arange(half_dim, dtype=jnp.float32) * 2.0 / head_size))
    angles = token_positions[:, None] * inverse[None, :]
    cosine = jnp.cos(angles)[:, None, :]
    sine_part = jnp.sin(angles)[:, None, :]
    first_half = vectors[..., :half_dim]
    second = vectors[..., half_dim:]
    return jnp.concatenate(
        [first_half * cosine - second * sine_part, second * cosine + first_half * sine_part], -1
    )


def layout(lengths, groups, tok_rows):
    req_slots = lengths.shape[0]
    row_ids = jnp.arange(tok_rows, dtype=jnp.int32)
    row_ends = jnp.cumsum(lengths)
    starts = row_ends - lengths
    request_row = jnp.sum((row_ids[:, None] >= row_ends[None, :]).astype(jnp.int32), 1)
    request_hot = (request_row[:, None] == jnp.arange(req_slots, dtype=jnp.int32)[None, :]).astype(
        jnp.int32
    )
    previous = jnp.concatenate([jnp.full((1,), -1, jnp.int32), groups[:-1]])
    is_prompt = (groups != previous).astype(jnp.int32)
    prompt_len = jnp.sum(
        lengths[None, :]
        * is_prompt[None, :]
        * (groups[None, :] == groups[:, None]).astype(jnp.int32),
        1,
    )
    offset_req = (1 - is_prompt) * prompt_len - starts
    group_row = jnp.sum(request_hot * groups[None, :], 1)
    prompt_row = jnp.sum(request_hot * is_prompt[None, :], 1)
    offset_row = jnp.sum(request_hot * offset_req[None, :], 1)
    token_positions = (row_ids + offset_row).astype(jnp.float32)
    group_ids = jnp.arange(3, dtype=jnp.int32)
    group_hot = (groups[None, :] == group_ids[:, None]).astype(jnp.int32)
    prompt_start = jnp.sum((starts * is_prompt)[None, :] * group_hot, 1)
    prompt_len = jnp.sum((lengths * is_prompt)[None, :] * group_hot, 1)
    rows = (request_row, group_row, prompt_row, prompt_start, prompt_len)
    return (request_hot, starts, rows, token_positions, row_ids)


BLOCK = 128


def attend_kernel(
    q_ref, d_ref, cs_ref, sn_ref, k_ref, v_ref, kp_ref, vp_ref, bias_ref, wo_ref, res_ref, out_ref,
    send_buf, relay_in, sum_buf, recv_buf, send_sems, recv_sems, *, tp_count, heads, kv_heads,
    n_blocks
):
    me = lax.axis_index("tp")
    row_dev = lax.axis_index("req")
    piece = out_ref.shape[1]
    half = piece // 2
    up = lax.rem(me + 1, tp_count)
    down = lax.rem(me + tp_count - 1, tp_count)
    across = lax.rem(me + 2, tp_count)
    barrier = pltpu.get_barrier_semaphore()
    for peer in (up, down):
        pl.semaphore_signal(
            barrier, inc=1, device_id=(row_dev, peer), device_id_type=pl.DeviceIdType.MESH
        )
    pl.semaphore_wait(barrier, 2)
    rep = heads // kv_heads

    def raw_copy(b, side):
        col = pl.multiple_of(across * piece + side * half, half)
        return pltpu.make_async_remote_copy(
            src_ref=send_buf.at[b, :, pl.ds(col, half)],
            dst_ref=relay_in.at[b, side],
            send_sem=send_sems.at[b * 4 + side],
            recv_sem=recv_sems.at[b * 4 + side],
            device_id=(row_dev, up if side == 0 else down),
            device_id_type=pl.DeviceIdType.MESH,
        )

    def sum_copy(b, side):
        row = pl.multiple_of(b * BLOCK, BLOCK)
        return pltpu.make_async_remote_copy(
            src_ref=sum_buf.at[b, side],
            dst_ref=recv_buf.at[side, pl.ds(row, BLOCK)],
            send_sem=send_sems.at[b * 4 + 2 + side],
            recv_sem=recv_sems.at[b * 4 + 2 + side],
            device_id=(row_dev, up if side == 0 else down),
            device_id_type=pl.DeviceIdType.MESH,
        )

    def forward(b):
        raw_copy(b, 0).wait_recv()
        raw_copy(b, 1).wait_recv()
        col_up = pl.multiple_of(up * piece, piece)
        col_down = pl.multiple_of(down * piece, piece)
        to_up = send_buf[b, :, pl.ds(col_up, piece)].astype(jnp.float32)
        to_down = send_buf[b, :, pl.ds(col_down, piece)].astype(jnp.float32)
        from_down = relay_in[b, 0].astype(jnp.float32)
        from_up = relay_in[b, 1].astype(jnp.float32)
        sum_buf[b, 0] = jnp.concatenate(
            [to_up[:, :half] + from_down, to_up[:, half:]], 1
        ).astype(sum_buf.dtype)
        sum_buf[b, 1] = jnp.concatenate(
            [to_down[:, :half], to_down[:, half:] + from_up], 1
        ).astype(sum_buf.dtype)
        sum_copy(b, 0).start()
        sum_copy(b, 1).start()

    def block_body(b, carry):
        row = pl.multiple_of(b * BLOCK, BLOCK)
        bias = bias_ref[b]
        cs = cs_ref[pl.ds(row, BLOCK), :]
        sn = sn_ref[pl.ds(row, BLOCK), :]
        outs = []
        for h in range(heads):
            g = h // rep
            qf = q_ref[pl.ds(row, BLOCK), pl.ds(h * 128, 128)] + d_ref[
                pl.ds(row, BLOCK), pl.ds(h * 128, 128)
            ].astype(jnp.float32)
            qh = (qf * cs + pltpu.roll(qf, 64, 1) * sn).astype(jnp.bfloat16)
            kw = k_ref[pl.ds(row, 2 * BLOCK), pl.ds(g * 128, 128)]
            vw = v_ref[pl.ds(row, 2 * BLOCK), pl.ds(g * 128, 128)]
            kp = kp_ref[:, pl.ds(g * 128, 128)]
            vp = vp_ref[:, pl.ds(g * 128, 128)]
            keys = jnp.concatenate([kw, kp], 0)
            vals = jnp.concatenate([vw, vp], 0)
            s = lax.dot_general(
                qh, keys, (((1,), (1,)), ((), ())), preferred_element_type=jnp.float32
            ) / HEAD_WIDTH**0.5
            s = s + bias
            m = jnp.max(s, -1, keepdims=True)
            w = jnp.exp(s - m)
            p = (w / jnp.sum(w, -1, keepdims=True)).astype(jnp.bfloat16)
            outs.append(
                jnp.dot(p, vals, preferred_element_type=jnp.float32).astype(jnp.bfloat16)
            )
        att = jnp.concatenate(outs, 1)
        part = jnp.dot(att, wo_ref[...], preferred_element_type=jnp.float32)
        send_buf[b] = part.astype(jnp.bfloat16)
        raw_copy(b, 0).start()
        raw_copy(b, 1).start()

        @pl.when(b > 0)
        def _():
            forward(b - 1)

        return carry

    lax.fori_loop(0, n_blocks, block_body, 0)
    forward(n_blocks - 1)

    own = pl.multiple_of(me * piece, piece)

    def finish_body(b, carry):
        for side in (0, 1):
            raw_copy(b, side).wait_send()
            sum_copy(b, side).wait_send()
            sum_copy(b, side).wait_recv()
        row = pl.multiple_of(b * BLOCK, BLOCK)
        total = res_ref[pl.ds(row, BLOCK), :].astype(jnp.float32)
        total = total + send_buf[b, :, pl.ds(own, piece)].astype(jnp.float32)
        for side in (0, 1):
            total = total + recv_buf[side, pl.ds(row, BLOCK), :].astype(jnp.float32)
        out_ref[pl.ds(row, BLOCK), :] = total.astype(out_ref.dtype)
        return carry

    lax.fori_loop(0, n_blocks, finish_body, 0)


def attend_and_reduce(q, delta, cs, sn, k_pad, v_pad, k_prompt, v_prompt, bias, wo, residual, tp_count):
    rows, q_width = q.shape
    n_blocks = rows // BLOCK
    piece = residual.shape[1]
    width = wo.shape[1]
    kernel = functools.partial(
        attend_kernel,
        tp_count=tp_count,
        heads=q_width // HEAD_WIDTH,
        kv_heads=k_pad.shape[1] // HEAD_WIDTH,
        n_blocks=n_blocks,
    )
    vmem = pltpu.MemorySpace.VMEM
    return pl.pallas_call(
        kernel,
        out_shape=jax.ShapeDtypeStruct((rows, piece), jnp.bfloat16),
        in_specs=[pl.BlockSpec(memory_space=vmem)] * 11,
        out_specs=pl.BlockSpec(memory_space=vmem),
        scratch_shapes=[
            pltpu.VMEM((n_blocks, BLOCK, width), jnp.bfloat16),
            pltpu.VMEM((n_blocks, 2, BLOCK, piece // 2), jnp.bfloat16),
            pltpu.VMEM((n_blocks, 2, BLOCK, piece), jnp.bfloat16),
            pltpu.VMEM((2, rows, piece), jnp.bfloat16),
            pltpu.SemaphoreType.DMA((n_blocks * 4,)),
            pltpu.SemaphoreType.DMA((n_blocks * 4,)),
        ],
        compiler_params=pltpu.CompilerParams(
            collective_id=0, has_side_effects=True, vmem_limit_bytes=48 * 1024 * 1024
        ),
    )(q, delta, cs, sn, k_pad, v_pad, k_prompt, v_prompt, bias, wo, residual)


def ids_kernel(wanted_ref, out_ref, landing, send_sems, recv_sems):
    me = lax.axis_index("req")
    col = lax.axis_index("tp")
    count = lax.axis_size("req")
    barrier = pltpu.get_barrier_semaphore()

    def greet(k, carry):
        peer = lax.rem(me + k, count)
        pl.semaphore_signal(
            barrier, inc=1, device_id=(peer, col), device_id_type=pl.DeviceIdType.MESH
        )
        return carry

    lax.fori_loop(1, count, greet, 0)
    pl.semaphore_wait(barrier, count - 1)

    def copy_to(k):
        dest = lax.rem(me + k, count)
        return pltpu.make_async_remote_copy(
            src_ref=wanted_ref.at[dest],
            dst_ref=landing.at[me],
            send_sem=send_sems.at[k],
            recv_sem=recv_sems.at[k],
            device_id=(dest, col),
            device_id_type=pl.DeviceIdType.MESH,
        )

    def copy_from(k):
        source = lax.rem(me + count - k, count)
        return pltpu.make_async_remote_copy(
            src_ref=wanted_ref.at[source],
            dst_ref=landing.at[source],
            send_sem=send_sems.at[k],
            recv_sem=recv_sems.at[k],
            device_id=(source, col),
            device_id_type=pl.DeviceIdType.MESH,
        )

    def send(k, carry):
        copy_to(k).start()
        return carry

    lax.fori_loop(1, count, send, 0)
    out_ref[me] = wanted_ref[me]

    def finish(k, carry):
        copy_to(k).wait_send()
        copy_from(k).wait_recv()
        source = lax.rem(me + count - k, count)
        out_ref[source] = landing[source]
        return carry

    lax.fori_loop(1, count, finish, 0)


def exchange_ids(wanted):
    count = wanted.shape[0]
    tiles = jnp.broadcast_to(wanted[:, None, None], (count, 8, 128))
    vmem = pltpu.MemorySpace.VMEM
    got = pl.pallas_call(
        ids_kernel,
        out_shape=jax.ShapeDtypeStruct((count, 8, 128), jnp.int32),
        in_specs=[pl.BlockSpec(memory_space=vmem)],
        out_specs=pl.BlockSpec(memory_space=vmem),
        scratch_shapes=[
            pltpu.VMEM((count, 8, 128), jnp.int32),
            pltpu.SemaphoreType.DMA((count,)),
            pltpu.SemaphoreType.DMA((count,)),
        ],
        compiler_params=pltpu.CompilerParams(collective_id=1, has_side_effects=True),
    )(tiles)
    return got[:, 0, 0]


def per_device(
    tokens,
    input_norm_gain,
    query_matrix,
    key_matrix,
    value_matrix,
    output_matrix,
    adapter_down_maps,
    adapter_up_maps,
    request_row_counts,
    prompt_group_per_request,
    adapter_per_request,
    adapter_table_slot,
):
    tp_count = lax.axis_size("tp")
    req_count = lax.axis_size("req")
    tp_index = lax.axis_index("tp")
    tok_rows, width = tokens.shape
    piece_width = width // tp_count
    lengths = request_row_counts[0]
    groups = prompt_group_per_request[0]
    adapters = adapter_per_request[0]
    req_slots = lengths.shape[0]
    request_hot, starts, row_info, token_positions, row_ids = layout(lengths, groups, tok_rows)
    adapters_per_part = adapter_down_maps.shape[0]
    rank_extent = adapter_down_maps.shape[2]
    slots = adapter_table_slot[adapters]
    holder = slots // adapters_per_part
    local_slot = slots % adapters_per_part
    holder_ids = jnp.arange(req_count, dtype=jnp.int32)
    holder_hot = (holder[None, :] == holder_ids[:, None]).astype(jnp.int32)
    wanted = jnp.sum(holder_hot * local_slot[None, :], 1)
    wanted_in = exchange_ids(wanted)
    table = jnp.concatenate([jnp.transpose(adapter_down_maps, (0, 2, 1)), adapter_up_maps], 1)
    maps_out = table[wanted_in]
    tokens, maps_out = lax.optimization_barrier((tokens, maps_out))
    float_tok = tokens.astype(jnp.float32)
    normalized_input = (
        float_tok
        * lax.rsqrt(jnp.mean(float_tok * float_tok, -1, keepdims=True) + 1e-06)
        * input_norm_gain
    ).astype(jnp.bfloat16)
    maps_in = lax.all_to_all(maps_out, "req", split_axis=0, concat_axis=0, tiled=True)
    down_in = maps_in[:, :rank_extent, :].reshape(req_count * rank_extent, piece_width)
    up_in = maps_in[:, rank_extent:, :].reshape(req_count * rank_extent, piece_width)
    normed_slice = lax.dynamic_slice_in_dim(
        normalized_input, tp_index * piece_width, piece_width, 1
    )
    holder_row = jnp.sum(request_hot * holder[None, :], 1)
    pick = (holder_row[:, None] == holder_ids[None, :])[:, :, None]
    wide_rank = jnp.dot(
        normed_slice, down_in.T, preferred_element_type=jnp.float32
    ).reshape(tok_rows, req_count, rank_extent)
    partial_rank = jnp.sum(jnp.where(pick, wide_rank, jnp.float32(0.0)), 1)
    arrived = [
        lax.ppermute(partial_rank, "tp", [(i, (i + k) % tp_count) for i in range(tp_count)])
        for k in range(1, tp_count)
    ]
    for piece in arrived:
        partial_rank = partial_rank + piece
    rank = partial_rank.astype(jnp.bfloat16)
    spread = jnp.where(pick, rank[:, None, :], jnp.zeros((), jnp.bfloat16)).reshape(
        tok_rows, req_count * rank_extent
    )
    query_delta = (
        2.0 * jnp.dot(spread, up_in, preferred_element_type=jnp.float32)
    ).astype(jnp.bfloat16)
    heads_local = query_matrix.shape[1] // HEAD_WIDTH
    kv_local = key_matrix.shape[1] // HEAD_WIDTH
    query_full = jnp.dot(normalized_input, query_matrix, preferred_element_type=jnp.float32)
    half_dim = HEAD_WIDTH // 2
    inverse = 1000000.0 ** (-(jnp.arange(half_dim, dtype=jnp.float32) * 2.0 / HEAD_WIDTH))
    angles = token_positions[:, None] * inverse[None, :]
    cosine = jnp.cos(angles)
    sine = jnp.sin(angles)
    cos_pair = jnp.concatenate([cosine, cosine], 1)
    sin_pair = jnp.concatenate([-sine, sine], 1)
    key_complete = jnp.dot(normalized_input, key_matrix, preferred_element_type=jnp.float32)
    key_head_rows = apply_rotary(
        key_complete.reshape(tok_rows, kv_local, HEAD_WIDTH), token_positions
    ).astype(jnp.bfloat16)
    value_head_rows = (
        jnp.dot(normalized_input, value_matrix, preferred_element_type=jnp.float32)
        .astype(jnp.bfloat16)
        .reshape(tok_rows, kv_local, HEAD_WIDTH)
    )
    request_row, group_row, prompt_row, prompt_start, prompt_len = row_info
    n_blocks = tok_rows // BLOCK
    group_count = prompt_start.shape[0]
    kv_width = kv_local * HEAD_WIDTH
    key_flat = key_head_rows.reshape(tok_rows, kv_width)
    value_flat = value_head_rows.reshape(tok_rows, kv_width)
    front = jnp.zeros((BLOCK, kv_width), jnp.bfloat16)
    k_pad = jnp.concatenate([front, key_flat], 0)
    v_pad = jnp.concatenate([front, value_flat], 0)
    clamp_start = jnp.clip(prompt_start, 0, tok_rows - LMAX)
    extra = BLOCK - group_count * LMAX
    k_prompt = jnp.concatenate(
        [lax.dynamic_slice_in_dim(key_flat, clamp_start[g], LMAX, 0) for g in range(group_count)]
        + [jnp.zeros((extra, kv_width), jnp.bfloat16)],
        0,
    )
    v_prompt = jnp.concatenate(
        [lax.dynamic_slice_in_dim(value_flat, clamp_start[g], LMAX, 0) for g in range(group_count)]
        + [jnp.zeros((extra, kv_width), jnp.bfloat16)],
        0,
    )
    def windows(values, fill):
        padded = jnp.concatenate([jnp.full((BLOCK,), fill, values.dtype), values]).reshape(
            n_blocks + 1, BLOCK
        )
        return jnp.concatenate([padded[:-1], padded[1:]], 1)

    win_row = windows(row_ids, -1)
    win_req = windows(request_row, -1)
    win_grp = windows(group_row, -1)
    win_prm = windows(prompt_row, 0)
    q_row = row_ids.reshape(n_blocks, BLOCK)[:, :, None]
    q_req = request_row.reshape(n_blocks, BLOCK)[:, :, None]
    q_grp = group_row.reshape(n_blocks, BLOCK)[:, :, None]
    win_vis = (
        (win_row[:, None, :] >= 0)
        & (win_grp[:, None, :] == q_grp)
        & (win_row[:, None, :] <= q_row)
        & ((win_req[:, None, :] == q_req) | (win_prm[:, None, :] == 1))
    )
    p_row = (clamp_start[:, None] + jnp.arange(LMAX, dtype=jnp.int32)[None, :]).reshape(-1)
    p_lo = jnp.repeat(prompt_start, LMAX)
    p_hi = jnp.repeat(prompt_start + prompt_len, LMAX)
    p_grp = jnp.repeat(jnp.arange(group_count, dtype=jnp.int32), LMAX)
    p_row = jnp.concatenate([p_row, jnp.zeros((extra,), jnp.int32)])
    p_lo = jnp.concatenate([p_lo, jnp.ones((extra,), jnp.int32)])
    p_hi = jnp.concatenate([p_hi, jnp.zeros((extra,), jnp.int32)])
    p_grp = jnp.concatenate([p_grp, jnp.full((extra,), -1, jnp.int32)])
    win_first = q_row[:, :1, :] - BLOCK
    prompt_vis = (
        (p_grp[None, None, :] == q_grp)
        & (p_row[None, None, :] >= p_lo[None, None, :])
        & (p_row[None, None, :] < p_hi[None, None, :])
        & (p_row[None, None, :] < win_first)
        & (p_row[None, None, :] <= q_row)
    )
    vis = jnp.concatenate([win_vis, prompt_vis], 2)
    bias = jnp.where(vis, jnp.float32(0.0), jnp.float32(-1e30))
    residual = lax.dynamic_slice_in_dim(tokens, tp_index * piece_width, piece_width, 1)
    return attend_and_reduce(
        query_full,
        query_delta,
        cos_pair,
        sin_pair,
        k_pad,
        v_pad,
        k_prompt,
        v_prompt,
        bias,
        output_matrix,
        residual,
        tp_count,
    )


def solution(mesh):
    return jax.shard_map(
        per_device,
        mesh=mesh,
        in_specs=(
            P("req", None),
            P(),
            P(None, "tp"),
            P(None, "tp"),
            P(None, "tp"),
            P("tp", None),
            P("req", "tp", None),
            P("req", None, "tp"),
            P("req", None),
            P("req", None),
            P("req", None),
            P(),
        ),
        out_specs=P("req", "tp"),
        check_vma=False,
    )
```
